32 devices in a mesh: wide: 8 (over z, core), narrow: 4 (over y, x).
Axes of the slice: x: 2, y: 2, z: 4, core: 2. Of those that a mesh axis runs over, the one named last changes fastest.
Arguments:
- homolog_embedding: float32 [32, 1024, 256], P('wide', 'narrow'), may hold values from -6 to 6
- pair_state: float32 [1024, 1024, 128], P('wide', 'narrow'), may hold values from -6 to 6
- probe_projector: float32 [256, 256], replicated, may hold values from -0.375 to 0.375
- lookup_projector: float32 [256, 256], replicated, may hold values from -0.375 to 0.375
- content_projector: float32 [256, 256], replicated, may hold values from -0.375 to 0.375
- sigmoid_projector: float32 [256, 256], replicated, may hold values from -0.375 to 0.375
- sigmoid_offset: float32 [256], replicated, may hold values from -4 to 4
- pair_bias_weight: float32 [128, 8], replicated, may hold values from -4 to 4
- mixing_projector: float32 [256, 256], replicated, may hold values from -0.375 to 0.375
- mixing_offset: float32 [256], replicated, may hold values from -3 to 3
- first_factor_projector: float32 [256, 32], replicated, may hold values from -0.375 to 0.375
- second_factor_projector: float32 [256, 32], replicated, may hold values from -0.375 to 0.375
- outer_product_weight: float32 [1024, 128], replicated, may hold values from -0.5 to 0.5
- outer_product_bias: float32 [128], replicated, may hold values from -3 to 3
- up_weight: float32 [128, 512], replicated, may hold values from -0.5 to 0.5
- expand_bias: float32 [512], replicated, may hold values from -3 to 3
- down_weight: float32 [512, 128], replicated, may hold values from -0.25 to 0.25
Outputs:
- alignment_state_next: float32 [32, 1024, 256], P('wide', 'narrow')
- pair_state_next: float32 [1024, 1024, 128], P('wide', 'narrow')
The draws below stay inside these ranges and needn't reach their ends.
All inputs are finite; a program needn't handle non-finite values.
Results may differ from the reference program's by a relative error of at most 0.0003.
Values sent between devices are 32-bit elements; how exact they have to be, the bound alone decides.
No kernel may reach another device: no remote copies, remote signals or barrier semaphores. Data moves between devices by JAX's collectives and lax.ppermute only.
A program may use at most 192 MiB of HBM per device.

```python
import math
import jax
import jax.numpy as jnp
from jax import lax

FEATURE_DEPTH = 256
CZ = 128
H = 8
HIDDEN_FACTORS = 32
AMINO_SPAN = 1024
HEAD_SIZE = 32
FT = 512
ALIGNED_CHAINS = 32


def draw_pair_state(key, part):
    normal_part = jax.random.normal(key, (AMINO_SPAN, AMINO_SPAN, CZ), jnp.float32)
    return jnp.clip(normal_part, -6.0, 6.0)


def draw_pair_bias_weight(key, part):
    weights = jnp.clip(jax.random.normal(key, (CZ, H), jnp.float32) * CZ ** (-0.5), -0.6, 0.6)
    return weights


def block_levels(own_key, extent, split, least, high):
    factor_of = 1.0
    for dim, parts in split:
        steps = jax.random.uniform(jax.random.fold_in(jax.random.fold_in(own_key, 6), dim), (parts,), jnp.float32, least / len(split), high / len(split))
        factor_of = factor_of * jnp.repeat(jnp.exp(steps), extent[dim] // parts).reshape((-1,) + (1,) * (len(extent) - 1 - dim))
    return factor_of


def centred(key, shape, width, bound, split=(), kind=jnp.bfloat16):
    array = width * jax.random.normal(key, shape, jnp.float32)
    if split:
        array = array * block_levels(key, shape, split, -0.22, 0.18)
    return jnp.clip(array, -bound, bound).astype(kind)


def setup_inputs(seed: int = 0) -> dict:
    splits = jax.random.split(jax.random.key(seed), 18)
    return {
        "homolog_embedding": centred(splits[0], (ALIGNED_CHAINS, AMINO_SPAN, FEATURE_DEPTH), 1.0, 6.0, ((0, 8), (1, 4)), jnp.float32),
        "pair_state": draw_pair_state(jax.random.fold_in(splits[17], 71), 0),
        "probe_projector": centred(splits[2], (FEATURE_DEPTH, FEATURE_DEPTH), FEATURE_DEPTH ** -0.5, 0.375, (), jnp.float32),
        "lookup_projector": centred(splits[3], (FEATURE_DEPTH, FEATURE_DEPTH), FEATURE_DEPTH ** -0.5, 0.375, (), jnp.float32),
        "content_projector": centred(splits[4], (FEATURE_DEPTH, FEATURE_DEPTH), FEATURE_DEPTH ** -0.5, 0.375, (), jnp.float32),
        "sigmoid_projector": centred(splits[5], (FEATURE_DEPTH, FEATURE_DEPTH), FEATURE_DEPTH ** -0.5, 0.375, (), jnp.float32),
        "sigmoid_offset": centred(splits[6], (FEATURE_DEPTH,), 1.0, 4.0, (), jnp.float32),
        "pair_bias_weight": draw_pair_bias_weight(jax.random.fold_in(splits[17], 71), 0),
        "mixing_projector": centred(splits[8], (FEATURE_DEPTH, FEATURE_DEPTH), FEATURE_DEPTH ** -0.5, 0.375, (), jnp.float32),
        "mixing_offset": centred(splits[9], (FEATURE_DEPTH,), 0.5, 3.0, (), jnp.float32),
        "first_factor_projector": centred(splits[10], (FEATURE_DEPTH, HIDDEN_FACTORS), FEATURE_DEPTH ** -0.5, 0.375, (), jnp.float32),
        "second_factor_projector": centred(splits[11], (FEATURE_DEPTH, HIDDEN_FACTORS), FEATURE_DEPTH ** -0.5, 0.375, (), jnp.float32),
        "outer_product_weight": centred(splits[12], (HIDDEN_FACTORS * HIDDEN_FACTORS, CZ), (HIDDEN_FACTORS * HIDDEN_FACTORS // 8) ** -0.5, 0.5, (), jnp.float32),
        "outer_product_bias": centred(splits[13], (CZ,), 0.5, 3.0, (), jnp.float32),
        "up_weight": centred(splits[14], (CZ, FT), CZ ** -0.5, 0.5, (), jnp.float32),
        "expand_bias": centred(splits[15], (FT,), 0.5, 3.0, (), jnp.float32),
        "down_weight": centred(splits[16], (FT, CZ), FT ** -0.5, 0.25, (), jnp.float32),
    }


finest_precision = lax.Precision.HIGHEST

def layer_normalize(tensor):
    row_mean = lax.optimization_barrier(jnp.mean(tensor, axis=-1, keepdims=True))
    centered = tensor - row_mean
    variance = lax.optimization_barrier(jnp.mean(centered * centered, axis=-1, keepdims=True))
    return centered * lax.rsqrt(variance + 1e-05)

def matrix_multiply(first_arr, second_arr):
    return jnp.dot(first_arr, second_arr, precision=finest_precision, preferred_element_type=jnp.float32)

def reference(homolog_embedding, pair_state, probe_projector, lookup_projector, content_projector, sigmoid_projector, sigmoid_offset, pair_bias_weight, mixing_projector, mixing_offset, first_factor_projector, second_factor_projector, outer_product_weight, outer_product_bias, up_weight, expand_bias, down_weight):
    alignment_normed = layer_normalize(homolog_embedding)
    query_vectors = matrix_multiply(alignment_normed, probe_projector) / math.sqrt(HEAD_SIZE)
    key_rows = matrix_multiply(alignment_normed, lookup_projector)
    value_rows = matrix_multiply(alignment_normed, content_projector)
    gate_logits = matrix_multiply(alignment_normed, sigmoid_projector) + sigmoid_offset
    pair_bias = jnp.einsum('ijc,ch->hij', layer_normalize(pair_state), pair_bias_weight, precision=finest_precision)

    def per_sequence(operands):
        query_seq = operands[0].reshape(AMINO_SPAN, H, HEAD_SIZE)
        key_seq = operands[1].reshape(AMINO_SPAN, H, HEAD_SIZE)
        content_by_homolog = operands[2].reshape(AMINO_SPAN, H, HEAD_SIZE)
        scores = jnp.einsum('ihd,jhd->hij', query_seq, key_seq, precision=finest_precision) + pair_bias
        row_max = lax.optimization_barrier(jnp.max(scores, axis=-1, keepdims=True))
        exponent = jnp.exp(scores - row_max)
        softmax_probabilities = exponent / lax.optimization_barrier(jnp.sum(exponent, axis=-1, keepdims=True))
        returned_tensor = jnp.einsum('arz,zas->ras', softmax_probabilities, content_by_homolog, precision=finest_precision).reshape(AMINO_SPAN, FEATURE_DEPTH)
        return returned_tensor * jax.nn.sigmoid(operands[3])
    attended_values = lax.map(per_sequence, (query_vectors, key_rows, value_rows, gate_logits))
    alignment_state_next = homolog_embedding + matrix_multiply(attended_values, mixing_projector) + mixing_offset
    outer_product_normed = layer_normalize(alignment_state_next)
    left_proj = matrix_multiply(outer_product_normed, first_factor_projector)
    right_proj = matrix_multiply(outer_product_normed, second_factor_projector)
    row_block = min(32, AMINO_SPAN)

    def outer_rows(block_index):
        left_part = lax.dynamic_slice_in_dim(left_proj, block_index * row_block, row_block, 1)
        product = jnp.einsum('sic,sjd->ijcd', left_part, right_proj, precision=finest_precision) / ALIGNED_CHAINS
        flat = product.reshape(row_block * AMINO_SPAN, HIDDEN_FACTORS * HIDDEN_FACTORS)
        return matrix_multiply(flat, outer_product_weight).reshape(row_block, AMINO_SPAN, CZ)
    update = lax.map(outer_rows, jnp.arange(AMINO_SPAN // row_block, dtype=jnp.int32)).reshape(AMINO_SPAN, AMINO_SPAN, CZ)
    pair_mid = pair_state + update + outer_product_bias

    def transition(pair_rows):
        hidden = jax.nn.relu(matrix_multiply(layer_normalize(pair_rows), up_weight) + expand_bias)
        return pair_rows + matrix_multiply(hidden, down_weight)
    pair_state_next = lax.map(transition, pair_mid.reshape(AMINO_SPAN // row_block, row_block, AMINO_SPAN, CZ)).reshape(AMINO_SPAN, AMINO_SPAN, CZ)
    return (alignment_state_next, pair_state_next)
```

```python
import functools
import math

import jax
import jax.numpy as jnp
from jax import lax
from jax.experimental import pallas as pl
from jax.experimental.pallas import tpu as pltpu
from jax.sharding import PartitionSpec as P

F32, BF16 = jnp.float32, jnp.bfloat16
PARAMS = pltpu.CompilerParams(vmem_limit_bytes=60 * 2**20)


def split(x):
    hi = x.astype(BF16)
    lo = (x - hi.astype(F32)).astype(BF16)
    return hi, lo


def mm(a, b):
    return jnp.dot(a, b, preferred_element_type=F32)


def mm_nt(a, b):
    return lax.dot_general(a, b, (((1,), (1,)), ((), ())), preferred_element_type=F32)


def norm_rows(x):
    mean = jnp.mean(x, axis=-1, keepdims=True)
    c = x - mean
    var = jnp.mean(c * c, axis=-1, keepdims=True)
    return c * lax.rsqrt(var + 1e-05)


def whole(a):
    return pl.BlockSpec(a.shape, lambda *_: (0,) * a.ndim, pipeline_mode=pl.Buffered(1))


def bias_kernel(pair_ref, w_ref, out_ref):
    rows, cols, cz = pair_ref.shape
    heads = w_ref.shape[1]
    wh, wl = split(w_ref[...].T)
    lhs = jnp.concatenate(
        [jnp.concatenate([wh, wh], axis=1), jnp.concatenate([wl, wl], axis=1)], axis=0
    )
    for i in range(rows):
        yh, yl = split(norm_rows(pair_ref[i]))
        r = mm_nt(lhs, jnp.concatenate([yh, yl], axis=1))
        out_ref[:, i, :] = r[:heads] + r[heads:]


def bias_tile(pair, w, step=8):
    rows, cols, cz = pair.shape
    heads = w.shape[1]
    return pl.pallas_call(
        bias_kernel,
        out_shape=jax.ShapeDtypeStruct((heads, rows, cols), F32),
        grid=(rows // step,),
        in_specs=[pl.BlockSpec((step, cols, cz), lambda i: (i, 0, 0)), whole(w)],
        out_specs=pl.BlockSpec((heads, step, cols), lambda i: (0, i, 0)),
        compiler_params=PARAMS,
        name="bias_tile",
    )(pair, w)


def project_kernel(parts, scale, x_ref, wq_ref, wk_ref, wv_ref, wg_ref, bg_ref, qkv_ref, gate_ref, w_hi, w_lo):
    ch = x_ref.shape[-1]
    own = ch // parts

    @pl.when(pl.program_id(0) == 0)
    def _():
        for t, (ref, f) in enumerate(((wq_ref, scale), (wk_ref, 1.0), (wv_ref, 1.0), (wg_ref, 1.0))):
            hi, lo = split(ref[...].T * f)
            w_hi[t * ch:(t + 1) * ch, :] = hi
            w_lo[t * ch:(t + 1) * ch, :] = lo

    yh, yl = split(norm_rows(x_ref[0]))
    r = mm_nt(w_hi[...], yh) + mm_nt(w_hi[...], yl) + mm_nt(w_lo[...], yh)
    for t in range(3):
        for n in range(parts):
            lo = t * ch + n * own
            qkv_ref[n, t, 0] = r[lo:lo + own]
    gate_ref[0] = jax.nn.sigmoid(r[3 * ch:] + bg_ref[...])


def project(x, wq, wk, wv, wg, bg, parts, head_width):
    seqs, span, ch = x.shape
    own = ch // parts
    bg = bg.reshape(ch, 1)
    return pl.pallas_call(
        functools.partial(project_kernel, parts, 1.0 / math.sqrt(head_width)),
        out_shape=(
            jax.ShapeDtypeStruct((parts, 3, seqs, own, span), F32),
            jax.ShapeDtypeStruct((seqs, ch, span), F32),
        ),
        grid=(seqs,),
        in_specs=[pl.BlockSpec((1, span, ch), lambda s: (s, 0, 0))] + [whole(a) for a in (wq, wk, wv, wg, bg)],
        out_specs=(
            pl.BlockSpec((parts, 3, 1, own, span), lambda s: (0, 0, s, 0, 0)),
            pl.BlockSpec((1, ch, span), lambda s: (s, 0, 0)),
        ),
        scratch_shapes=[pltpu.VMEM((4 * ch, ch), BF16), pltpu.VMEM((4 * ch, ch), BF16)],
        compiler_params=PARAMS,
        name="project",
    )(x, wq, wk, wv, wg, bg)


def attention_kernel(hw, q_ref, k_ref, v_ref, bias_ref, out_ref, ks, vs):
    parts = k_ref.shape[0]
    span = k_ref.shape[-1]
    s = pl.program_id(1)

    @pl.when(pl.program_id(0) == 0)
    def _():
        for n in range(parts):
            at = slice(n * span, (n + 1) * span)
            hi, lo = split(k_ref[n, 0, 0])
            ks[s, 0:hw, at] = hi
            ks[s, hw:2 * hw, at] = lo
            ks[s, 2 * hw:3 * hw, at] = hi
            v = v_ref[n, 0, 0]
            vh = v.astype(BF16).astype(F32)
            st = jnp.concatenate([vh, v - vh, jnp.ones((hw, span), F32), jnp.zeros((hw, span), F32)], axis=0)
            vs[s, at, :] = st.T.astype(BF16)

    q = q_ref[0, 0, 0]
    qh = q.astype(BF16).astype(F32)
    qst = jnp.concatenate([qh, qh, q - qh, jnp.zeros_like(q)], axis=0).T[:, :3 * hw].astype(BF16)
    bias = jnp.concatenate(
        [
            jnp.concatenate([bias_ref[w, n] for n in range(parts)], axis=1)
            for w in range(bias_ref.shape[0])
        ],
        axis=0,
    )
    scores = mm(qst, ks[s]) + bias
    top = jnp.max(scores, axis=1, keepdims=True)
    ph, plo = split(jnp.exp(scores - top))
    t = (mm(ph, vs[s]) + mm(plo, vs[s])).T
    out_ref[0, 0] = (t[0:hw] + t[hw:2 * hw]) / t[2 * hw:2 * hw + 1]


def attention(qkv, bias, head, hw):
    parts, _, seqs, own, span = qkv.shape
    wide, _, rows, _ = bias.shape
    per = span // rows
    return pl.pallas_call(
        functools.partial(attention_kernel, hw),
        out_shape=jax.ShapeDtypeStruct((parts, seqs, hw, span), F32),
        grid=(parts, seqs),
        in_specs=[
            pl.BlockSpec((1, 1, 1, hw, span), lambda b, s: (b, 0, s, head, 0)),
            pl.BlockSpec((parts, 1, 1, hw, span), lambda b, s: (0, 1, s, head, 0)),
            pl.BlockSpec((parts, 1, 1, hw, span), lambda b, s: (0, 2, s, head, 0)),
            pl.BlockSpec((per, parts, rows, span), lambda b, s: (b, 0, 0, 0)),
        ],
        out_specs=pl.BlockSpec((1, 1, hw, span), lambda b, s: (b, s, 0, 0)),
        scratch_shapes=[
            pltpu.VMEM((seqs, 3 * hw, parts * span), BF16),
            pltpu.VMEM((seqs, parts * span, 4 * hw), BF16),
        ],
        compiler_params=PARAMS,
        name="attention",
    )(qkv, qkv, qkv, bias)


def merge_kernel(*refs):
    heads = len(refs) - 12
    att = refs[:heads]
    gate_ref, x_ref, wm_ref, bm_ref, f1_ref, f2_ref, next_ref, left_ref, right_ref, m_hi, m_lo, f_st = refs[heads:]
    parts, _, hw, span = att[0].shape
    ch = x_ref.shape[-1]
    hid = f1_ref.shape[1]
    blocks, _, _, rows = left_ref.shape

    @pl.when(pl.program_id(0) == 0)
    def _():
        hi, lo = split(wm_ref[...])
        m_hi[...] = hi
        m_lo[...] = lo
        hi, lo = split(jnp.concatenate([f1_ref[...], f2_ref[...]], axis=1).T)
        f_st[0:2 * hid, :] = hi
        f_st[2 * hid:4 * hid, :] = lo

    a = jnp.concatenate([att[h][n, 0] for n in range(parts) for h in range(heads)], axis=0)
    ah, al = split((a * gate_ref[0]).T)
    y = x_ref[0] + (mm(ah, m_hi[...]) + mm(al, m_hi[...]) + mm(ah, m_lo[...])) + bm_ref[...]
    next_ref[0] = y
    zh, zl = split(norm_rows(y))
    p = mm_nt(f_st[...], zh)
    p = p[:2 * hid] + p[2 * hid:] + mm_nt(f_st[0:2 * hid, :], zl)
    for b in range(blocks):
        left_ref[b, 0] = p[:hid, b * rows:(b + 1) * rows]
    right_ref[0] = p[hid:]


def merge(att, gate, x, wm, bm, f1, f2, rows):
    seqs, span, ch = x.shape
    parts, _, hw, _ = att[0].shape
    hid = f1.shape[1]
    bm = bm.reshape(1, ch)
    blocks = span // rows
    return pl.pallas_call(
        merge_kernel,
        out_shape=(
            jax.ShapeDtypeStruct(x.shape, F32),
            jax.ShapeDtypeStruct((blocks, seqs, hid, rows), F32),
            jax.ShapeDtypeStruct((seqs, hid, span), F32),
        ),
        grid=(seqs,),
        in_specs=[pl.BlockSpec((parts, 1, hw, span), lambda s: (0, s, 0, 0)) for _ in att]
        + [
            pl.BlockSpec((1, ch, span), lambda s: (s, 0, 0)),
            pl.BlockSpec((1, span, ch), lambda s: (s, 0, 0)),
        ]
        + [whole(a) for a in (wm, bm, f1, f2)],
        out_specs=(
            pl.BlockSpec((1, span, ch), lambda s: (s, 0, 0)),
            pl.BlockSpec((blocks, 1, hid, rows), lambda s: (0, s, 0, 0)),
            pl.BlockSpec((1, hid, span), lambda s: (s, 0, 0)),
        ),
        scratch_shapes=[
            pltpu.VMEM((ch, ch), BF16),
            pltpu.VMEM((ch, ch), BF16),
            pltpu.VMEM((4 * hid, ch), BF16),
        ],
        compiler_params=PARAMS,
        name="merge",
    )(*att, gate, x, wm, bm, f1, f2)


def pair_kernel(
    step_rows, seqs, left_ref, right_ref, w_ref, pair_ref, ob_ref, up_ref, eb_ref, dn_ref,
    out_ref, r_hi, r_lo, w_st, up_st, dn_st,
):
    cz = pair_ref.shape[2]
    c_n = w_ref.shape[0]
    d_n = w_ref.shape[1] // cz

    @pl.when(pl.program_id(0) == 0)
    def _():
        hi, lo = split(right_ref[...])
        r_hi[...] = hi
        r_lo[...] = lo
        hi, lo = split(w_ref[...])
        w_st[0:c_n, :] = hi
        w_st[c_n:2 * c_n, :] = lo
        w_st[2 * c_n:3 * c_n, :] = hi
        hi, lo = split(up_ref[...])
        up_st[0:cz, :] = hi
        up_st[cz:2 * cz, :] = hi
        up_st[2 * cz:3 * cz, :] = lo
        hi, lo = split(dn_ref[...])
        dn_st[:, 0:cz] = hi
        dn_st[:, cz:2 * cz] = lo

    def body(p, carry):
        lrow = left_ref[pl.ds(pl.multiple_of(p * 2 * seqs, 2 * seqs), 2 * seqs), :]
        lhi = lrow.astype(BF16).astype(F32)
        u = mm(jnp.concatenate([lhi, lhi, lrow - lhi], axis=1).astype(BF16), w_st[...])
        his, los = [], []
        for q in range(2):
            sub = u[q * seqs:(q + 1) * seqs, :]
            hi, lo = split(jnp.concatenate([sub[:, d * cz:(d + 1) * cz] for d in range(d_n)], axis=0))
            his.append(hi)
            los.append(lo)
        cross = mm(r_lo[...], jnp.concatenate(his, axis=1))
        mids = []
        for q in range(2):
            a = mm(r_hi[...], jnp.concatenate([his[q], los[q]], axis=1))
            o = a[:, :cz] + a[:, cz:] + cross[:, q * cz:(q + 1) * cz]
            mids.append(pair_ref[2 * p + q] + o / seqs + ob_ref[...])
        for q in range(2):
            yh, yl = split(norm_rows(mids[q]))
            h = mm(jnp.concatenate([yh, yl, yh], axis=1), up_st[...])
            hh, hl = split(jnp.maximum(h + eb_ref[...], 0.0))
            a = mm(hh, dn_st[...])
            out_ref[2 * p + q] = mids[q] + (a[:, :cz] + a[:, cz:] + mm(hl, dn_st[:, 0:cz]))
        return carry

    lax.fori_loop(0, step_rows // 2, body, 0, unroll=2)


def pair_update(left_rows, right_cols, w2, pair, ob, up, eb, dn, step_rows=8):
    rows, cols, cz = pair.shape
    seqs = left_rows.shape[0] // rows
    c_n = w2.shape[0]
    ob = ob.reshape(1, -1)
    eb = eb.reshape(1, -1)
    return pl.pallas_call(
        functools.partial(pair_kernel, step_rows, seqs),
        out_shape=jax.ShapeDtypeStruct(pair.shape, F32),
        grid=(rows // step_rows,),
        in_specs=[
            pl.BlockSpec((step_rows * seqs, left_rows.shape[1]), lambda i: (i, 0)),
            whole(right_cols), whole(w2),
            pl.BlockSpec((step_rows, cols, cz), lambda i: (i, 0, 0)),
            whole(ob), whole(up), whole(eb), whole(dn),
        ],
        out_specs=pl.BlockSpec((step_rows, cols, cz), lambda i: (i, 0, 0)),
        scratch_shapes=[
            pltpu.VMEM(right_cols.shape, BF16),
            pltpu.VMEM(right_cols.shape, BF16),
            pltpu.VMEM((3 * c_n, w2.shape[1]), BF16),
            pltpu.VMEM((3 * cz, up.shape[1]), BF16),
            pltpu.VMEM((up.shape[1], 2 * cz), BF16),
        ],
        compiler_params=PARAMS,
        name="pair_update",
    )(left_rows, right_cols, w2, pair, ob, up, eb, dn)


def per_device(
    parts,
    homolog_embedding,
    pair_state,
    probe_projector,
    lookup_projector,
    content_projector,
    sigmoid_projector,
    sigmoid_offset,
    pair_bias_weight,
    mixing_projector,
    mixing_offset,
    first_factor_projector,
    second_factor_projector,
    outer_product_weight,
    outer_product_bias,
    up_weight,
    expand_bias,
    down_weight,
):
    seqs, span, ch = homolog_embedding.shape
    rows, cols, cz = pair_state.shape
    heads = pair_bias_weight.shape[1]
    hw = ch // heads
    own_heads = heads // parts
    hid = first_factor_projector.shape[1]

    bias = bias_tile(pair_state, pair_bias_weight).reshape(parts, own_heads, rows, cols)
    bias = lax.all_to_all(bias, "narrow", 0, 0, tiled=True)
    gathered = [
        lax.all_gather(bias[:, h], "wide", axis=0, tiled=False) for h in range(own_heads)
    ]
    qkv, gate = project(
        homolog_embedding, probe_projector, lookup_projector, content_projector, sigmoid_projector,
        sigmoid_offset, parts, hw,
    )
    qkv = lax.all_to_all(qkv, "narrow", 0, 0, tiled=True)
    att = [
        lax.all_to_all(attention(qkv, gathered[h], h, hw), "narrow", 0, 0, tiled=True)
        for h in range(own_heads)
    ]
    alignment_state_next, left, right = merge(
        att, gate, homolog_embedding, mixing_projector, mixing_offset,
        first_factor_projector, second_factor_projector, rows,
    )
    left = lax.all_gather(left, "narrow", axis=0, tiled=True)
    left = lax.all_to_all(left, "wide", 0, 0, tiled=True)
    right = lax.all_gather(right, "wide", axis=0, tiled=True)
    left = left.reshape(-1, hid, rows)
    all_seqs = left.shape[0]
    left_rows = jnp.transpose(left, (2, 0, 1)).reshape(rows * all_seqs, hid)
    right_cols = jnp.transpose(right, (2, 1, 0)).reshape(cols, hid * all_seqs)
    pair_state_next = pair_update(
        left_rows, right_cols, outer_product_weight.reshape(hid, hid * cz), pair_state,
        outer_product_bias, up_weight, expand_bias, down_weight,
    )
    return (alignment_state_next, pair_state_next)


def solution(mesh):
    placed = (P("wide", "narrow", None), P("wide", "narrow", None)) + (P(),) * 15
    return jax.shard_map(
        functools.partial(per_device, mesh.shape["narrow"]),
        mesh=mesh,
        in_specs=placed,
        out_specs=(P("wide", "narrow", None), P("wide", "narrow", None)),
        check_vma=False,
    )
```

```python
import functools
import math

import jax
import jax.numpy as jnp
from jax import lax
from jax.experimental import pallas as pl
from jax.experimental.pallas import tpu as pltpu
from jax.sharding import PartitionSpec as P

F32, BF16 = jnp.float32, jnp.bfloat16
PARAMS = pltpu.CompilerParams(vmem_limit_bytes=60 * 2**20)


def split(x):
    hi = x.astype(BF16)
    lo = (x - hi.astype(F32)).astype(BF16)
    return hi, lo


def mm(a, b):
    return jnp.dot(a, b, preferred_element_type=F32)


def mm_nt(a, b):
    return lax.dot_general(a, b, (((1,), (1,)), ((), ())), preferred_element_type=F32)


def norm_rows(x):
    mean = jnp.mean(x, axis=-1, keepdims=True)
    c = x - mean
    var = jnp.mean(c * c, axis=-1, keepdims=True)
    return c * lax.rsqrt(var + 1e-05)


def whole(a):
    return pl.BlockSpec(a.shape, lambda *_: (0,) * a.ndim, pipeline_mode=pl.Buffered(1))


def bias_kernel(pair_ref, w_ref, out_ref):
    rows, cols, cz = pair_ref.shape
    heads = w_ref.shape[1]
    wh, wl = split(w_ref[...].T)
    lhs = jnp.concatenate(
        [jnp.concatenate([wh, wh], axis=1), jnp.concatenate([wl, wl], axis=1)], axis=0
    )
    for i in range(rows):
        yh, yl = split(norm_rows(pair_ref[i]))
        r = mm_nt(lhs, jnp.concatenate([yh, yl], axis=1))
        out_ref[:, i, :] = r[:heads] + r[heads:]


def bias_tile(pair, w, step=8):
    rows, cols, cz = pair.shape
    heads = w.shape[1]
    return pl.pallas_call(
        bias_kernel,
        out_shape=jax.ShapeDtypeStruct((heads, rows, cols), F32),
        grid=(rows // step,),
        in_specs=[pl.BlockSpec((step, cols, cz), lambda i: (i, 0, 0)), whole(w)],
        out_specs=pl.BlockSpec((heads, step, cols), lambda i: (0, i, 0)),
        compiler_params=PARAMS,
        name="bias_tile",
    )(pair, w)


def project_kernel(parts, scale, x_ref, wq_ref, wk_ref, wv_ref, wg_ref, bg_ref, qkv_ref, gate_ref, w_hi, w_lo):
    ch = x_ref.shape[-1]
    own = ch // parts

    @pl.when(pl.program_id(0) == 0)
    def _():
        for t, (ref, f) in enumerate(((wq_ref, scale), (wk_ref, 1.0), (wv_ref, 1.0), (wg_ref, 1.0))):
            hi, lo = split(ref[...].T * f)
            w_hi[t * ch:(t + 1) * ch, :] = hi
            w_lo[t * ch:(t + 1) * ch, :] = lo

    yh, yl = split(norm_rows(x_ref[0]))
    r = mm_nt(w_hi[...], yh) + mm_nt(w_hi[...], yl) + mm_nt(w_lo[...], yh)
    for t in range(3):
        for n in range(parts):
            lo = t * ch + n * own
            qkv_ref[n, t, 0] = r[lo:lo + own]
    gate_ref[0] = jax.nn.sigmoid(r[3 * ch:] + bg_ref[...])


def project(x, wq, wk, wv, wg, bg, parts, head_width):
    seqs, span, ch = x.shape
    own = ch // parts
    bg = bg.reshape(ch, 1)
    return pl.pallas_call(
        functools.partial(project_kernel, parts, 1.0 / math.sqrt(head_width)),
        out_shape=(
            jax.ShapeDtypeStruct((parts, 3, seqs, own, span), F32),
            jax.ShapeDtypeStruct((seqs, ch, span), F32),
        ),
        grid=(seqs,),
        in_specs=[pl.BlockSpec((1, span, ch), lambda s: (s, 0, 0))] + [whole(a) for a in (wq, wk, wv, wg, bg)],
        out_specs=(
            pl.BlockSpec((parts, 3, 1, own, span), lambda s: (0, 0, s, 0, 0)),
            pl.BlockSpec((1, ch, span), lambda s: (s, 0, 0)),
        ),
        scratch_shapes=[pltpu.VMEM((4 * ch, ch), BF16), pltpu.VMEM((4 * ch, ch), BF16)],
        compiler_params=PARAMS,
        name="project",
    )(x, wq, wk, wv, wg, bg)


def attention_kernel(hw, q_ref, k_ref, v_ref, bias_ref, out_ref, ks, vs):
    parts = k_ref.shape[0]
    span = k_ref.shape[-1]
    s = pl.program_id(1)

    @pl.when(pl.program_id(0) == 0)
    def _():
        for n in range(parts):
            at = slice(n * span, (n + 1) * span)
            hi, lo = split(k_ref[n, 0, 0])
            ks[s, 0:hw, at] = hi
            ks[s, hw:2 * hw, at] = lo
            ks[s, 2 * hw:3 * hw, at] = hi
            v = v_ref[n, 0, 0]
            vh = v.astype(BF16).astype(F32)
            st = jnp.concatenate([vh, v - vh, jnp.ones((hw, span), F32), jnp.zeros((hw, span), F32)], axis=0)
            vs[s, at, :] = st.T.astype(BF16)

    q = q_ref[0, 0, 0]
    qh = q.astype(BF16).astype(F32)
    qst = jnp.concatenate([qh, qh, q - qh, jnp.zeros_like(q)], axis=0).T[:, :3 * hw].astype(BF16)
    bias = jnp.concatenate(
        [
            jnp.concatenate([bias_ref[w, n] for n in range(parts)], axis=1)
            for w in range(bias_ref.shape[0])
        ],
        axis=0,
    )
    scores = mm(qst, ks[s]) + bias
    top = jnp.max(scores, axis=1, keepdims=True)
    ph, plo = split(jnp.exp(scores - top))
    t = (mm(ph, vs[s]) + mm(plo, vs[s])).T
    out_ref[0, 0] = (t[0:hw] + t[hw:2 * hw]) / t[2 * hw:2 * hw + 1]


def attention(qkv, bias, head, hw):
    parts, _, seqs, own, span = qkv.shape
    wide, _, rows, _ = bias.shape
    per = span // rows
    return pl.pallas_call(
        functools.partial(attention_kernel, hw),
        out_shape=jax.ShapeDtypeStruct((parts, seqs, hw, span), F32),
        grid=(parts, seqs),
        in_specs=[
            pl.BlockSpec((1, 1, 1, hw, span), lambda b, s: (b, 0, s, head, 0)),
            pl.BlockSpec((parts, 1, 1, hw, span), lambda b, s: (0, 1, s, head, 0)),
            pl.BlockSpec((parts, 1, 1, hw, span), lambda b, s: (0, 2, s, head, 0)),
            pl.BlockSpec((per, parts, rows, span), lambda b, s: (b, 0, 0, 0)),
        ],
        out_specs=pl.BlockSpec((1, 1, hw, span), lambda b, s: (b, s, 0, 0)),
        scratch_shapes=[
            pltpu.VMEM((seqs, 3 * hw, parts * span), BF16),
            pltpu.VMEM((seqs, parts * span, 4 * hw), BF16),
        ],
        compiler_params=PARAMS,
        name="attention",
    )(qkv, qkv, qkv, bias)


def merge_kernel(*refs):
    heads = len(refs) - 12
    att = refs[:heads]
    gate_ref, x_ref, wm_ref, bm_ref, f1_ref, f2_ref, next_ref, left_ref, right_ref, m_hi, m_lo, f_st = refs[heads:]
    parts, _, hw, span = att[0].shape
    ch = x_ref.shape[-1]
    hid = f1_ref.shape[1]
    blocks, _, _, rows = left_ref.shape

    @pl.when(pl.program_id(0) == 0)
    def _():
        hi, lo = split(wm_ref[...])
        m_hi[...] = hi
        m_lo[...] = lo
        hi, lo = split(jnp.concatenate([f1_ref[...], f2_ref[...]], axis=1).T)
        f_st[0:2 * hid, :] = hi
        f_st[2 * hid:4 * hid, :] = lo

    a = jnp.concatenate([att[h][n, 0] for n in range(parts) for h in range(heads)], axis=0)
    ah, al = split((a * gate_ref[0]).T)
    y = x_ref[0] + (mm(ah, m_hi[...]) + mm(al, m_hi[...]) + mm(ah, m_lo[...])) + bm_ref[...]
    next_ref[0] = y
    zh, zl = split(norm_rows(y))
    p = mm_nt(f_st[...], zh)
    p = p[:2 * hid] + p[2 * hid:] + mm_nt(f_st[0:2 * hid, :], zl)
    for b in range(blocks):
        left_ref[b, 0] = p[:hid, b * rows:(b + 1) * rows]
    right_ref[0] = p[hid:]


def merge(att, gate, x, wm, bm, f1, f2, rows):
    seqs, span, ch = x.shape
    parts, _, hw, _ = att[0].shape
    hid = f1.shape[1]
    bm = bm.reshape(1, ch)
    blocks = span // rows
    return pl.pallas_call(
        merge_kernel,
        out_shape=(
            jax.ShapeDtypeStruct(x.shape, F32),
            jax.ShapeDtypeStruct((blocks, seqs, hid, rows), F32),
            jax.ShapeDtypeStruct((seqs, hid, span), F32),
        ),
        grid=(seqs,),
        in_specs=[pl.BlockSpec((parts, 1, hw, span), lambda s: (0, s, 0, 0)) for _ in att]
        + [
            pl.BlockSpec((1, ch, span), lambda s: (s, 0, 0)),
            pl.BlockSpec((1, span, ch), lambda s: (s, 0, 0)),
        ]
        + [whole(a) for a in (wm, bm, f1, f2)],
        out_specs=(
            pl.BlockSpec((1, span, ch), lambda s: (s, 0, 0)),
            pl.BlockSpec((blocks, 1, hid, rows), lambda s: (0, s, 0, 0)),
            pl.BlockSpec((1, hid, span), lambda s: (s, 0, 0)),
        ),
        scratch_shapes=[
            pltpu.VMEM((ch, ch), BF16),
            pltpu.VMEM((ch, ch), BF16),
            pltpu.VMEM((4 * hid, ch), BF16),
        ],
        compiler_params=PARAMS,
        name="merge",
    )(*att, gate, x, wm, bm, f1, f2)


def pair_kernel(
    step_rows, group, seqs, left_ref, right_ref, w_ref, pair_ref, ob_ref, up_ref, eb_ref, dn_ref,
    out_ref, r_hi, r_lo, w_st, up_st, dn_st,
):
    _, cols, cz = pair_ref.shape
    c_n = w_ref.shape[0]
    d_n = w_ref.shape[1] // cz

    @pl.when(pl.program_id(0) == 0)
    def _():
        hi, lo = split(right_ref[...])
        r_hi[...] = hi
        r_lo[...] = lo
        hi, lo = split(w_ref[...])
        w_st[0:c_n, :] = hi
        w_st[c_n:2 * c_n, :] = lo
        w_st[2 * c_n:3 * c_n, :] = hi
        hi, lo = split(up_ref[...])
        up_st[0:cz, :] = hi
        up_st[cz:2 * cz, :] = hi
        up_st[2 * cz:3 * cz, :] = lo
        hi, lo = split(dn_ref[...])
        dn_st[:, 0:cz] = hi
        dn_st[:, cz:2 * cz] = lo

    def body(p, carry):
        lrow = left_ref[pl.ds(pl.multiple_of(p * group * seqs, group * seqs), group * seqs), :]
        lhi = lrow.astype(BF16).astype(F32)
        u = mm(jnp.concatenate([lhi, lhi, lrow - lhi], axis=1).astype(BF16), w_st[...])
        his, los = [], []
        for q in range(group):
            sub = u[q * seqs:(q + 1) * seqs, :]
            hi, lo = split(jnp.concatenate([sub[:, d * cz:(d + 1) * cz] for d in range(d_n)], axis=0))
            his.append(hi)
            los.append(lo)
        mids = []
        for q in range(0, group, 2):
            cross = mm(r_lo[...], jnp.concatenate(his[q:q + 2], axis=1))
            for i in range(2):
                a = mm(r_hi[...], jnp.concatenate([his[q + i], los[q + i]], axis=1))
                o = a[:, :cz] + a[:, cz:] + cross[:, i * cz:(i + 1) * cz]
                mids.append(pair_ref[group * p + q + i] + o / seqs + ob_ref[...])
        for q in range(0, group, 2):
            mid = jnp.concatenate(mids[q:q + 2], axis=0)
            yh, yl = split(norm_rows(mid))
            h = mm(jnp.concatenate([yh, yl, yh], axis=1), up_st[...])
            hh, hl = split(jnp.maximum(h + eb_ref[...], 0.0))
            a = mm(hh, dn_st[...])
            o = mid + (a[:, :cz] + a[:, cz:] + mm(hl, dn_st[:, 0:cz]))
            for i in range(2):
                out_ref[group * p + q + i] = o[i * cols:(i + 1) * cols]
        return carry

    lax.fori_loop(0, step_rows // group, body, 0)


def pair_update(left_rows, right_cols, w2, pair, ob, up, eb, dn, step_rows=8, group=4):
    rows, cols, cz = pair.shape
    seqs = left_rows.shape[0] // rows
    c_n = w2.shape[0]
    ob = ob.reshape(1, -1)
    eb = eb.reshape(1, -1)
    return pl.pallas_call(
        functools.partial(pair_kernel, step_rows, group, seqs),
        out_shape=jax.ShapeDtypeStruct(pair.shape, F32),
        grid=(rows // step_rows,),
        in_specs=[
            pl.BlockSpec((step_rows * seqs, left_rows.shape[1]), lambda i: (i, 0)),
            whole(right_cols), whole(w2),
            pl.BlockSpec((step_rows, cols, cz), lambda i: (i, 0, 0)),
            whole(ob), whole(up), whole(eb), whole(dn),
        ],
        out_specs=pl.BlockSpec((step_rows, cols, cz), lambda i: (i, 0, 0)),
        scratch_shapes=[
            pltpu.VMEM(right_cols.shape, BF16),
            pltpu.VMEM(right_cols.shape, BF16),
            pltpu.VMEM((3 * c_n, w2.shape[1]), BF16),
            pltpu.VMEM((3 * cz, up.shape[1]), BF16),
            pltpu.VMEM((up.shape[1], 2 * cz), BF16),
        ],
        compiler_params=PARAMS,
        name="pair_update",
    )(left_rows, right_cols, w2, pair, ob, up, eb, dn)


def spread_heads(
    parts,
    homolog_embedding,
    pair_state,
    probe_projector,
    lookup_projector,
    content_projector,
    sigmoid_projector,
    sigmoid_offset,
    pair_bias_weight,
    mixing_projector,
    mixing_offset,
    first_factor_projector,
    second_factor_projector,
    outer_product_weight,
    outer_product_bias,
    up_weight,
    expand_bias,
    down_weight,
):
    seqs, span, ch = homolog_embedding.shape
    rows, cols, cz = pair_state.shape
    heads = pair_bias_weight.shape[1]
    hw = ch // heads
    own_heads = heads // parts
    hid = first_factor_projector.shape[1]

    bias = bias_tile(pair_state, pair_bias_weight).reshape(parts, own_heads, rows, cols)
    bias = lax.all_to_all(bias, "narrow", 0, 0, tiled=True)
    gathered = [
        lax.all_gather(bias[:, h], "wide", axis=0, tiled=False) for h in range(own_heads)
    ]
    qkv, gate = project(
        homolog_embedding, probe_projector, lookup_projector, content_projector, sigmoid_projector,
        sigmoid_offset, parts, hw,
    )
    qkv = lax.all_to_all(qkv, "narrow", 0, 0, tiled=True)
    att = [
        lax.all_to_all(attention(qkv, gathered[h], h, hw), "narrow", 0, 0, tiled=True)
        for h in range(own_heads)
    ]
    alignment_state_next, left, right = merge(
        att, gate, homolog_embedding, mixing_projector, mixing_offset,
        first_factor_projector, second_factor_projector, rows,
    )
    left = lax.all_gather(left, "narrow", axis=0, tiled=True)
    left = lax.all_to_all(left, "wide", 0, 0, tiled=True)
    right = lax.all_gather(right, "wide", axis=0, tiled=True)
    left = left.reshape(-1, hid, rows)
    all_seqs = left.shape[0]
    left_rows = jnp.transpose(left, (2, 0, 1)).reshape(rows * all_seqs, hid)
    right_cols = jnp.transpose(right, (2, 1, 0)).reshape(cols, hid * all_seqs)
    pair_state_next = pair_update(
        left_rows, right_cols, outer_product_weight.reshape(hid, hid * cz), pair_state,
        outer_product_bias, up_weight, expand_bias, down_weight,
    )
    return (alignment_state_next, pair_state_next)


AXES = ("wide", "narrow")
PLANES, CORES = 4, 2
PARTNER = {1: 2, 2: 1}
OUTWARD = {1: 0, 2: 3}
ORDER = ((0, 1, 2, 3), (1, 0, 2, 3), (2, 3, 1, 0), (3, 2, 1, 0))


def send(x, parts, route):
    pairs = []
    for z in range(PLANES):
        for c in range(CORES):
            for n in range(parts):
                to = route(z, c, n)
                if to is not None:
                    pairs.append(((z * CORES + c) * parts + n, (to[0] * CORES + to[1]) * parts + to[2]))
    return lax.ppermute(x, AXES, pairs)


def exchange(blocks, parts):
    out = [blocks[0]]
    for k in range(1, len(blocks)):
        dn, dc = divmod(k, CORES)
        out.append(send(blocks[k], parts, lambda z, c, n: (z, c ^ dc, n ^ dn)))
    return out


def line_gather(x, parts):
    middle = lambda table: lambda z, c, n: (table[z], c, n) if z in table else None
    near = send(x, parts, lambda z, c, n: (z ^ 1, c, n))
    across = send(x, parts, middle(PARTNER))
    out2 = send(across, parts, middle(OUTWARD))
    far = send(near, parts, middle(PARTNER))
    out3 = send(far, parts, middle(OUTWARD))
    return near, (across, out2), (far, out3)


def head_bias_kernel(group, pair_ref, w_ref, *refs):
    out_refs, w_st = refs[:-1], refs[-1]
    rows, cols, cz = pair_ref.shape
    heads = len(out_refs)
    lanes = heads * group

    @pl.when(pl.program_id(0) == 0)
    def _():
        w = w_ref[...]
        hi = w.astype(BF16).astype(F32)
        row_of = lax.broadcasted_iota(jnp.int32, w.shape, 1) % group
        for i in range(group):
            h = jnp.where(row_of == i, hi, 0.0).astype(BF16)
            l = jnp.where(row_of == i, w - hi, 0.0).astype(BF16)
            for t in range(2):
                w_st[i, t * cz:(t + 1) * cz, 0:lanes] = h
                w_st[i, t * cz:(t + 1) * cz, lanes:2 * lanes] = l

    for g in range(0, rows, group):
        ys = []
        for i in range(group):
            yh, yl = split(norm_rows(pair_ref[g + i]))
            ys += [yh, yl]
        r = mm(jnp.concatenate(ys, axis=1), w_st[...].reshape(group * 2 * cz, 2 * lanes))
        t = (r[:, :lanes] + r[:, lanes:]).T
        for k in range(heads):
            out_refs[k][g:g + group, :] = t[k * group:(k + 1) * group]


def head_bias(pair, w, heads, step=32):
    rows, cols, cz = pair.shape
    group = w.shape[1] // heads
    return pl.pallas_call(
        functools.partial(head_bias_kernel, group),
        out_shape=(jax.ShapeDtypeStruct((rows, cols), F32),) * heads,
        grid=(rows // step,),
        in_specs=[pl.BlockSpec((step, cols, cz), lambda i: (i, 0, 0)), whole(w)],
        out_specs=(pl.BlockSpec((step, cols), lambda i: (i, 0)),) * heads,
        scratch_shapes=[pltpu.VMEM((group, 2 * cz, 2 * heads * group), BF16)],
        compiler_params=PARAMS,
        name="head_bias",
    )(pair, w)


def head_project_kernel(heads, scale, me_ref, x_ref, wq_ref, wk_ref, wv_ref, wg_ref, bg_ref, *refs):
    qkv_refs, (gate_ref, w_t, b_p, w_hi, w_lo) = refs[:heads], refs[heads:]
    ch = x_ref.shape[-1]
    hw = ch // heads

    @pl.when(pl.program_id(0) == 0)
    def _():
        me = me_ref[0]
        for t, (ref, f) in enumerate(((wq_ref, scale), (wk_ref, 1.0), (wv_ref, 1.0), (wg_ref, 1.0))):
            w_t[...] = ref[...].T * f
            for k in range(heads):
                src = pl.ds(pl.multiple_of((me ^ k) * hw, hw), hw)
                hi, lo = split(w_t[src, :])
                at = slice(t * ch + k * hw, t * ch + (k + 1) * hw)
                w_hi[at, :] = hi
                w_lo[at, :] = lo
                if t == 3:
                    b_p[k * hw:(k + 1) * hw, :] = bg_ref[src, :]

    yh, yl = split(norm_rows(x_ref[0]))
    r = mm_nt(w_hi[...], yh) + mm_nt(w_hi[...], yl) + mm_nt(w_lo[...], yh)
    for t in range(3):
        for k in range(heads):
            lo = t * ch + k * hw
            qkv_refs[k][t, 0] = r[lo:lo + hw]
    gate_ref[0] = jax.nn.sigmoid(r[3 * ch:] + b_p[...])


def head_project(me, x, wq, wk, wv, wg, bg, heads):
    seqs, span, ch = x.shape
    hw = ch // heads
    bg = bg.reshape(ch, 1)
    return pl.pallas_call(
        functools.partial(head_project_kernel, heads, 1.0 / math.sqrt(hw)),
        out_shape=(jax.ShapeDtypeStruct((3, seqs, hw, span), F32),) * heads
        + (jax.ShapeDtypeStruct((seqs, ch, span), F32),),
        grid_spec=pltpu.PrefetchScalarGridSpec(
            num_scalar_prefetch=1,
            grid=(seqs,),
            in_specs=[pl.BlockSpec((1, span, ch), lambda s, _: (s, 0, 0))]
            + [whole(a) for a in (wq, wk, wv, wg, bg)],
            out_specs=(pl.BlockSpec((3, 1, hw, span), lambda s, _: (0, s, 0, 0)),) * heads
            + (pl.BlockSpec((1, ch, span), lambda s, _: (s, 0, 0)),),
            scratch_shapes=[
                pltpu.VMEM((ch, ch), F32),
                pltpu.VMEM((ch, 1), F32),
                pltpu.VMEM((4 * ch, ch), BF16),
                pltpu.VMEM((4 * ch, ch), BF16),
            ],
        ),
        compiler_params=PARAMS,
        name="head_project",
    )(me, x, wq, wk, wv, wg, bg)


def stage_kernel(n_ref, *refs):
    pieces, (q_ref, k_ref, v_ref) = refs[:-3], refs[-3:]
    _, _, hw, span = pieces[0].shape
    for p, ref in enumerate(pieces):
        part, core = divmod(p, CORES)
        at = slice(part * span, (part + 1) * span)
        q = ref[0, 0]
        qh = q.astype(BF16).astype(F32)
        q_ref[core, 0, n_ref[0] ^ part] = (
            jnp.concatenate([qh, qh, q - qh, jnp.zeros_like(q)], axis=0).T.astype(BF16)
        )
        hi, lo = split(ref[1, 0])
        k_ref[core, 0, 0:hw, at] = hi
        k_ref[core, 0, hw:2 * hw, at] = lo
        k_ref[core, 0, 2 * hw:3 * hw, at] = hi
        k_ref[core, 0, 3 * hw:4 * hw, at] = jnp.zeros_like(hi)
        v = ref[2, 0]
        vh = v.astype(BF16).astype(F32)
        st = jnp.concatenate([vh, v - vh, jnp.ones((hw, span), F32), jnp.zeros((hw, span), F32)], axis=0)
        v_ref[core, 0, at, :] = st.T.astype(BF16)


def stage(n, pieces, parts):
    _, seqs, hw, span = pieces[0].shape
    return pl.pallas_call(
        stage_kernel,
        out_shape=(
            jax.ShapeDtypeStruct((CORES, seqs, parts, span, 4 * hw), BF16),
            jax.ShapeDtypeStruct((CORES, seqs, 4 * hw, parts * span), BF16),
            jax.ShapeDtypeStruct((CORES, seqs, parts * span, 4 * hw), BF16),
        ),
        grid_spec=pltpu.PrefetchScalarGridSpec(
            num_scalar_prefetch=1,
            grid=(seqs,),
            in_specs=[pl.BlockSpec((3, 1, hw, span), lambda s, _: (0, s, 0, 0)) for _ in pieces],
            out_specs=(
                pl.BlockSpec((CORES, 1, parts, span, 4 * hw), lambda s, _: (0, s, 0, 0, 0)),
                pl.BlockSpec((CORES, 1, 4 * hw, parts * span), lambda s, _: (0, s, 0, 0)),
                pl.BlockSpec((CORES, 1, parts * span, 4 * hw), lambda s, _: (0, s, 0, 0)),
            ),
        ),
        compiler_params=PARAMS,
        name="stage",
    )(n, *pieces)


def head_attention_kernel(hw, at_ref, q_ref, k_ref, v_ref, *refs):
    bias_refs, out_ref = refs[:-2], refs[-1]
    _, parts, rows, _ = bias_refs[0].shape
    cores, seqs = q_ref.shape[:2]
    bias = jnp.concatenate(
        [
            jnp.concatenate([sum(b[h ^ at_ref[2], n] for b in bias_refs) for n in range(parts)], axis=1)
            for h in range(CORES)
        ],
        axis=0,
    )
    for g in range(cores):
        for s in range(seqs):
            scores = mm(q_ref[g, s, 0], k_ref[g, s]) + bias
            top = jnp.max(scores, axis=1, keepdims=True)
            ph, plo = split(jnp.exp(scores - top))
            t = (mm(ph, v_ref[g, s]) + mm(plo, v_ref[g, s])).T
            out_ref[0, g, s] = (t[0:hw] + t[hw:2 * hw]) / t[2 * hw:2 * hw + 1]


def head_attention(at, q, k, v, tiles, prev, hw, step=2):
    cores, seqs, parts, span, _ = q.shape
    return pl.pallas_call(
        functools.partial(head_attention_kernel, hw),
        out_shape=jax.ShapeDtypeStruct(prev.shape, F32),
        grid_spec=pltpu.PrefetchScalarGridSpec(
            num_scalar_prefetch=1,
            grid=(seqs // step,),
            in_specs=[
                pl.BlockSpec((cores, step, 1, span, 4 * hw), lambda s, at: (0, s, at[0], 0, 0)),
                pl.BlockSpec((cores, step, 4 * hw, parts * span), lambda s, at: (0, s, 0, 0)),
                pl.BlockSpec((cores, step, parts * span, 4 * hw), lambda s, at: (0, s, 0, 0)),
            ]
            + [whole(b) for b in tiles]
            + [pl.BlockSpec(memory_space=pl.ANY)],
            out_specs=pl.BlockSpec((1, cores, step, hw, span), lambda s, at: (at[1], 0, s, 0, 0)),
        ),
        input_output_aliases={4 + len(tiles): 0},
        compiler_params=PARAMS,
        name="head_attention",
    )(at, q, k, v, *tiles, prev)


def head_merge_kernel(heads, me_ref, *refs):
    pieces = refs[:heads]
    gate_ref, x_ref, wm_ref, bm_ref, f1_ref, f2_ref = refs[heads:heads + 6]
    next_ref, left_refs, right_ref = refs[heads + 6], refs[heads + 7:heads + 9], refs[heads + 9]
    m_hi, m_lo, f_st = refs[heads + 10:]
    _, hw, span = pieces[0].shape
    hid = f1_ref.shape[1]
    rows = span // CORES

    @pl.when(pl.program_id(0) == 0)
    def _():
        for k in range(heads):
            hi, lo = split(wm_ref[pl.ds(pl.multiple_of((me_ref[0] ^ k) * hw, hw), hw), :])
            m_hi[k * hw:(k + 1) * hw, :] = hi
            m_lo[k * hw:(k + 1) * hw, :] = lo
        hi, lo = split(jnp.concatenate([f1_ref[...], f2_ref[...]], axis=1).T)
        f_st[0:2 * hid, :] = hi
        f_st[2 * hid:4 * hid, :] = lo

    a = jnp.concatenate([p[0] for p in pieces], axis=0)
    ah, al = split((a * gate_ref[0]).T)
    y = x_ref[0] + (mm(ah, m_hi[...]) + mm(al, m_hi[...]) + mm(ah, m_lo[...])) + bm_ref[...]
    next_ref[0] = y
    zh, zl = split(norm_rows(y))
    p = mm_nt(f_st[...], zh)
    p = p[:2 * hid] + p[2 * hid:] + mm_nt(f_st[0:2 * hid, :], zl)
    swap = me_ref[1] == 1
    left_refs[0][0] = jnp.where(swap, p[:hid, rows:], p[:hid, :rows])
    left_refs[1][0] = jnp.where(swap, p[:hid, :rows], p[:hid, rows:])
    right_ref[0] = p[hid:]


def head_merge(me, pieces, gate, x, wm, bm, f1, f2):
    seqs, span, ch = x.shape
    heads = len(pieces)
    hw = ch // heads
    hid = f1.shape[1]
    rows = span // CORES
    bm = bm.reshape(1, ch)
    return pl.pallas_call(
        functools.partial(head_merge_kernel, heads),
        out_shape=(jax.ShapeDtypeStruct(x.shape, F32),)
        + (jax.ShapeDtypeStruct((seqs, hid, rows), F32),) * CORES
        + (jax.ShapeDtypeStruct((seqs, hid, span), F32),),
        grid_spec=pltpu.PrefetchScalarGridSpec(
            num_scalar_prefetch=1,
            grid=(seqs,),
            in_specs=[pl.BlockSpec((1, hw, span), lambda s, _: (s, 0, 0)) for _ in pieces]
            + [
                pl.BlockSpec((1, ch, span), lambda s, _: (s, 0, 0)),
                pl.BlockSpec((1, span, ch), lambda s, _: (s, 0, 0)),
            ]
            + [whole(a) for a in (wm, bm, f1, f2)],
            out_specs=(pl.BlockSpec((1, span, ch), lambda s, _: (s, 0, 0)),)
            + (pl.BlockSpec((1, hid, rows), lambda s, _: (s, 0, 0)),) * CORES
            + (pl.BlockSpec((1, hid, span), lambda s, _: (s, 0, 0)),),
            scratch_shapes=[
                pltpu.VMEM((ch, ch), BF16),
                pltpu.VMEM((ch, ch), BF16),
                pltpu.VMEM((4 * hid, ch), BF16),
            ],
        ),
        compiler_params=PARAMS,
        name="head_merge",
    )(me, *pieces, gate, x, wm, bm, f1, f2)


def pack_kernel(slots_ref, *refs):
    left_refs, (own_ref, sib_ref, lr_ref, rc_ref, right) = refs[:-5], refs[-5:]
    cores, seqs, hid, rows = left_refs[0].shape
    slots = len(left_refs) * cores
    for i in range(own_ref.shape[0]):
        at = slots_ref[i] * cores
        for t, ref in enumerate((own_ref, sib_ref)):
            right[pl.ds((at + t) * seqs, seqs)] = ref[i]
    rt = jnp.concatenate([right[:, d, :] for d in range(hid)], axis=0)
    rc_ref[...] = rt.T
    for p, ref in enumerate(left_refs):
        for t in range(cores):
            for s in range(seqs):
                at = (p * cores + t) * seqs + s
                lr_ref[pl.ds(at, rows, stride=slots * seqs), :] = ref[t, s].T


def pack(slots, lefts, own, sib):
    cores, seqs, hid, rows = lefts[0].shape
    planes, _, _, cols = own.shape
    total = planes * cores * seqs
    return pl.pallas_call(
        pack_kernel,
        out_shape=(
            jax.ShapeDtypeStruct((rows * total, hid), F32),
            jax.ShapeDtypeStruct((cols, hid * total), F32),
        ),
        in_specs=[pl.BlockSpec(memory_space=pltpu.SMEM)]
        + [pl.BlockSpec(memory_space=pltpu.VMEM)] * (len(lefts) + 2),
        out_specs=(pl.BlockSpec(memory_space=pltpu.VMEM),) * 2,
        scratch_shapes=[pltpu.VMEM((total, hid, cols), F32)],
        compiler_params=PARAMS,
        name="pack",
    )(slots, *lefts, own, sib)


def after(x, *deps):
    return lax.optimization_barrier((x, deps))[0]


def per_head(
    parts,
    homolog_embedding,
    pair_state,
    probe_projector,
    lookup_projector,
    content_projector,
    sigmoid_projector,
    sigmoid_offset,
    pair_bias_weight,
    mixing_projector,
    mixing_offset,
    first_factor_projector,
    second_factor_projector,
    outer_product_weight,
    outer_product_bias,
    up_weight,
    expand_bias,
    down_weight,
):
    seqs, span, ch = homolog_embedding.shape
    rows, cols, cz = pair_state.shape
    heads = pair_bias_weight.shape[1]
    hw = ch // heads
    hid = first_factor_projector.shape[1]
    wide = lax.axis_index("wide")
    n = lax.axis_index("narrow")
    z, c = wide // CORES, wide % CORES
    me = n * CORES + c
    order = jnp.asarray(ORDER, jnp.int32)[z]

    group = 16
    lane = jnp.arange(heads * group, dtype=jnp.int32) // group
    own_first = jnp.take(pair_bias_weight, lane ^ me, axis=1)
    tiles = head_bias(pair_state, own_first, heads)
    *qkv, gate = head_project(
        me[None], after(homolog_embedding, tiles[0]), probe_projector, lookup_projector, content_projector,
        sigmoid_projector, sigmoid_offset, heads,
    )
    tiles = after(exchange(tiles, parts), gate)
    bias = jnp.stack(
        [jnp.stack([tiles[p * CORES + r] for p in range(parts)]) for r in range(CORES)]
    )
    near, second, third = line_gather(bias, parts)
    qkv = exchange(after(qkv, bias), parts)
    q, k, v = stage(n[None], after(qkv, near, second[0]), parts)
    att = jnp.zeros((parts, CORES, seqs, hw, span), F32)
    bias = after(bias, second[1], third[0])
    for i, tile in enumerate(((bias,), (near,), second, third)):
        at = jnp.stack([order[i], order[i] ^ n, c])
        att = head_attention(at, q, k, v, tile, att, hw)
    pieces = exchange([att[p, r] for p in range(parts) for r in range(CORES)], parts)
    alignment_state_next, left_a, left_b, right = head_merge(
        jnp.stack([me, c]), pieces, gate, homolog_embedding, mixing_projector, mixing_offset,
        first_factor_projector, second_factor_projector,
    )
    turn = lambda z0, c0, n0: (n0, c0, z0)
    left_a, left_b = send(left_a, parts, turn), send(left_b, parts, turn)
    sibling = lambda z0, c0, n0: (z0, c0 ^ 1, n0)
    left = jnp.stack([left_a, send(left_b, parts, sibling)])
    near, second, third = line_gather(right, parts)
    lefts = [left] + [
        send(left, parts, lambda z0, c0, n0, d=d: (z0, c0, n0 ^ d)) for d in range(1, parts)
    ]
    own = jnp.stack([right, near, sum(second), sum(third)])
    left_rows, right_cols = pack(order ^ n, lefts, own, send(own, parts, sibling))
    pair_state_next = pair_update(
        left_rows, right_cols, outer_product_weight.reshape(hid, hid * cz), pair_state,
        outer_product_bias, up_weight, expand_bias, down_weight,
    )
    return (alignment_state_next, pair_state_next)


def step(mesh, *args):
    wide, parts = mesh.shape["wide"], mesh.shape["narrow"]
    heads = args[7].shape[1]
    if wide == PLANES * CORES and parts == PLANES and heads == CORES * parts:
        return per_head(parts, *args)
    return spread_heads(parts, *args)


def solution(mesh):
    placed = (P("wide", "narrow", None), P("wide", "narrow", None)) + (P(),) * 15
    return jax.shard_map(
        functools.partial(step, mesh),
        mesh=mesh,
        in_specs=placed,
        out_specs=(P("wide", "narrow", None), P("wide", "narrow", None)),
        check_vma=False,
    )
```

```python
import functools
import math

import jax
import jax.numpy as jnp
from jax import lax
from jax.experimental import pallas as pl
from jax.experimental.pallas import tpu as pltpu
from jax.sharding import PartitionSpec as P


F32, BF16 = jnp.float32, jnp.bfloat16
PARAMS = pltpu.CompilerParams(vmem_limit_bytes=60 * 2**20)


def split(x):
    hi = x.astype(BF16)
    lo = (x - hi.astype(F32)).astype(BF16)
    return hi, lo


def mm(a, b):
    return jnp.dot(a, b, preferred_element_type=F32)


def mm_nt(a, b):
    return lax.dot_general(a, b, (((1,), (1,)), ((), ())), preferred_element_type=F32)


def norm_rows(x):
    mean = jnp.mean(x, axis=-1, keepdims=True)
    c = x - mean
    var = jnp.mean(c * c, axis=-1, keepdims=True)
    return c * lax.rsqrt(var + 1e-05)


def whole(a):
    return pl.BlockSpec(a.shape, lambda *_: (0,) * a.ndim, pipeline_mode=pl.Buffered(1))


def bias_kernel(pair_ref, w_ref, out_ref):
    rows, _, _ = pair_ref.shape
    heads = w_ref.shape[1]
    wh, wl = split(w_ref[...].T)
    lhs = jnp.concatenate(
        [jnp.concatenate([wh, wh], axis=1), jnp.concatenate([wl, wl], axis=1)], axis=0
    )
    for i in range(rows):
        yh, yl = split(norm_rows(pair_ref[i]))
        r = mm_nt(lhs, jnp.concatenate([yh, yl], axis=1))
        out_ref[:, i, :] = r[:heads] + r[heads:]


def bias_tile(pair, w, step=8):
    rows, cols, cz = pair.shape
    heads = w.shape[1]
    return pl.pallas_call(
        bias_kernel,
        out_shape=jax.ShapeDtypeStruct((heads, rows, cols), F32),
        grid=(rows // step,),
        in_specs=[pl.BlockSpec((step, cols, cz), lambda i: (i, 0, 0)), whole(w)],
        out_specs=pl.BlockSpec((heads, step, cols), lambda i: (0, i, 0)),
        compiler_params=PARAMS,
        name="bias_tile",
    )(pair, w)


def project_kernel(parts, scale, x_ref, wq_ref, wk_ref, wv_ref, wg_ref, bg_ref, qkv_ref, gate_ref, w_hi, w_lo):
    ch = x_ref.shape[-1]
    own = ch // parts

    @pl.when(pl.program_id(0) == 0)
    def _():
        for t, (ref, f) in enumerate(((wq_ref, scale), (wk_ref, 1.0), (wv_ref, 1.0), (wg_ref, 1.0))):
            hi, lo = split(ref[...].T * f)
            w_hi[t * ch:(t + 1) * ch, :] = hi
            w_lo[t * ch:(t + 1) * ch, :] = lo

    yh, yl = split(norm_rows(x_ref[0]))
    r = mm_nt(w_hi[...], yh) + mm_nt(w_hi[...], yl) + mm_nt(w_lo[...], yh)
    for t in range(3):
        for n in range(parts):
            lo = t * ch + n * own
            qkv_ref[n, t, 0] = r[lo:lo + own]
    gate_ref[0] = jax.nn.sigmoid(r[3 * ch:] + bg_ref[...])


def project(x, wq, wk, wv, wg, bg, parts, head_width):
    seqs, span, ch = x.shape
    own = ch // parts
    bg = bg.reshape(ch, 1)
    return pl.pallas_call(
        functools.partial(project_kernel, parts, 1.0 / math.sqrt(head_width)),
        out_shape=(
            jax.ShapeDtypeStruct((parts, 3, seqs, own, span), F32),
            jax.ShapeDtypeStruct((seqs, ch, span), F32),
        ),
        grid=(seqs,),
        in_specs=[pl.BlockSpec((1, span, ch), lambda s: (s, 0, 0))] + [whole(a) for a in (wq, wk, wv, wg, bg)],
        out_specs=(
            pl.BlockSpec((parts, 3, 1, own, span), lambda s: (0, 0, s, 0, 0)),
            pl.BlockSpec((1, ch, span), lambda s: (s, 0, 0)),
        ),
        scratch_shapes=[pltpu.VMEM((4 * ch, ch), BF16), pltpu.VMEM((4 * ch, ch), BF16)],
        compiler_params=PARAMS,
        name="project",
    )(x, wq, wk, wv, wg, bg)


def attention_kernel(hw, q_ref, k_ref, v_ref, bias_ref, out_ref, ks, vs):
    parts = k_ref.shape[0]
    span = k_ref.shape[-1]
    s = pl.program_id(1)

    @pl.when(pl.program_id(0) == 0)
    def _():
        for n in range(parts):
            at = slice(n * span, (n + 1) * span)
            hi, lo = split(k_ref[n, 0, 0])
            ks[s, 0:hw, at] = hi
            ks[s, hw:2 * hw, at] = lo
            ks[s, 2 * hw:3 * hw, at] = hi
            v = v_ref[n, 0, 0]
            vh = v.astype(BF16).astype(F32)
            st = jnp.concatenate([vh, v - vh, jnp.ones((hw, span), F32), jnp.zeros((hw, span), F32)], axis=0)
            vs[s, at, :] = st.T.astype(BF16)

    q = q_ref[0, 0, 0]
    qh = q.astype(BF16).astype(F32)
    qst = jnp.concatenate([qh, qh, q - qh, jnp.zeros_like(q)], axis=0).T[:, :3 * hw].astype(BF16)
    bias = jnp.concatenate(
        [
            jnp.concatenate([bias_ref[w, n] for n in range(parts)], axis=1)
            for w in range(bias_ref.shape[0])
        ],
        axis=0,
    )
    scores = mm(qst, ks[s]) + bias
    top = jnp.max(scores, axis=1, keepdims=True)
    ph, plo = split(jnp.exp(scores - top))
    t = (mm(ph, vs[s]) + mm(plo, vs[s])).T
    out_ref[0, 0] = (t[0:hw] + t[hw:2 * hw]) / t[2 * hw:2 * hw + 1]


def attention(qkv, bias, head, hw):
    parts, _, seqs, _, span = qkv.shape
    _, _, rows, _ = bias.shape
    per = span // rows
    return pl.pallas_call(
        functools.partial(attention_kernel, hw),
        out_shape=jax.ShapeDtypeStruct((parts, seqs, hw, span), F32),
        grid=(parts, seqs),
        in_specs=[
            pl.BlockSpec((1, 1, 1, hw, span), lambda b, s: (b, 0, s, head, 0)),
            pl.BlockSpec((parts, 1, 1, hw, span), lambda b, s: (0, 1, s, head, 0)),
            pl.BlockSpec((parts, 1, 1, hw, span), lambda b, s: (0, 2, s, head, 0)),
            pl.BlockSpec((per, parts, rows, span), lambda b, s: (b, 0, 0, 0)),
        ],
        out_specs=pl.BlockSpec((1, 1, hw, span), lambda b, s: (b, s, 0, 0)),
        scratch_shapes=[
            pltpu.VMEM((seqs, 3 * hw, parts * span), BF16),
            pltpu.VMEM((seqs, parts * span, 4 * hw), BF16),
        ],
        compiler_params=PARAMS,
        name="attention",
    )(qkv, qkv, qkv, bias)


def merge_kernel(*refs):
    heads = len(refs) - 12
    att = refs[:heads]
    gate_ref, x_ref, wm_ref, bm_ref, f1_ref, f2_ref, next_ref, left_ref, right_ref, m_hi, m_lo, f_st = refs[heads:]
    parts, _, _, _ = att[0].shape
    hid = f1_ref.shape[1]
    blocks, _, _, rows = left_ref.shape

    @pl.when(pl.program_id(0) == 0)
    def _():
        hi, lo = split(wm_ref[...])
        m_hi[...] = hi
        m_lo[...] = lo
        hi, lo = split(jnp.concatenate([f1_ref[...], f2_ref[...]], axis=1).T)
        f_st[0:2 * hid, :] = hi
        f_st[2 * hid:4 * hid, :] = lo

    a = jnp.concatenate([att[h][n, 0] for n in range(parts) for h in range(heads)], axis=0)
    ah, al = split((a * gate_ref[0]).T)
    y = x_ref[0] + (mm(ah, m_hi[...]) + mm(al, m_hi[...]) + mm(ah, m_lo[...])) + bm_ref[...]
    next_ref[0] = y
    zh, zl = split(norm_rows(y))
    p = mm_nt(f_st[...], zh)
    p = p[:2 * hid] + p[2 * hid:] + mm_nt(f_st[0:2 * hid, :], zl)
    for b in range(blocks):
        left_ref[b, 0] = p[:hid, b * rows:(b + 1) * rows]
    right_ref[0] = p[hid:]


def merge(att, gate, x, wm, bm, f1, f2, rows):
    seqs, span, ch = x.shape
    parts, _, hw, _ = att[0].shape
    hid = f1.shape[1]
    bm = bm.reshape(1, ch)
    blocks = span // rows
    return pl.pallas_call(
        merge_kernel,
        out_shape=(
            jax.ShapeDtypeStruct(x.shape, F32),
            jax.ShapeDtypeStruct((blocks, seqs, hid, rows), F32),
            jax.ShapeDtypeStruct((seqs, hid, span), F32),
        ),
        grid=(seqs,),
        in_specs=[pl.BlockSpec((parts, 1, hw, span), lambda s: (0, s, 0, 0)) for _ in att]
        + [
            pl.BlockSpec((1, ch, span), lambda s: (s, 0, 0)),
            pl.BlockSpec((1, span, ch), lambda s: (s, 0, 0)),
        ]
        + [whole(a) for a in (wm, bm, f1, f2)],
        out_specs=(
            pl.BlockSpec((1, span, ch), lambda s: (s, 0, 0)),
            pl.BlockSpec((blocks, 1, hid, rows), lambda s: (0, s, 0, 0)),
            pl.BlockSpec((1, hid, span), lambda s: (s, 0, 0)),
        ),
        scratch_shapes=[
            pltpu.VMEM((ch, ch), BF16),
            pltpu.VMEM((ch, ch), BF16),
            pltpu.VMEM((4 * hid, ch), BF16),
        ],
        compiler_params=PARAMS,
        name="merge",
    )(*att, gate, x, wm, bm, f1, f2)


def pair_kernel(
    step_rows, group, seqs, left_ref, right_ref, w_ref, pair_ref, ob_ref, up_ref, eb_ref, dn_ref,
    out_ref, r_hi, r_lo, w_st, up_st, dn_st,
):
    _, cols, cz = pair_ref.shape
    c_n = w_ref.shape[0]
    d_n = w_ref.shape[1] // cz

    @pl.when(pl.program_id(0) == 0)
    def _():
        hi, lo = split(right_ref[...])
        r_hi[...] = hi
        r_lo[...] = lo
        hi, lo = split(w_ref[...])
        w_st[0:c_n, :] = hi
        w_st[c_n:2 * c_n, :] = lo
        w_st[2 * c_n:3 * c_n, :] = hi
        hi, lo = split(up_ref[...])
        up_st[0:cz, :] = hi
        up_st[cz:2 * cz, :] = hi
        up_st[2 * cz:3 * cz, :] = lo
        hi, lo = split(dn_ref[...])
        dn_st[:, 0:cz] = hi
        dn_st[:, cz:2 * cz] = lo

    def body(p, carry):
        lrow = left_ref[pl.ds(pl.multiple_of(p * group * seqs, group * seqs), group * seqs), :]
        lhi = lrow.astype(BF16).astype(F32)
        u = mm(jnp.concatenate([lhi, lhi, lrow - lhi], axis=1).astype(BF16), w_st[...])
        his, los = [], []
        for q in range(group):
            sub = u[q * seqs:(q + 1) * seqs, :]
            hi, lo = split(jnp.concatenate([sub[:, d * cz:(d + 1) * cz] for d in range(d_n)], axis=0))
            his.append(hi)
            los.append(lo)
        mids = []
        for q in range(0, group, 2):
            cross = mm(r_lo[...], jnp.concatenate(his[q:q + 2], axis=1))
            for i in range(2):
                a = mm(r_hi[...], jnp.concatenate([his[q + i], los[q + i]], axis=1))
                o = a[:, :cz] + a[:, cz:] + cross[:, i * cz:(i + 1) * cz]
                mids.append(pair_ref[group * p + q + i] + o / seqs + ob_ref[...])
        for q in range(0, group, 2):
            mid = jnp.concatenate(mids[q:q + 2], axis=0)
            yh, yl = split(norm_rows(mid))
            h = mm(jnp.concatenate([yh, yl, yh], axis=1), up_st[...])
            hh, hl = split(jnp.maximum(h + eb_ref[...], 0.0))
            a = mm(hh, dn_st[...])
            o = mid + (a[:, :cz] + a[:, cz:] + mm(hl, dn_st[:, 0:cz]))
            for i in range(2):
                out_ref[group * p + q + i] = o[i * cols:(i + 1) * cols]
        return carry

    lax.fori_loop(0, step_rows // group, body, 0)


def pair_update(left_rows, right_cols, w2, pair, ob, up, eb, dn, step_rows=8, group=4):
    rows, cols, cz = pair.shape
    seqs = left_rows.shape[0] // rows
    c_n = w2.shape[0]
    ob = ob.reshape(1, -1)
    eb = eb.reshape(1, -1)
    return pl.pallas_call(
        functools.partial(pair_kernel, step_rows, group, seqs),
        out_shape=jax.ShapeDtypeStruct(pair.shape, F32),
        grid=(rows // step_rows,),
        in_specs=[
            pl.BlockSpec((step_rows * seqs, left_rows.shape[1]), lambda i: (i, 0)),
            whole(right_cols), whole(w2),
            pl.BlockSpec((step_rows, cols, cz), lambda i: (i, 0, 0)),
            whole(ob), whole(up), whole(eb), whole(dn),
        ],
        out_specs=pl.BlockSpec((step_rows, cols, cz), lambda i: (i, 0, 0)),
        scratch_shapes=[
            pltpu.VMEM(right_cols.shape, BF16),
            pltpu.VMEM(right_cols.shape, BF16),
            pltpu.VMEM((3 * c_n, w2.shape[1]), BF16),
            pltpu.VMEM((3 * cz, up.shape[1]), BF16),
            pltpu.VMEM((up.shape[1], 2 * cz), BF16),
        ],
        compiler_params=PARAMS,
        name="pair_update",
    )(left_rows, right_cols, w2, pair, ob, up, eb, dn)


def spread_heads(
    parts,
    homolog_embedding,
    pair_state,
    probe_projector,
    lookup_projector,
    content_projector,
    sigmoid_projector,
    sigmoid_offset,
    pair_bias_weight,
    mixing_projector,
    mixing_offset,
    first_factor_projector,
    second_factor_projector,
    outer_product_weight,
    outer_product_bias,
    up_weight,
    expand_bias,
    down_weight,
):
    _, _, ch = homolog_embedding.shape
    rows, cols, cz = pair_state.shape
    heads = pair_bias_weight.shape[1]
    hw = ch // heads
    own_heads = heads // parts
    hid = first_factor_projector.shape[1]

    bias = bias_tile(pair_state, pair_bias_weight).reshape(parts, own_heads, rows, cols)
    bias = lax.all_to_all(bias, "narrow", 0, 0, tiled=True)
    gathered = [
        lax.all_gather(bias[:, h], "wide", axis=0, tiled=False) for h in range(own_heads)
    ]
    qkv, gate = project(
        homolog_embedding, probe_projector, lookup_projector, content_projector, sigmoid_projector,
        sigmoid_offset, parts, hw,
    )
    qkv = lax.all_to_all(qkv, "narrow", 0, 0, tiled=True)
    att = [
        lax.all_to_all(attention(qkv, gathered[h], h, hw), "narrow", 0, 0, tiled=True)
        for h in range(own_heads)
    ]
    alignment_state_next, left, right = merge(
        att, gate, homolog_embedding, mixing_projector, mixing_offset,
        first_factor_projector, second_factor_projector, rows,
    )
    left = lax.all_gather(left, "narrow", axis=0, tiled=True)
    left = lax.all_to_all(left, "wide", 0, 0, tiled=True)
    right = lax.all_gather(right, "wide", axis=0, tiled=True)
    left = left.reshape(-1, hid, rows)
    all_seqs = left.shape[0]
    left_rows = jnp.transpose(left, (2, 0, 1)).reshape(rows * all_seqs, hid)
    right_cols = jnp.transpose(right, (2, 1, 0)).reshape(cols, hid * all_seqs)
    pair_state_next = pair_update(
        left_rows, right_cols, outer_product_weight.reshape(hid, hid * cz), pair_state,
        outer_product_bias, up_weight, expand_bias, down_weight,
    )
    return (alignment_state_next, pair_state_next)


AXES = ("wide", "narrow")
PLANES, CORES = 4, 2
PARTNER = {1: 2, 2: 1}
OUTWARD = {1: 0, 2: 3}
ORDER = ((0, 1, 2, 3), (1, 0, 2, 3), (2, 3, 1, 0), (3, 2, 1, 0))


def send(x, parts, route):
    pairs = []
    for z in range(PLANES):
        for c in range(CORES):
            for n in range(parts):
                to = route(z, c, n)
                if to is not None:
                    pairs.append(((z * CORES + c) * parts + n, (to[0] * CORES + to[1]) * parts + to[2]))
    return lax.ppermute(x, AXES, pairs)


def exchange(blocks, parts):
    out = [blocks[0]]
    for k in range(1, len(blocks)):
        dn, dc = divmod(k, CORES)
        out.append(send(blocks[k], parts, lambda z, c, n: (z, c ^ dc, n ^ dn)))
    return out


def line_gather(x, parts):
    middle = lambda table: lambda z, c, n: (table[z], c, n) if z in table else None
    near = send(x, parts, lambda z, c, n: (z ^ 1, c, n))
    across = send(x, parts, middle(PARTNER))
    out2 = send(across, parts, middle(OUTWARD))
    far = send(near, parts, middle(PARTNER))
    out3 = send(far, parts, middle(OUTWARD))
    return near, (across, out2), (far, out3)


def head_bias_kernel(group, pair_ref, w_ref, *refs):
    out_refs, w_st = refs[:-1], refs[-1]
    rows, _, cz = pair_ref.shape
    heads = len(out_refs)
    lanes = heads * group

    @pl.when(pl.program_id(0) == 0)
    def _():
        w = w_ref[...]
        hi = w.astype(BF16).astype(F32)
        row_of = lax.broadcasted_iota(jnp.int32, w.shape, 1) % group
        for i in range(group):
            h = jnp.where(row_of == i, hi, 0.0).astype(BF16)
            l = jnp.where(row_of == i, w - hi, 0.0).astype(BF16)
            for t in range(2):
                w_st[i, t * cz:(t + 1) * cz, 0:lanes] = h
                w_st[i, t * cz:(t + 1) * cz, lanes:2 * lanes] = l

    for g in range(0, rows, group):
        ys = []
        for i in range(group):
            yh, yl = split(norm_rows(pair_ref[g + i]))
            ys += [yh, yl]
        r = mm(jnp.concatenate(ys, axis=1), w_st[...].reshape(group * 2 * cz, 2 * lanes))
        t = (r[:, :lanes] + r[:, lanes:]).T
        for k in range(heads):
            out_refs[k][g:g + group, :] = t[k * group:(k + 1) * group]


def head_bias(pair, w, heads, step=32):
    rows, cols, cz = pair.shape
    group = w.shape[1] // heads
    return pl.pallas_call(
        functools.partial(head_bias_kernel, group),
        out_shape=(jax.ShapeDtypeStruct((rows, cols), F32),) * heads,
        grid=(rows // step,),
        in_specs=[pl.BlockSpec((step, cols, cz), lambda i: (i, 0, 0)), whole(w)],
        out_specs=(pl.BlockSpec((step, cols), lambda i: (i, 0)),) * heads,
        scratch_shapes=[pltpu.VMEM((group, 2 * cz, 2 * heads * group), BF16)],
        compiler_params=PARAMS,
        name="head_bias",
    )(pair, w)


def head_project_kernel(heads, scale, me_ref, x_ref, wq_ref, wk_ref, wv_ref, wg_ref, bg_ref, *refs):
    qkv_refs, (gate_ref, w_t, b_p, w_hi, w_lo) = refs[:heads], refs[heads:]
    ch = x_ref.shape[-1]
    hw = ch // heads

    @pl.when(pl.program_id(0) == 0)
    def _():
        me = me_ref[0]
        for t, (ref, f) in enumerate(((wq_ref, scale), (wk_ref, 1.0), (wv_ref, 1.0), (wg_ref, 1.0))):
            w_t[...] = ref[...].T * f
            for k in range(heads):
                src = pl.ds(pl.multiple_of((me ^ k) * hw, hw), hw)
                hi, lo = split(w_t[src, :])
                at = slice(t * ch + k * hw, t * ch + (k + 1) * hw)
                w_hi[at, :] = hi
                w_lo[at, :] = lo
                if t == 3:
                    b_p[k * hw:(k + 1) * hw, :] = bg_ref[src, :]

    yh, yl = split(norm_rows(x_ref[0]))
    r = mm_nt(w_hi[...], yh) + mm_nt(w_hi[...], yl) + mm_nt(w_lo[...], yh)
    for t in range(3):
        for k in range(heads):
            lo = t * ch + k * hw
            qkv_refs[k][t, 0] = r[lo:lo + hw]
    gate_ref[0] = jax.nn.sigmoid(r[3 * ch:] + b_p[...])


def head_project(me, x, wq, wk, wv, wg, bg, heads):
    seqs, span, ch = x.shape
    hw = ch // heads
    bg = bg.reshape(ch, 1)
    return pl.pallas_call(
        functools.partial(head_project_kernel, heads, 1.0 / math.sqrt(hw)),
        out_shape=(jax.ShapeDtypeStruct((3, seqs, hw, span), F32),) * heads
        + (jax.ShapeDtypeStruct((seqs, ch, span), F32),),
        grid_spec=pltpu.PrefetchScalarGridSpec(
            num_scalar_prefetch=1,
            grid=(seqs,),
            in_specs=[pl.BlockSpec((1, span, ch), lambda s, _: (s, 0, 0))]
            + [whole(a) for a in (wq, wk, wv, wg, bg)],
            out_specs=(pl.BlockSpec((3, 1, hw, span), lambda s, _: (0, s, 0, 0)),) * heads
            + (pl.BlockSpec((1, ch, span), lambda s, _: (s, 0, 0)),),
            scratch_shapes=[
                pltpu.VMEM((ch, ch), F32),
                pltpu.VMEM((ch, 1), F32),
                pltpu.VMEM((4 * ch, ch), BF16),
                pltpu.VMEM((4 * ch, ch), BF16),
            ],
        ),
        compiler_params=PARAMS,
        name="head_project",
    )(me, x, wq, wk, wv, wg, bg)


def stage_kernel(n_ref, *refs):
    pieces, (q_ref, k_ref, v_ref) = refs[:-3], refs[-3:]
    _, _, hw, span = pieces[0].shape
    for p, ref in enumerate(pieces):
        part, core = divmod(p, CORES)
        at = slice(part * span, (part + 1) * span)
        q = ref[0, 0]
        qh = q.astype(BF16).astype(F32)
        q_ref[core, 0, n_ref[0] ^ part] = (
            jnp.concatenate([qh, qh, q - qh, jnp.zeros_like(q)], axis=0).T.astype(BF16)
        )
        hi, lo = split(ref[1, 0])
        k_ref[core, 0, 0:hw, at] = hi
        k_ref[core, 0, hw:2 * hw, at] = lo
        k_ref[core, 0, 2 * hw:3 * hw, at] = hi
        k_ref[core, 0, 3 * hw:4 * hw, at] = jnp.zeros_like(hi)
        v = ref[2, 0]
        vh = v.astype(BF16).astype(F32)
        st = jnp.concatenate([vh, v - vh, jnp.ones((hw, span), F32), jnp.zeros((hw, span), F32)], axis=0)
        v_ref[core, 0, at, :] = st.T.astype(BF16)


def stage(n, pieces, parts):
    _, seqs, hw, span = pieces[0].shape
    return pl.pallas_call(
        stage_kernel,
        out_shape=(
            jax.ShapeDtypeStruct((CORES, seqs, parts, span, 4 * hw), BF16),
            jax.ShapeDtypeStruct((CORES, seqs, 4 * hw, parts * span), BF16),
            jax.ShapeDtypeStruct((CORES, seqs, parts * span, 4 * hw), BF16),
        ),
        grid_spec=pltpu.PrefetchScalarGridSpec(
            num_scalar_prefetch=1,
            grid=(seqs,),
            in_specs=[pl.BlockSpec((3, 1, hw, span), lambda s, _: (0, s, 0, 0)) for _ in pieces],
            out_specs=(
                pl.BlockSpec((CORES, 1, parts, span, 4 * hw), lambda s, _: (0, s, 0, 0, 0)),
                pl.BlockSpec((CORES, 1, 4 * hw, parts * span), lambda s, _: (0, s, 0, 0)),
                pl.BlockSpec((CORES, 1, parts * span, 4 * hw), lambda s, _: (0, s, 0, 0)),
            ),
        ),
        compiler_params=PARAMS,
        name="stage",
    )(n, *pieces)


def head_attention_kernel(hw, at_ref, q_ref, k_ref, v_ref, *refs):
    bias_refs, out_ref = refs[:-2], refs[-1]
    _, parts, _, _ = bias_refs[0].shape
    cores, seqs = q_ref.shape[:2]
    bias = jnp.concatenate(
        [
            jnp.concatenate([sum(b[h ^ at_ref[2], n] for b in bias_refs) for n in range(parts)], axis=1)
            for h in range(CORES)
        ],
        axis=0,
    )
    for g in range(cores):
        for s in range(seqs):
            scores = mm(q_ref[g, s, 0], k_ref[g, s]) + bias
            top = jnp.max(scores, axis=1, keepdims=True)
            ph, plo = split(jnp.exp(scores - top))
            t = (mm(ph, v_ref[g, s]) + mm(plo, v_ref[g, s])).T
            out_ref[0, g, s] = (t[0:hw] + t[hw:2 * hw]) / t[2 * hw:2 * hw + 1]


def head_attention(at, q, k, v, tiles, prev, hw, step=2):
    cores, seqs, parts, span, _ = q.shape
    return pl.pallas_call(
        functools.partial(head_attention_kernel, hw),
        out_shape=jax.ShapeDtypeStruct(prev.shape, F32),
        grid_spec=pltpu.PrefetchScalarGridSpec(
            num_scalar_prefetch=1,
            grid=(seqs // step,),
            in_specs=[
                pl.BlockSpec((cores, step, 1, span, 4 * hw), lambda s, at: (0, s, at[0], 0, 0)),
                pl.BlockSpec((cores, step, 4 * hw, parts * span), lambda s, at: (0, s, 0, 0)),
                pl.BlockSpec((cores, step, parts * span, 4 * hw), lambda s, at: (0, s, 0, 0)),
            ]
            + [whole(b) for b in tiles]
            + [pl.BlockSpec(memory_space=pl.ANY)],
            out_specs=pl.BlockSpec((1, cores, step, hw, span), lambda s, at: (at[1], 0, s, 0, 0)),
        ),
        input_output_aliases={4 + len(tiles): 0},
        compiler_params=PARAMS,
        name="head_attention",
    )(at, q, k, v, *tiles, prev)


def head_merge_kernel(heads, me_ref, *refs):
    pieces = refs[:heads]
    gate_ref, x_ref, wm_ref, bm_ref, f1_ref, f2_ref = refs[heads:heads + 6]
    next_ref, left_refs, right_ref = refs[heads + 6], refs[heads + 7:heads + 9], refs[heads + 9]
    m_hi, m_lo, f_st = refs[heads + 10:]
    _, hw, span = pieces[0].shape
    hid = f1_ref.shape[1]
    rows = span // CORES

    @pl.when(pl.program_id(0) == 0)
    def _():
        for k in range(heads):
            hi, lo = split(wm_ref[pl.ds(pl.multiple_of((me_ref[0] ^ k) * hw, hw), hw), :])
            m_hi[k * hw:(k + 1) * hw, :] = hi
            m_lo[k * hw:(k + 1) * hw, :] = lo
        hi, lo = split(jnp.concatenate([f1_ref[...], f2_ref[...]], axis=1).T)
        f_st[0:2 * hid, :] = hi
        f_st[2 * hid:4 * hid, :] = lo

    a = jnp.concatenate([p[0] for p in pieces], axis=0)
    ah, al = split((a * gate_ref[0]).T)
    y = x_ref[0] + (mm(ah, m_hi[...]) + mm(al, m_hi[...]) + mm(ah, m_lo[...])) + bm_ref[...]
    next_ref[0] = y
    zh, zl = split(norm_rows(y))
    p = mm_nt(f_st[...], zh)
    p = p[:2 * hid] + p[2 * hid:] + mm_nt(f_st[0:2 * hid, :], zl)
    swap = me_ref[1] == 1
    left_refs[0][0] = jnp.where(swap, p[:hid, rows:], p[:hid, :rows])
    left_refs[1][0] = jnp.where(swap, p[:hid, :rows], p[:hid, rows:])
    right_ref[0] = p[hid:]


def head_merge(me, pieces, gate, x, wm, bm, f1, f2):
    seqs, span, ch = x.shape
    heads = len(pieces)
    hw = ch // heads
    hid = f1.shape[1]
    rows = span // CORES
    bm = bm.reshape(1, ch)
    return pl.pallas_call(
        functools.partial(head_merge_kernel, heads),
        out_shape=(jax.ShapeDtypeStruct(x.shape, F32),)
        + (jax.ShapeDtypeStruct((seqs, hid, rows), F32),) * CORES
        + (jax.ShapeDtypeStruct((seqs, hid, span), F32),),
        grid_spec=pltpu.PrefetchScalarGridSpec(
            num_scalar_prefetch=1,
            grid=(seqs,),
            in_specs=[pl.BlockSpec((1, hw, span), lambda s, _: (s, 0, 0)) for _ in pieces]
            + [
                pl.BlockSpec((1, ch, span), lambda s, _: (s, 0, 0)),
                pl.BlockSpec((1, span, ch), lambda s, _: (s, 0, 0)),
            ]
            + [whole(a) for a in (wm, bm, f1, f2)],
            out_specs=(pl.BlockSpec((1, span, ch), lambda s, _: (s, 0, 0)),)
            + (pl.BlockSpec((1, hid, rows), lambda s, _: (s, 0, 0)),) * CORES
            + (pl.BlockSpec((1, hid, span), lambda s, _: (s, 0, 0)),),
            scratch_shapes=[
                pltpu.VMEM((ch, ch), BF16),
                pltpu.VMEM((ch, ch), BF16),
                pltpu.VMEM((4 * hid, ch), BF16),
            ],
        ),
        compiler_params=PARAMS,
        name="head_merge",
    )(me, *pieces, gate, x, wm, bm, f1, f2)


def pack_kernel(slots_ref, *refs):
    left_refs, (own_ref, sib_ref, lr_ref, rc_ref, right) = refs[:-5], refs[-5:]
    cores, seqs, hid, rows = left_refs[0].shape
    slots = len(left_refs) * cores
    for i in range(own_ref.shape[0]):
        at = slots_ref[i] * cores
        for t, ref in enumerate((own_ref, sib_ref)):
            right[pl.ds((at + t) * seqs, seqs)] = ref[i]
    rt = jnp.concatenate([right[:, d, :] for d in range(hid)], axis=0)
    rc_ref[...] = rt.T
    for p, ref in enumerate(left_refs):
        for t in range(cores):
            for s in range(seqs):
                at = (p * cores + t) * seqs + s
                lr_ref[pl.ds(at, rows, stride=slots * seqs), :] = ref[t, s].T


def pack(slots, lefts, own, sib):
    cores, seqs, hid, rows = lefts[0].shape
    planes, _, _, cols = own.shape
    total = planes * cores * seqs
    return pl.pallas_call(
        pack_kernel,
        out_shape=(
            jax.ShapeDtypeStruct((rows * total, hid), F32),
            jax.ShapeDtypeStruct((cols, hid * total), F32),
        ),
        in_specs=[pl.BlockSpec(memory_space=pltpu.SMEM)]
        + [pl.BlockSpec(memory_space=pltpu.VMEM)] * (len(lefts) + 2),
        out_specs=(pl.BlockSpec(memory_space=pltpu.VMEM),) * 2,
        scratch_shapes=[pltpu.VMEM((total, hid, cols), F32)],
        compiler_params=PARAMS,
        name="pack",
    )(slots, *lefts, own, sib)


def after(x, *deps):
    return lax.optimization_barrier((x, deps))[0]


def per_head(
    parts,
    homolog_embedding,
    pair_state,
    probe_projector,
    lookup_projector,
    content_projector,
    sigmoid_projector,
    sigmoid_offset,
    pair_bias_weight,
    mixing_projector,
    mixing_offset,
    first_factor_projector,
    second_factor_projector,
    outer_product_weight,
    outer_product_bias,
    up_weight,
    expand_bias,
    down_weight,
):
    seqs, span, ch = homolog_embedding.shape
    _, _, cz = pair_state.shape
    heads = pair_bias_weight.shape[1]
    hw = ch // heads
    hid = first_factor_projector.shape[1]
    wide = lax.axis_index("wide")
    n = lax.axis_index("narrow")
    z, c = wide // CORES, wide % CORES
    me = n * CORES + c
    order = jnp.asarray(ORDER, jnp.int32)[z]

    group = 16
    lane = jnp.arange(heads * group, dtype=jnp.int32) // group
    own_first = jnp.take(pair_bias_weight, lane ^ me, axis=1)
    tiles = head_bias(pair_state, own_first, heads)
    *qkv, gate = head_project(
        me[None], after(homolog_embedding, tiles[0]), probe_projector, lookup_projector, content_projector,
        sigmoid_projector, sigmoid_offset, heads,
    )
    tiles = after(exchange(tiles, parts), gate)
    bias = jnp.stack(
        [jnp.stack([tiles[p * CORES + r] for p in range(parts)]) for r in range(CORES)]
    )
    near, second, third = line_gather(bias, parts)
    qkv = exchange(after(qkv, bias), parts)
    q, k, v = stage(n[None], after(qkv, near, second[0]), parts)
    att = jnp.zeros((parts, CORES, seqs, hw, span), F32)
    bias = after(bias, second[1], third[0])
    for i, tile in enumerate(((bias,), (near,), second, third)):
        at = jnp.stack([order[i], order[i] ^ n, c])
        att = head_attention(at, q, k, v, tile, att, hw)
    pieces = exchange([att[p, r] for p in range(parts) for r in range(CORES)], parts)
    alignment_state_next, left_a, left_b, right = head_merge(
        jnp.stack([me, c]), pieces, gate, homolog_embedding, mixing_projector, mixing_offset,
        first_factor_projector, second_factor_projector,
    )
    turn = lambda z0, c0, n0: (n0, c0, z0)
    left_b, left_a = send(left_b, parts, turn), send(left_a, parts, turn)
    sibling = lambda z0, c0, n0: (z0, c0 ^ 1, n0)
    left = jnp.stack([left_a, send(left_b, parts, sibling)])
    near, second, third = line_gather(right, parts)
    lefts = [left] + [send(left, parts, lambda z0, c0, n0, d=d: (z0, c0, n0 ^ d)) for d in range(1, parts)]
    own = jnp.stack([right, near, sum(second), sum(third)])
    left_rows, right_cols = pack(order ^ n, lefts, own, send(own, parts, sibling))
    pair_state_next = pair_update(
        left_rows, right_cols, outer_product_weight.reshape(hid, hid * cz), pair_state,
        outer_product_bias, up_weight, expand_bias, down_weight,
    )
    return (alignment_state_next, pair_state_next)


def lines(mesh):
    return mesh.shape["wide"] == PLANES * CORES and mesh.shape["narrow"] == PLANES


def step(mesh, *args):
    parts = mesh.shape["narrow"]
    heads = args[7].shape[1]
    if lines(mesh) and heads == CORES * parts:
        return per_head(parts, *args)
    return spread_heads(parts, *args)


def solution(mesh):
    placed = (P("wide", "narrow", None), P("wide", "narrow", None)) + (P(),) * 15
    return jax.shard_map(
        functools.partial(step, mesh),
        mesh=mesh,
        in_specs=placed,
        out_specs=(P("wide", "narrow", None), P("wide", "narrow", None)),
        check_vma=False,
    )
```

```python
import functools
import math

import jax
import jax.numpy as jnp
from jax import lax
from jax.experimental import pallas as pl
from jax.experimental.pallas import tpu as pltpu
from jax.sharding import PartitionSpec as P


F32, BF16 = jnp.float32, jnp.bfloat16
PARAMS = pltpu.CompilerParams(vmem_limit_bytes=60 * 2**20)


def split(x):
    hi = x.astype(BF16)
    lo = (x - hi.astype(F32)).astype(BF16)
    return hi, lo


def mm(a, b):
    return jnp.dot(a, b, preferred_element_type=F32)


def mm_nt(a, b):
    return lax.dot_general(a, b, (((1,), (1,)), ((), ())), preferred_element_type=F32)


def norm_rows(x):
    mean = jnp.mean(x, axis=-1, keepdims=True)
    c = x - mean
    var = jnp.mean(c * c, axis=-1, keepdims=True)
    return c * lax.rsqrt(var + 1e-05)


def whole(a):
    return pl.BlockSpec(a.shape, lambda *_: (0,) * a.ndim, pipeline_mode=pl.Buffered(1))


def bias_kernel(pair_ref, w_ref, out_ref):
    rows, _, _ = pair_ref.shape
    heads = w_ref.shape[1]
    wh, wl = split(w_ref[...].T)
    lhs = jnp.concatenate(
        [jnp.concatenate([wh, wh], axis=1), jnp.concatenate([wl, wl], axis=1)], axis=0
    )
    for i in range(rows):
        yh, yl = split(norm_rows(pair_ref[i]))
        r = mm_nt(lhs, jnp.concatenate([yh, yl], axis=1))
        out_ref[:, i, :] = r[:heads] + r[heads:]


def bias_tile(pair, w, step=8):
    rows, cols, cz = pair.shape
    heads = w.shape[1]
    return pl.pallas_call(
        bias_kernel,
        out_shape=jax.ShapeDtypeStruct((heads, rows, cols), F32),
        grid=(rows // step,),
        in_specs=[pl.BlockSpec((step, cols, cz), lambda i: (i, 0, 0)), whole(w)],
        out_specs=pl.BlockSpec((heads, step, cols), lambda i: (0, i, 0)),
        compiler_params=PARAMS,
        name="bias_tile",
    )(pair, w)


def project_kernel(parts, scale, x_ref, wq_ref, wk_ref, wv_ref, wg_ref, bg_ref, qkv_ref, gate_ref, w_hi, w_lo):
    ch = x_ref.shape[-1]
    own = ch // parts

    @pl.when(pl.program_id(0) == 0)
    def _():
        for t, (ref, f) in enumerate(((wq_ref, scale), (wk_ref, 1.0), (wv_ref, 1.0), (wg_ref, 1.0))):
            hi, lo = split(ref[...].T * f)
            w_hi[t * ch:(t + 1) * ch, :] = hi
            w_lo[t * ch:(t + 1) * ch, :] = lo

    yh, yl = split(norm_rows(x_ref[0]))
    r = mm_nt(w_hi[...], yh) + mm_nt(w_hi[...], yl) + mm_nt(w_lo[...], yh)
    for t in range(3):
        for n in range(parts):
            lo = t * ch + n * own
            qkv_ref[n, t, 0] = r[lo:lo + own]
    gate_ref[0] = jax.nn.sigmoid(r[3 * ch:] + bg_ref[...])


def project(x, wq, wk, wv, wg, bg, parts, head_width):
    seqs, span, ch = x.shape
    own = ch // parts
    bg = bg.reshape(ch, 1)
    return pl.pallas_call(
        functools.partial(project_kernel, parts, 1.0 / math.sqrt(head_width)),
        out_shape=(
            jax.ShapeDtypeStruct((parts, 3, seqs, own, span), F32),
            jax.ShapeDtypeStruct((seqs, ch, span), F32),
        ),
        grid=(seqs,),
        in_specs=[pl.BlockSpec((1, span, ch), lambda s: (s, 0, 0))] + [whole(a) for a in (wq, wk, wv, wg, bg)],
        out_specs=(
            pl.BlockSpec((parts, 3, 1, own, span), lambda s: (0, 0, s, 0, 0)),
            pl.BlockSpec((1, ch, span), lambda s: (s, 0, 0)),
        ),
        scratch_shapes=[pltpu.VMEM((4 * ch, ch), BF16), pltpu.VMEM((4 * ch, ch), BF16)],
        compiler_params=PARAMS,
        name="project",
    )(x, wq, wk, wv, wg, bg)


def attention_kernel(hw, q_ref, k_ref, v_ref, bias_ref, out_ref, ks, vs):
    parts = k_ref.shape[0]
    span = k_ref.shape[-1]
    s = pl.program_id(1)

    @pl.when(pl.program_id(0) == 0)
    def _():
        for n in range(parts):
            at = slice(n * span, (n + 1) * span)
            hi, lo = split(k_ref[n, 0, 0])
            ks[s, 0:hw, at] = hi
            ks[s, hw:2 * hw, at] = lo
            ks[s, 2 * hw:3 * hw, at] = hi
            v = v_ref[n, 0, 0]
            vh = v.astype(BF16).astype(F32)
            st = jnp.concatenate([vh, v - vh, jnp.ones((hw, span), F32), jnp.zeros((hw, span), F32)], axis=0)
            vs[s, at, :] = st.T.astype(BF16)

    q = q_ref[0, 0, 0]
    qh = q.astype(BF16).astype(F32)
    qst = jnp.concatenate([qh, qh, q - qh, jnp.zeros_like(q)], axis=0).T[:, :3 * hw].astype(BF16)
    bias = jnp.concatenate(
        [
            jnp.concatenate([bias_ref[w, n] for n in range(parts)], axis=1)
            for w in range(bias_ref.shape[0])
        ],
        axis=0,
    )
    scores = mm(qst, ks[s]) + bias
    top = jnp.max(scores, axis=1, keepdims=True)
    ph, plo = split(jnp.exp(scores - top))
    t = (mm(ph, vs[s]) + mm(plo, vs[s])).T
    out_ref[0, 0] = (t[0:hw] + t[hw:2 * hw]) / t[2 * hw:2 * hw + 1]


def attention(qkv, bias, head, hw):
    parts, _, seqs, _, span = qkv.shape
    _, _, rows, _ = bias.shape
    per = span // rows
    return pl.pallas_call(
        functools.partial(attention_kernel, hw),
        out_shape=jax.ShapeDtypeStruct((parts, seqs, hw, span), F32),
        grid=(parts, seqs),
        in_specs=[
            pl.BlockSpec((1, 1, 1, hw, span), lambda b, s: (b, 0, s, head, 0)),
            pl.BlockSpec((parts, 1, 1, hw, span), lambda b, s: (0, 1, s, head, 0)),
            pl.BlockSpec((parts, 1, 1, hw, span), lambda b, s: (0, 2, s, head, 0)),
            pl.BlockSpec((per, parts, rows, span), lambda b, s: (b, 0, 0, 0)),
        ],
        out_specs=pl.BlockSpec((1, 1, hw, span), lambda b, s: (b, s, 0, 0)),
        scratch_shapes=[
            pltpu.VMEM((seqs, 3 * hw, parts * span), BF16),
            pltpu.VMEM((seqs, parts * span, 4 * hw), BF16),
        ],
        compiler_params=PARAMS,
        name="attention",
    )(qkv, qkv, qkv, bias)


def merge_kernel(*refs):
    heads = len(refs) - 12
    att = refs[:heads]
    gate_ref, x_ref, wm_ref, bm_ref, f1_ref, f2_ref, next_ref, left_ref, right_ref, m_hi, m_lo, f_st = refs[heads:]
    parts, _, _, _ = att[0].shape
    hid = f1_ref.shape[1]
    blocks, _, _, rows = left_ref.shape

    @pl.when(pl.program_id(0) == 0)
    def _():
        hi, lo = split(wm_ref[...])
        m_hi[...] = hi
        m_lo[...] = lo
        hi, lo = split(jnp.concatenate([f1_ref[...], f2_ref[...]], axis=1).T)
        f_st[0:2 * hid, :] = hi
        f_st[2 * hid:4 * hid, :] = lo

    a = jnp.concatenate([att[h][n, 0] for n in range(parts) for h in range(heads)], axis=0)
    ah, al = split((a * gate_ref[0]).T)
    y = x_ref[0] + (mm(ah, m_hi[...]) + mm(al, m_hi[...]) + mm(ah, m_lo[...])) + bm_ref[...]
    next_ref[0] = y
    zh, zl = split(norm_rows(y))
    p = mm_nt(f_st[...], zh)
    p = p[:2 * hid] + p[2 * hid:] + mm_nt(f_st[0:2 * hid, :], zl)
    for b in range(blocks):
        left_ref[b, 0] = p[:hid, b * rows:(b + 1) * rows]
    right_ref[0] = p[hid:]


def merge(att, gate, x, wm, bm, f1, f2, rows):
    seqs, span, ch = x.shape
    parts, _, hw, _ = att[0].shape
    hid = f1.shape[1]
    bm = bm.reshape(1, ch)
    blocks = span // rows
    return pl.pallas_call(
        merge_kernel,
        out_shape=(
            jax.ShapeDtypeStruct(x.shape, F32),
            jax.ShapeDtypeStruct((blocks, seqs, hid, rows), F32),
            jax.ShapeDtypeStruct((seqs, hid, span), F32),
        ),
        grid=(seqs,),
        in_specs=[pl.BlockSpec((parts, 1, hw, span), lambda s: (0, s, 0, 0)) for _ in att]
        + [
            pl.BlockSpec((1, ch, span), lambda s: (s, 0, 0)),
            pl.BlockSpec((1, span, ch), lambda s: (s, 0, 0)),
        ]
        + [whole(a) for a in (wm, bm, f1, f2)],
        out_specs=(
            pl.BlockSpec((1, span, ch), lambda s: (s, 0, 0)),
            pl.BlockSpec((blocks, 1, hid, rows), lambda s: (0, s, 0, 0)),
            pl.BlockSpec((1, hid, span), lambda s: (s, 0, 0)),
        ),
        scratch_shapes=[
            pltpu.VMEM((ch, ch), BF16),
            pltpu.VMEM((ch, ch), BF16),
            pltpu.VMEM((4 * hid, ch), BF16),
        ],
        compiler_params=PARAMS,
        name="merge",
    )(*att, gate, x, wm, bm, f1, f2)


def pair_kernel(
    step_rows, group, seqs, left_ref, right_ref, w_ref, pair_ref, ob_ref, up_ref, eb_ref, dn_ref,
    out_ref, r_hi, r_lo, w_st, up_st, dn_st,
):
    _, cols, cz = pair_ref.shape
    c_n = w_ref.shape[0]
    d_n = w_ref.shape[1] // cz

    @pl.when(pl.program_id(0) == 0)
    def _():
        hi, lo = split(right_ref[...])
        r_hi[...] = hi
        r_lo[...] = lo
        hi, lo = split(w_ref[...])
        w_st[0:c_n, :] = hi
        w_st[c_n:2 * c_n, :] = lo
        w_st[2 * c_n:3 * c_n, :] = hi
        hi, lo = split(up_ref[...])
        up_st[0:cz, :] = hi
        up_st[cz:2 * cz, :] = hi
        up_st[2 * cz:3 * cz, :] = lo
        hi, lo = split(dn_ref[...])
        dn_st[:, 0:cz] = hi
        dn_st[:, cz:2 * cz] = lo

    def body(p, carry):
        lrow = left_ref[pl.ds(pl.multiple_of(p * group * seqs, group * seqs), group * seqs), :]
        lhi = lrow.astype(BF16).astype(F32)
        u = mm(jnp.concatenate([lhi, lhi, lrow - lhi], axis=1).astype(BF16), w_st[...])
        his, los = [], []
        for q in range(group):
            sub = u[q * seqs:(q + 1) * seqs, :]
            hi, lo = split(jnp.concatenate([sub[:, d * cz:(d + 1) * cz] for d in range(d_n)], axis=0))
            his.append(hi)
            los.append(lo)
        mids = []
        for q in range(0, group, 2):
            cross = mm(r_lo[...], jnp.concatenate(his[q:q + 2], axis=1))
            for i in range(2):
                a = mm(r_hi[...], jnp.concatenate([his[q + i], los[q + i]], axis=1))
                o = a[:, :cz] + a[:, cz:] + cross[:, i * cz:(i + 1) * cz]
                mids.append(pair_ref[group * p + q + i] + o / seqs + ob_ref[...])
        for q in range(0, group, 2):
            mid = jnp.concatenate(mids[q:q + 2], axis=0)
            yh, yl = split(norm_rows(mid))
            h = mm(jnp.concatenate([yh, yl, yh], axis=1), up_st[...])
            hh, hl = split(jnp.maximum(h + eb_ref[...], 0.0))
            a = mm(hh, dn_st[...])
            o = mid + (a[:, :cz] + a[:, cz:] + mm(hl, dn_st[:, 0:cz]))
            for i in range(2):
                out_ref[group * p + q + i] = o[i * cols:(i + 1) * cols]
        return carry

    lax.fori_loop(0, step_rows // group, body, 0)


def pair_update(left_rows, right_cols, w2, pair, ob, up, eb, dn, step_rows=8, group=4):
    rows, cols, cz = pair.shape
    seqs = left_rows.shape[0] // rows
    c_n = w2.shape[0]
    ob = ob.reshape(1, -1)
    eb = eb.reshape(1, -1)
    return pl.pallas_call(
        functools.partial(pair_kernel, step_rows, group, seqs),
        out_shape=jax.ShapeDtypeStruct(pair.shape, F32),
        grid=(rows // step_rows,),
        in_specs=[
            pl.BlockSpec((step_rows * seqs, left_rows.shape[1]), lambda i: (i, 0)),
            whole(right_cols), whole(w2),
            pl.BlockSpec((step_rows, cols, cz), lambda i: (i, 0, 0)),
            whole(ob), whole(up), whole(eb), whole(dn),
        ],
        out_specs=pl.BlockSpec((step_rows, cols, cz), lambda i: (i, 0, 0)),
        scratch_shapes=[
            pltpu.VMEM(right_cols.shape, BF16),
            pltpu.VMEM(right_cols.shape, BF16),
            pltpu.VMEM((3 * c_n, w2.shape[1]), BF16),
            pltpu.VMEM((3 * cz, up.shape[1]), BF16),
            pltpu.VMEM((up.shape[1], 2 * cz), BF16),
        ],
        compiler_params=PARAMS,
        name="pair_update",
    )(left_rows, right_cols, w2, pair, ob, up, eb, dn)


def spread_heads(
    parts,
    homolog_embedding,
    pair_state,
    probe_projector,
    lookup_projector,
    content_projector,
    sigmoid_projector,
    sigmoid_offset,
    pair_bias_weight,
    mixing_projector,
    mixing_offset,
    first_factor_projector,
    second_factor_projector,
    outer_product_weight,
    outer_product_bias,
    up_weight,
    expand_bias,
    down_weight,
):
    _, _, ch = homolog_embedding.shape
    rows, cols, cz = pair_state.shape
    heads = pair_bias_weight.shape[1]
    hw = ch // heads
    own_heads = heads // parts
    hid = first_factor_projector.shape[1]

    bias = bias_tile(pair_state, pair_bias_weight).reshape(parts, own_heads, rows, cols)
    bias = lax.all_to_all(bias, "narrow", 0, 0, tiled=True)
    gathered = [
        lax.all_gather(bias[:, h], "wide", axis=0, tiled=False) for h in range(own_heads)
    ]
    qkv, gate = project(
        homolog_embedding, probe_projector, lookup_projector, content_projector, sigmoid_projector,
        sigmoid_offset, parts, hw,
    )
    qkv = lax.all_to_all(qkv, "narrow", 0, 0, tiled=True)
    att = [
        lax.all_to_all(attention(qkv, gathered[h], h, hw), "narrow", 0, 0, tiled=True)
        for h in range(own_heads)
    ]
    alignment_state_next, left, right = merge(
        att, gate, homolog_embedding, mixing_projector, mixing_offset,
        first_factor_projector, second_factor_projector, rows,
    )
    left = lax.all_gather(left, "narrow", axis=0, tiled=True)
    left = lax.all_to_all(left, "wide", 0, 0, tiled=True)
    right = lax.all_gather(right, "wide", axis=0, tiled=True)
    left = left.reshape(-1, hid, rows)
    all_seqs = left.shape[0]
    left_rows = jnp.transpose(left, (2, 0, 1)).reshape(rows * all_seqs, hid)
    right_cols = jnp.transpose(right, (2, 1, 0)).reshape(cols, hid * all_seqs)
    pair_state_next = pair_update(
        left_rows, right_cols, outer_product_weight.reshape(hid, hid * cz), pair_state,
        outer_product_bias, up_weight, expand_bias, down_weight,
    )
    return (alignment_state_next, pair_state_next)


AXES = ("wide", "narrow")
PLANES, CORES = 4, 2
PARTNER = {1: 2, 2: 1}
OUTWARD = {1: 0, 2: 3}
ORDER = ((0, 1, 2, 3), (1, 0, 2, 3), (2, 3, 1, 0), (3, 2, 1, 0))


def send(x, parts, route):
    pairs = []
    for z in range(PLANES):
        for c in range(CORES):
            for n in range(parts):
                to = route(z, c, n)
                if to is not None:
                    pairs.append(((z * CORES + c) * parts + n, (to[0] * CORES + to[1]) * parts + to[2]))
    return lax.ppermute(x, AXES, pairs)


def exchange(blocks, parts):
    out = [blocks[0]]
    for k in range(1, len(blocks)):
        dn, dc = divmod(k, CORES)
        out.append(send(blocks[k], parts, lambda z, c, n: (z, c ^ dc, n ^ dn)))
    return out


def line_gather(x, parts):
    middle = lambda table: lambda z, c, n: (table[z], c, n) if z in table else None
    near = send(x, parts, lambda z, c, n: (z ^ 1, c, n))
    across = send(x, parts, middle(PARTNER))
    out2 = send(across, parts, middle(OUTWARD))
    far = send(near, parts, middle(PARTNER))
    out3 = send(far, parts, middle(OUTWARD))
    return near, (across, out2), (far, out3)


def head_bias_kernel(group, pair_ref, w_ref, *out_refs):
    rows, cols, cz = pair_ref.shape
    heads = w_ref.shape[1]
    wh, wl = split(w_ref[...].T)
    lhs = jnp.concatenate(
        [jnp.concatenate([wh, wh], axis=1), jnp.concatenate([wl, wl], axis=1)], axis=0
    )
    for i in range(0, rows, group):
        yh, yl = split(norm_rows(pair_ref[i:i + group].reshape(group * cols, cz)))
        r = mm_nt(lhs, jnp.concatenate([yh, yl], axis=1))
        r = r[:heads] + r[heads:]
        for g in range(group):
            for k in range(heads):
                out_refs[k][i + g:i + g + 1, :] = r[k:k + 1, g * cols:(g + 1) * cols]


def head_bias(pair, w, step=32, group=4):
    rows, cols, cz = pair.shape
    heads = w.shape[1]
    return pl.pallas_call(
        functools.partial(head_bias_kernel, group),
        out_shape=(jax.ShapeDtypeStruct((rows, cols), F32),) * heads,
        grid=(rows // step,),
        in_specs=[pl.BlockSpec((step, cols, cz), lambda i: (i, 0, 0)), whole(w)],
        out_specs=(pl.BlockSpec((step, cols), lambda i: (i, 0)),) * heads,
        compiler_params=PARAMS,
        name="head_bias",
    )(pair, w)


def head_project_kernel(heads, scale, me_ref, x_ref, wq_ref, wk_ref, wv_ref, wg_ref, bg_ref, *refs):
    qkv_refs, (gate_ref, w_t, b_p, w_hi, w_lo) = refs[:heads], refs[heads:]
    ch = x_ref.shape[-1]
    hw = ch // heads

    @pl.when(pl.program_id(0) == 0)
    def _():
        me = me_ref[0]
        for t, (ref, f) in enumerate(((wq_ref, scale), (wk_ref, 1.0), (wv_ref, 1.0), (wg_ref, 1.0))):
            w_t[...] = ref[...].T * f
            for k in range(heads):
                src = pl.ds(pl.multiple_of((me ^ k) * hw, hw), hw)
                hi, lo = split(w_t[src, :])
                at = slice(t * ch + k * hw, t * ch + (k + 1) * hw)
                w_hi[at, :] = hi
                w_lo[at, :] = lo
                if t == 3:
                    b_p[k * hw:(k + 1) * hw, :] = bg_ref[src, :]

    yh, yl = split(norm_rows(x_ref[0]))
    r = mm_nt(w_hi[...], yh) + mm_nt(w_hi[...], yl) + mm_nt(w_lo[...], yh)
    for t in range(3):
        for k in range(heads):
            lo = t * ch + k * hw
            qkv_refs[k][t, 0] = r[lo:lo + hw]
    gate_ref[0] = jax.nn.sigmoid(r[3 * ch:] + b_p[...])


def head_project(me, x, wq, wk, wv, wg, bg, heads):
    seqs, span, ch = x.shape
    hw = ch // heads
    bg = bg.reshape(ch, 1)
    return pl.pallas_call(
        functools.partial(head_project_kernel, heads, 1.0 / math.sqrt(hw)),
        out_shape=(jax.ShapeDtypeStruct((3, seqs, hw, span), F32),) * heads
        + (jax.ShapeDtypeStruct((seqs, ch, span), F32),),
        grid_spec=pltpu.PrefetchScalarGridSpec(
            num_scalar_prefetch=1,
            grid=(seqs,),
            in_specs=[pl.BlockSpec((1, span, ch), lambda s, _: (s, 0, 0))]
            + [whole(a) for a in (wq, wk, wv, wg, bg)],
            out_specs=(pl.BlockSpec((3, 1, hw, span), lambda s, _: (0, s, 0, 0)),) * heads
            + (pl.BlockSpec((1, ch, span), lambda s, _: (s, 0, 0)),),
            scratch_shapes=[
                pltpu.VMEM((ch, ch), F32),
                pltpu.VMEM((ch, 1), F32),
                pltpu.VMEM((4 * ch, ch), BF16),
                pltpu.VMEM((4 * ch, ch), BF16),
            ],
        ),
        compiler_params=PARAMS,
        name="head_project",
    )(me, x, wq, wk, wv, wg, bg)


def stage_kernel(n_ref, *refs):
    pieces, (q_ref, k_ref, v_ref) = refs[:-3], refs[-3:]
    _, _, hw, span = pieces[0].shape
    for p, ref in enumerate(pieces):
        part, core = divmod(p, CORES)
        at = slice(part * span, (part + 1) * span)
        q = ref[0, 0]
        qh = q.astype(BF16).astype(F32)
        q_ref[core, 0, (n_ref[0] - 1) ^ part] = (
            jnp.concatenate([qh, qh, q - qh, jnp.zeros_like(q)], axis=0).T.astype(BF16)
        )
        hi, lo = split(ref[1, 0])
        k_ref[core, 0, 0:hw, at] = hi
        k_ref[core, 0, hw:2 * hw, at] = lo
        k_ref[core, 0, 2 * hw:3 * hw, at] = hi
        k_ref[core, 0, 3 * hw:4 * hw, at] = jnp.zeros_like(hi)
        v = ref[2, 0]
        vh = v.astype(BF16).astype(F32)
        st = jnp.concatenate([vh, v - vh, jnp.ones((hw, span), F32), jnp.zeros((hw, span), F32)], axis=0)
        v_ref[core, 0, at, :] = st.T.astype(BF16)


def stage(n, pieces, parts):
    _, seqs, hw, span = pieces[0].shape
    return pl.pallas_call(
        stage_kernel,
        out_shape=(
            jax.ShapeDtypeStruct((CORES, seqs, parts, span, 4 * hw), BF16),
            jax.ShapeDtypeStruct((CORES, seqs, 4 * hw, parts * span), BF16),
            jax.ShapeDtypeStruct((CORES, seqs, parts * span, 4 * hw), BF16),
        ),
        grid_spec=pltpu.PrefetchScalarGridSpec(
            num_scalar_prefetch=1,
            grid=(seqs,),
            in_specs=[pl.BlockSpec((3, 1, hw, span), lambda s, _: (0, s, 0, 0)) for _ in pieces],
            out_specs=(
                pl.BlockSpec((CORES, 1, parts, span, 4 * hw), lambda s, _: (0, s, 0, 0, 0)),
                pl.BlockSpec((CORES, 1, 4 * hw, parts * span), lambda s, _: (0, s, 0, 0)),
                pl.BlockSpec((CORES, 1, parts * span, 4 * hw), lambda s, _: (0, s, 0, 0)),
            ),
        ),
        compiler_params=PARAMS,
        name="stage",
    )(n, *pieces)


def head_attention_kernel(hw, turn, tiles, at_ref, q_ref, k_ref, v_ref, *refs):
    bias_refs, out_ref = refs[:tiles], refs[-1]
    parts = bias_refs[0].shape[1]
    cores, seqs = q_ref.shape[:2]
    core = at_ref[3 * turn + 2]
    bias = jnp.concatenate(
        [
            jnp.concatenate([sum(b[h ^ core, n] for b in bias_refs) for n in range(parts)], axis=1)
            for h in range(CORES)
        ],
        axis=0,
    )
    for g in range(cores):
        for s in range(seqs):
            scores = mm(q_ref[g, s, 0], k_ref[g, s]) + bias
            top = jnp.max(scores, axis=1, keepdims=True)
            ph, plo = split(jnp.exp(scores - top))
            t = (mm(ph, v_ref[g, s]) + mm(plo, v_ref[g, s])).T
            out_ref[0, g, s] = (t[0:hw] + t[hw:2 * hw]) / t[2 * hw:2 * hw + 1]


def head_attention(at, turn, q, k, v, tiles, prev, hw, step=2):
    cores, seqs, parts, span, _ = q.shape
    before = () if prev is None else (prev,)
    return pl.pallas_call(
        functools.partial(head_attention_kernel, hw, turn, len(tiles)),
        out_shape=jax.ShapeDtypeStruct((parts, cores, seqs, hw, span), F32),
        grid_spec=pltpu.PrefetchScalarGridSpec(
            num_scalar_prefetch=1,
            grid=(seqs // step,),
            in_specs=[
                pl.BlockSpec((cores, step, 1, span, 4 * hw), lambda s, at: (0, s, at[3 * turn], 0, 0)),
                pl.BlockSpec((cores, step, 4 * hw, parts * span), lambda s, at: (0, s, 0, 0)),
                pl.BlockSpec((cores, step, parts * span, 4 * hw), lambda s, at: (0, s, 0, 0)),
            ]
            + [whole(b) for b in tiles]
            + [pl.BlockSpec(memory_space=pl.ANY) for _ in before],
            out_specs=pl.BlockSpec((1, cores, step, hw, span), lambda s, at: (at[3 * turn + 1], 0, s, 0, 0)),
        ),
        input_output_aliases={4 + len(tiles): 0} if before else {},
        compiler_params=PARAMS,
        name="head_attention",
    )(at, q, k, v, *tiles, *before)


def head_merge_kernel(heads, me_ref, *refs):
    pieces = refs[:heads]
    gate_ref, x_ref, wm_ref, bm_ref, f1_ref, f2_ref = refs[heads:heads + 6]
    next_ref, left_refs, right_ref = refs[heads + 6], refs[heads + 7:heads + 9], refs[heads + 9]
    m_hi, m_lo, f_st = refs[heads + 10:]
    _, hw, span = pieces[0].shape
    hid = f1_ref.shape[1]
    rows = span // CORES

    @pl.when(pl.program_id(0) == 0)
    def _():
        for k in range(heads):
            hi, lo = split(wm_ref[pl.ds(pl.multiple_of((me_ref[0] ^ k) * hw, hw), hw), :])
            m_hi[k * hw:(k + 1) * hw, :] = hi
            m_lo[k * hw:(k + 1) * hw, :] = lo
        hi, lo = split(jnp.concatenate([f1_ref[...], f2_ref[...]], axis=1).T)
        f_st[0:2 * hid, :] = hi
        f_st[2 * hid:4 * hid, :] = lo

    a = jnp.concatenate([p[0] for p in pieces], axis=0)
    ah, al = split((a * gate_ref[0]).T)
    y = x_ref[0] + (mm(ah, m_hi[...]) + mm(al, m_hi[...]) + mm(ah, m_lo[...])) + bm_ref[...]
    next_ref[0] = y
    zh, zl = split(norm_rows(y))
    p = mm_nt(f_st[...], zh)
    p = p[:2 * hid] + p[2 * hid:] + mm_nt(f_st[0:2 * hid, :], zl)
    swap = me_ref[1] == 1
    left_refs[0][0] = jnp.where(swap, p[:hid, rows:], p[:hid, :rows])
    left_refs[1][0] = jnp.where(swap, p[:hid, :rows], p[:hid, rows:])
    right_ref[0] = p[hid:]


def head_merge(me, pieces, gate, x, wm, bm, f1, f2):
    seqs, span, ch = x.shape
    heads = len(pieces)
    hw = ch // heads
    hid = f1.shape[1]
    rows = span // CORES
    bm = bm.reshape(1, ch)
    return pl.pallas_call(
        functools.partial(head_merge_kernel, heads),
        out_shape=(jax.ShapeDtypeStruct(x.shape, F32),)
        + (jax.ShapeDtypeStruct((seqs, hid, rows), F32),) * CORES
        + (jax.ShapeDtypeStruct((seqs, hid, span), F32),),
        grid_spec=pltpu.PrefetchScalarGridSpec(
            num_scalar_prefetch=1,
            grid=(seqs,),
            in_specs=[pl.BlockSpec((1, hw, span), lambda s, _: (s, 0, 0)) for _ in pieces]
            + [
                pl.BlockSpec((1, ch, span), lambda s, _: (s, 0, 0)),
                pl.BlockSpec((1, span, ch), lambda s, _: (s, 0, 0)),
            ]
            + [whole(a) for a in (wm, bm, f1, f2)],
            out_specs=(pl.BlockSpec((1, span, ch), lambda s, _: (s, 0, 0)),)
            + (pl.BlockSpec((1, hid, rows), lambda s, _: (s, 0, 0)),) * CORES
            + (pl.BlockSpec((1, hid, span), lambda s, _: (s, 0, 0)),),
            scratch_shapes=[
                pltpu.VMEM((ch, ch), BF16),
                pltpu.VMEM((ch, ch), BF16),
                pltpu.VMEM((4 * hid, ch), BF16),
            ],
        ),
        compiler_params=PARAMS,
        name="head_merge",
    )(me, *pieces, gate, x, wm, bm, f1, f2)


def pack_kernel(slots_ref, *refs):
    left_refs, (own_ref, sib_ref, lr_ref, rc_ref, right) = refs[:-5], refs[-5:]
    cores, seqs, hid, rows = left_refs[0].shape
    slots = len(left_refs) * cores
    for i in range(own_ref.shape[0]):
        at = slots_ref[i] * cores
        for t, ref in enumerate((own_ref, sib_ref)):
            right[pl.ds((at + t) * seqs, seqs)] = ref[i]
    rt = jnp.concatenate([right[:, d, :] for d in range(hid)], axis=0)
    rc_ref[...] = rt.T
    for p, ref in enumerate(left_refs):
        for t in range(cores):
            for s in range(seqs):
                at = (p * cores + t) * seqs + s
                lr_ref[pl.ds(at, rows, stride=slots * seqs), :] = ref[t, s].T


def pack(slots, lefts, own, sib):
    cores, seqs, hid, rows = lefts[0].shape
    planes, _, _, cols = own.shape
    total = planes * cores * seqs
    return pl.pallas_call(
        pack_kernel,
        out_shape=(
            jax.ShapeDtypeStruct((rows * total, hid), F32),
            jax.ShapeDtypeStruct((cols, hid * total), F32),
        ),
        in_specs=[pl.BlockSpec(memory_space=pltpu.SMEM)]
        + [pl.BlockSpec(memory_space=pltpu.VMEM)] * (len(lefts) + 2),
        out_specs=(pl.BlockSpec(memory_space=pltpu.VMEM),) * 2,
        scratch_shapes=[pltpu.VMEM((total, hid, cols), F32)],
        compiler_params=PARAMS,
        name="pack",
    )(slots, *lefts, own, sib)


def after(x, *deps):
    return lax.optimization_barrier((x, deps))[0]


def per_head(
    parts,
    homolog_embedding,
    pair_state,
    probe_projector,
    lookup_projector,
    content_projector,
    sigmoid_projector,
    sigmoid_offset,
    pair_bias_weight,
    mixing_projector,
    mixing_offset,
    first_factor_projector,
    second_factor_projector,
    outer_product_weight,
    outer_product_bias,
    up_weight,
    expand_bias,
    down_weight,
):
    _, _, ch = homolog_embedding.shape
    _, _, cz = pair_state.shape
    heads = pair_bias_weight.shape[1]
    hw = ch // heads
    hid = first_factor_projector.shape[1]
    wide = lax.axis_index("wide")
    n = lax.axis_index("narrow")
    z, c = wide // CORES, wide % CORES
    me = n * CORES + c
    order = jnp.asarray(ORDER, jnp.int32)[z]

    own_first = jnp.take(pair_bias_weight, jnp.arange(heads, dtype=jnp.int32) ^ me, axis=1)
    at = jnp.stack([order, order ^ n, jnp.full_like(order, c)], axis=1).reshape(-1)
    own_first, at = after(own_first, at), after(at, own_first)
    tiles = head_bias(pair_state, own_first)
    *qkv, gate = head_project(
        me[None], after(homolog_embedding, tiles[0], at), probe_projector, lookup_projector, content_projector,
        sigmoid_projector, sigmoid_offset, heads,
    )
    tiles = after(exchange(tiles, parts), gate)
    bias = jnp.stack(
        [jnp.stack([tiles[p * CORES + r] for p in range(parts)]) for r in range(CORES)]
    )
    near, second, third = line_gather(bias, parts)
    qkv = exchange(after(qkv, bias), parts)
    marked = after(n[None], near, second[0]) + 1
    q, k, v = stage(marked, after(qkv, near, second[0]), parts)
    bias = after(bias, second[1], third[0])
    att = None
    for i, tile in enumerate(((bias,), (near,), second, third)):
        att = head_attention(at, i, q, k, v, tile, att, hw)
    pieces = exchange([att[p, r] for p in range(parts) for r in range(CORES)], parts)
    alignment_state_next, left_a, left_b, right = head_merge(
        jnp.stack([me, c]), pieces, gate, homolog_embedding, mixing_projector, mixing_offset,
        first_factor_projector, second_factor_projector,
    )
    turn = lambda z0, c0, n0: (n0, c0, z0)
    left_b, left_a = send(left_b, parts, turn), send(left_a, parts, turn)
    sibling = lambda z0, c0, n0: (z0, c0 ^ 1, n0)
    left = jnp.stack([left_a, send(left_b, parts, sibling)])
    near, second, third = line_gather(right, parts)
    lefts = [left] + [send(left, parts, lambda z0, c0, n0, d=d: (z0, c0, n0 ^ d)) for d in range(1, parts)]
    own = jnp.stack([right, near, sum(second), sum(third)])
    left_rows, right_cols = pack(order ^ n, lefts, own, send(own, parts, sibling))
    pair_state_next = pair_update(
        left_rows, right_cols, outer_product_weight.reshape(hid, hid * cz), pair_state,
        outer_product_bias, up_weight, expand_bias, down_weight,
    )
    return (alignment_state_next, pair_state_next)


def lines(mesh):
    return mesh.shape["wide"] == PLANES * CORES and mesh.shape["narrow"] == PLANES


def step(mesh, *args):
    parts = mesh.shape["narrow"]
    heads = args[7].shape[1]
    if lines(mesh) and heads == CORES * parts:
        return per_head(parts, *args)
    return spread_heads(parts, *args)


def solution(mesh):
    placed = (P("wide", "narrow", None), P("wide", "narrow", None)) + (P(),) * 15
    return jax.shard_map(
        functools.partial(step, mesh),
        mesh=mesh,
        in_specs=placed,
        out_specs=(P("wide", "narrow", None), P("wide", "narrow", None)),
        check_vma=False,
    )
```

```python
import functools
import math

import jax
import jax.numpy as jnp
from jax import lax
from jax.experimental import pallas as pl
from jax.experimental.pallas import tpu as pltpu
from jax.sharding import PartitionSpec as P


F32, BF16 = jnp.float32, jnp.bfloat16
PARAMS = pltpu.CompilerParams(vmem_limit_bytes=60 * 2**20)


def split(x):
    hi = x.astype(BF16)
    lo = (x - hi.astype(F32)).astype(BF16)
    return hi, lo


def mm(a, b):
    return jnp.dot(a, b, preferred_element_type=F32)


def mm_nt(a, b):
    return lax.dot_general(a, b, (((1,), (1,)), ((), ())), preferred_element_type=F32)


def norm_rows(x):
    mean = jnp.mean(x, axis=-1, keepdims=True)
    c = x - mean
    var = jnp.mean(c * c, axis=-1, keepdims=True)
    return c * lax.rsqrt(var + 1e-05)


def whole(a):
    return pl.BlockSpec(a.shape, lambda *_: (0,) * a.ndim, pipeline_mode=pl.Buffered(1))


def bias_kernel(pair_ref, w_ref, out_ref):
    rows, _, _ = pair_ref.shape
    heads = w_ref.shape[1]
    wh, wl = split(w_ref[...].T)
    lhs = jnp.concatenate(
        [jnp.concatenate([wh, wh], axis=1), jnp.concatenate([wl, wl], axis=1)], axis=0
    )
    for i in range(rows):
        yh, yl = split(norm_rows(pair_ref[i]))
        r = mm_nt(lhs, jnp.concatenate([yh, yl], axis=1))
        out_ref[:, i, :] = r[:heads] + r[heads:]


def bias_tile(pair, w, step=8):
    rows, cols, cz = pair.shape
    heads = w.shape[1]
    return pl.pallas_call(
        bias_kernel,
        out_shape=jax.ShapeDtypeStruct((heads, rows, cols), F32),
        grid=(rows // step,),
        in_specs=[pl.BlockSpec((step, cols, cz), lambda i: (i, 0, 0)), whole(w)],
        out_specs=pl.BlockSpec((heads, step, cols), lambda i: (0, i, 0)),
        compiler_params=PARAMS,
        name="bias_tile",
    )(pair, w)


def project_kernel(parts, scale, x_ref, wq_ref, wk_ref, wv_ref, wg_ref, bg_ref, qkv_ref, gate_ref, w_hi, w_lo):
    ch = x_ref.shape[-1]
    own = ch // parts

    @pl.when(pl.program_id(0) == 0)
    def _():
        for t, (ref, f) in enumerate(((wq_ref, scale), (wk_ref, 1.0), (wv_ref, 1.0), (wg_ref, 1.0))):
            hi, lo = split(ref[...].T * f)
            w_hi[t * ch:(t + 1) * ch, :] = hi
            w_lo[t * ch:(t + 1) * ch, :] = lo

    yh, yl = split(norm_rows(x_ref[0]))
    r = mm_nt(w_hi[...], yh) + mm_nt(w_hi[...], yl) + mm_nt(w_lo[...], yh)
    for t in range(3):
        for n in range(parts):
            lo = t * ch + n * own
            qkv_ref[n, t, 0] = r[lo:lo + own]
    gate_ref[0] = jax.nn.sigmoid(r[3 * ch:] + bg_ref[...])


def project(x, wq, wk, wv, wg, bg, parts, head_width):
    seqs, span, ch = x.shape
    own = ch // parts
    bg = bg.reshape(ch, 1)
    return pl.pallas_call(
        functools.partial(project_kernel, parts, 1.0 / math.sqrt(head_width)),
        out_shape=(
            jax.ShapeDtypeStruct((parts, 3, seqs, own, span), F32),
            jax.ShapeDtypeStruct((seqs, ch, span), F32),
        ),
        grid=(seqs,),
        in_specs=[pl.BlockSpec((1, span, ch), lambda s: (s, 0, 0))] + [whole(a) for a in (wq, wk, wv, wg, bg)],
        out_specs=(
            pl.BlockSpec((parts, 3, 1, own, span), lambda s: (0, 0, s, 0, 0)),
            pl.BlockSpec((1, ch, span), lambda s: (s, 0, 0)),
        ),
        scratch_shapes=[pltpu.VMEM((4 * ch, ch), BF16), pltpu.VMEM((4 * ch, ch), BF16)],
        compiler_params=PARAMS,
        name="project",
    )(x, wq, wk, wv, wg, bg)


def attention_kernel(hw, q_ref, k_ref, v_ref, bias_ref, out_ref, ks, vs):
    parts = k_ref.shape[0]
    span = k_ref.shape[-1]
    s = pl.program_id(1)

    @pl.when(pl.program_id(0) == 0)
    def _():
        for n in range(parts):
            at = slice(n * span, (n + 1) * span)
            hi, lo = split(k_ref[n, 0, 0])
            ks[s, 0:hw, at] = hi
            ks[s, hw:2 * hw, at] = lo
            ks[s, 2 * hw:3 * hw, at] = hi
            v = v_ref[n, 0, 0]
            vh = v.astype(BF16).astype(F32)
            st = jnp.concatenate([vh, v - vh, jnp.ones((hw, span), F32), jnp.zeros((hw, span), F32)], axis=0)
            vs[s, at, :] = st.T.astype(BF16)

    q = q_ref[0, 0, 0]
    qh = q.astype(BF16).astype(F32)
    qst = jnp.concatenate([qh, qh, q - qh, jnp.zeros_like(q)], axis=0).T[:, :3 * hw].astype(BF16)
    bias = jnp.concatenate(
        [
            jnp.concatenate([bias_ref[w, n] for n in range(parts)], axis=1)
            for w in range(bias_ref.shape[0])
        ],
        axis=0,
    )
    scores = mm(qst, ks[s]) + bias
    top = jnp.max(scores, axis=1, keepdims=True)
    ph, plo = split(jnp.exp(scores - top))
    t = (mm(ph, vs[s]) + mm(plo, vs[s])).T
    out_ref[0, 0] = (t[0:hw] + t[hw:2 * hw]) / t[2 * hw:2 * hw + 1]


def attention(qkv, bias, head, hw):
    parts, _, seqs, _, span = qkv.shape
    _, _, rows, _ = bias.shape
    per = span // rows
    return pl.pallas_call(
        functools.partial(attention_kernel, hw),
        out_shape=jax.ShapeDtypeStruct((parts, seqs, hw, span), F32),
        grid=(parts, seqs),
        in_specs=[
            pl.BlockSpec((1, 1, 1, hw, span), lambda b, s: (b, 0, s, head, 0)),
            pl.BlockSpec((parts, 1, 1, hw, span), lambda b, s: (0, 1, s, head, 0)),
            pl.BlockSpec((parts, 1, 1, hw, span), lambda b, s: (0, 2, s, head, 0)),
            pl.BlockSpec((per, parts, rows, span), lambda b, s: (b, 0, 0, 0)),
        ],
        out_specs=pl.BlockSpec((1, 1, hw, span), lambda b, s: (b, s, 0, 0)),
        scratch_shapes=[
            pltpu.VMEM((seqs, 3 * hw, parts * span), BF16),
            pltpu.VMEM((seqs, parts * span, 4 * hw), BF16),
        ],
        compiler_params=PARAMS,
        name="attention",
    )(qkv, qkv, qkv, bias)


def merge_kernel(*refs):
    heads = len(refs) - 12
    att = refs[:heads]
    gate_ref, x_ref, wm_ref, bm_ref, f1_ref, f2_ref, next_ref, left_ref, right_ref, m_hi, m_lo, f_st = refs[heads:]
    parts, _, _, _ = att[0].shape
    hid = f1_ref.shape[1]
    blocks, _, _, rows = left_ref.shape

    @pl.when(pl.program_id(0) == 0)
    def _():
        hi, lo = split(wm_ref[...])
        m_hi[...] = hi
        m_lo[...] = lo
        hi, lo = split(jnp.concatenate([f1_ref[...], f2_ref[...]], axis=1).T)
        f_st[0:2 * hid, :] = hi
        f_st[2 * hid:4 * hid, :] = lo

    a = jnp.concatenate([att[h][n, 0] for n in range(parts) for h in range(heads)], axis=0)
    ah, al = split((a * gate_ref[0]).T)
    y = x_ref[0] + (mm(ah, m_hi[...]) + mm(al, m_hi[...]) + mm(ah, m_lo[...])) + bm_ref[...]
    next_ref[0] = y
    zh, zl = split(norm_rows(y))
    p = mm_nt(f_st[...], zh)
    p = p[:2 * hid] + p[2 * hid:] + mm_nt(f_st[0:2 * hid, :], zl)
    for b in range(blocks):
        left_ref[b, 0] = p[:hid, b * rows:(b + 1) * rows]
    right_ref[0] = p[hid:]


def merge(att, gate, x, wm, bm, f1, f2, rows):
    seqs, span, ch = x.shape
    parts, _, hw, _ = att[0].shape
    hid = f1.shape[1]
    bm = bm.reshape(1, ch)
    blocks = span // rows
    return pl.pallas_call(
        merge_kernel,
        out_shape=(
            jax.ShapeDtypeStruct(x.shape, F32),
            jax.ShapeDtypeStruct((blocks, seqs, hid, rows), F32),
            jax.ShapeDtypeStruct((seqs, hid, span), F32),
        ),
        grid=(seqs,),
        in_specs=[pl.BlockSpec((parts, 1, hw, span), lambda s: (0, s, 0, 0)) for _ in att]
        + [
            pl.BlockSpec((1, ch, span), lambda s: (s, 0, 0)),
            pl.BlockSpec((1, span, ch), lambda s: (s, 0, 0)),
        ]
        + [whole(a) for a in (wm, bm, f1, f2)],
        out_specs=(
            pl.BlockSpec((1, span, ch), lambda s: (s, 0, 0)),
            pl.BlockSpec((blocks, 1, hid, rows), lambda s: (0, s, 0, 0)),
            pl.BlockSpec((1, hid, span), lambda s: (s, 0, 0)),
        ),
        scratch_shapes=[
            pltpu.VMEM((ch, ch), BF16),
            pltpu.VMEM((ch, ch), BF16),
            pltpu.VMEM((4 * hid, ch), BF16),
        ],
        compiler_params=PARAMS,
        name="merge",
    )(*att, gate, x, wm, bm, f1, f2)


def pair_kernel(
    step_rows, group, seqs, left_ref, right_ref, w_ref, pair_ref, ob_ref, up_ref, eb_ref, dn_ref,
    out_ref, r_hi, r_lo, w_st, up_st, dn_st,
):
    _, cols, cz = pair_ref.shape
    c_n = w_ref.shape[0]
    d_n = w_ref.shape[1] // cz

    @pl.when(pl.program_id(0) == 0)
    def _():
        hi, lo = split(right_ref[...])
        r_hi[...] = hi
        r_lo[...] = lo
        hi, lo = split(w_ref[...])
        w_st[0:c_n, :] = hi
        w_st[c_n:2 * c_n, :] = lo
        w_st[2 * c_n:3 * c_n, :] = hi
        hi, lo = split(up_ref[...])
        up_st[0:cz, :] = hi
        up_st[cz:2 * cz, :] = hi
        up_st[2 * cz:3 * cz, :] = lo
        hi, lo = split(dn_ref[...])
        dn_st[:, 0:cz] = hi
        dn_st[:, cz:2 * cz] = lo

    def body(p, carry):
        lrow = left_ref[pl.ds(pl.multiple_of(p * group * seqs, group * seqs), group * seqs), :]
        lhi = lrow.astype(BF16).astype(F32)
        u = mm(jnp.concatenate([lhi, lhi, lrow - lhi], axis=1).astype(BF16), w_st[...])
        his, los = [], []
        for q in range(group):
            sub = u[q * seqs:(q + 1) * seqs, :]
            hi, lo = split(jnp.concatenate([sub[:, d * cz:(d + 1) * cz] for d in range(d_n)], axis=0))
            his.append(hi)
            los.append(lo)
        mids = []
        for q in range(0, group, 2):
            cross = mm(r_lo[...], jnp.concatenate(his[q:q + 2], axis=1))
            for i in range(2):
                a = mm(r_hi[...], jnp.concatenate([his[q + i], los[q + i]], axis=1))
                o = a[:, :cz] + a[:, cz:] + cross[:, i * cz:(i + 1) * cz]
                mids.append(pair_ref[group * p + q + i] + o / seqs + ob_ref[...])
        for q in range(0, group, 2):
            mid = jnp.concatenate(mids[q:q + 2], axis=0)
            yh, yl = split(norm_rows(mid))
            h = mm(jnp.concatenate([yh, yl, yh], axis=1), up_st[...])
            hh, hl = split(jnp.maximum(h + eb_ref[...], 0.0))
            a = mm(hh, dn_st[...])
            o = mid + (a[:, :cz] + a[:, cz:] + mm(hl, dn_st[:, 0:cz]))
            for i in range(2):
                out_ref[group * p + q + i] = o[i * cols:(i + 1) * cols]
        return carry

    lax.fori_loop(0, step_rows // group, body, 0)


def pair_update(left_rows, right_cols, w2, pair, ob, up, eb, dn, step_rows=8, group=4):
    rows, cols, cz = pair.shape
    seqs = left_rows.shape[0] // rows
    c_n = w2.shape[0]
    ob = ob.reshape(1, -1)
    eb = eb.reshape(1, -1)
    return pl.pallas_call(
        functools.partial(pair_kernel, step_rows, group, seqs),
        out_shape=jax.ShapeDtypeStruct(pair.shape, F32),
        grid=(rows // step_rows,),
        in_specs=[
            pl.BlockSpec((step_rows * seqs, left_rows.shape[1]), lambda i: (i, 0)),
            whole(right_cols), whole(w2),
            pl.BlockSpec((step_rows, cols, cz), lambda i: (i, 0, 0)),
            whole(ob), whole(up), whole(eb), whole(dn),
        ],
        out_specs=pl.BlockSpec((step_rows, cols, cz), lambda i: (i, 0, 0)),
        scratch_shapes=[
            pltpu.VMEM(right_cols.shape, BF16),
            pltpu.VMEM(right_cols.shape, BF16),
            pltpu.VMEM((3 * c_n, w2.shape[1]), BF16),
            pltpu.VMEM((3 * cz, up.shape[1]), BF16),
            pltpu.VMEM((up.shape[1], 2 * cz), BF16),
        ],
        compiler_params=PARAMS,
        name="pair_update",
    )(left_rows, right_cols, w2, pair, ob, up, eb, dn)


def spread_heads(
    parts,
    homolog_embedding,
    pair_state,
    probe_projector,
    lookup_projector,
    content_projector,
    sigmoid_projector,
    sigmoid_offset,
    pair_bias_weight,
    mixing_projector,
    mixing_offset,
    first_factor_projector,
    second_factor_projector,
    outer_product_weight,
    outer_product_bias,
    up_weight,
    expand_bias,
    down_weight,
):
    _, _, ch = homolog_embedding.shape
    rows, cols, cz = pair_state.shape
    heads = pair_bias_weight.shape[1]
    hw = ch // heads
    own_heads = heads // parts
    hid = first_factor_projector.shape[1]

    bias = bias_tile(pair_state, pair_bias_weight).reshape(parts, own_heads, rows, cols)
    bias = lax.all_to_all(bias, "narrow", 0, 0, tiled=True)
    gathered = [
        lax.all_gather(bias[:, h], "wide", axis=0, tiled=False) for h in range(own_heads)
    ]
    qkv, gate = project(
        homolog_embedding, probe_projector, lookup_projector, content_projector, sigmoid_projector,
        sigmoid_offset, parts, hw,
    )
    qkv = lax.all_to_all(qkv, "narrow", 0, 0, tiled=True)
    att = [
        lax.all_to_all(attention(qkv, gathered[h], h, hw), "narrow", 0, 0, tiled=True)
        for h in range(own_heads)
    ]
    alignment_state_next, left, right = merge(
        att, gate, homolog_embedding, mixing_projector, mixing_offset,
        first_factor_projector, second_factor_projector, rows,
    )
    left = lax.all_gather(left, "narrow", axis=0, tiled=True)
    left = lax.all_to_all(left, "wide", 0, 0, tiled=True)
    right = lax.all_gather(right, "wide", axis=0, tiled=True)
    left = left.reshape(-1, hid, rows)
    all_seqs = left.shape[0]
    left_rows = jnp.transpose(left, (2, 0, 1)).reshape(rows * all_seqs, hid)
    right_cols = jnp.transpose(right, (2, 1, 0)).reshape(cols, hid * all_seqs)
    pair_state_next = pair_update(
        left_rows, right_cols, outer_product_weight.reshape(hid, hid * cz), pair_state,
        outer_product_bias, up_weight, expand_bias, down_weight,
    )
    return (alignment_state_next, pair_state_next)


AXES = ("wide", "narrow")
PLANES, CORES = 4, 2
PARTNER = {1: 2, 2: 1}
OUTWARD = {1: 0, 2: 3}
ORDER = ((0, 1, 2, 3), (1, 0, 2, 3), (2, 3, 1, 0), (3, 2, 1, 0))


def send(x, parts, route):
    pairs = []
    for z in range(PLANES):
        for c in range(CORES):
            for n in range(parts):
                to = route(z, c, n)
                if to is not None:
                    pairs.append(((z * CORES + c) * parts + n, (to[0] * CORES + to[1]) * parts + to[2]))
    return lax.ppermute(x, AXES, pairs)


def exchange(blocks, parts):
    out = [blocks[0]]
    for k in range(1, len(blocks)):
        dn, dc = divmod(k, CORES)
        out.append(send(blocks[k], parts, lambda z, c, n: (z, c ^ dc, n ^ dn)))
    return out


def line_gather(x, parts):
    middle = lambda table: lambda z, c, n: (table[z], c, n) if z in table else None
    near = send(x, parts, lambda z, c, n: (z ^ 1, c, n))
    across = send(x, parts, middle(PARTNER))
    out2 = send(across, parts, middle(OUTWARD))
    far = send(near, parts, middle(PARTNER))
    out3 = send(far, parts, middle(OUTWARD))
    return near, (across, out2), (far, out3)


def own_head(ids_ref):
    return ids_ref[1] * CORES + ids_ref[0] % CORES


def head_bias_kernel(group, ids_ref, pair_ref, w_ref, *refs):
    out_refs, lhs = refs[:-1], refs[-1]
    rows, cols, cz = pair_ref.shape
    heads = w_ref.shape[0]

    @pl.when(pl.program_id(0) == 0)
    def _():
        me = own_head(ids_ref)
        own = jnp.concatenate([w_ref[pl.ds(me ^ k, 1), :] for k in range(heads)], axis=0)
        hi = own.astype(BF16).astype(F32)
        both = jnp.concatenate([hi, own - hi], axis=0)
        lhs[...] = jnp.concatenate([both, both], axis=1).astype(BF16)

    for i in range(0, rows, group):
        yh, yl = split(norm_rows(pair_ref[i:i + group].reshape(group * cols, cz)))
        r = mm_nt(lhs[...], jnp.concatenate([yh, yl], axis=1))
        r = r[:heads] + r[heads:]
        for g in range(group):
            for k in range(heads):
                out_refs[k][i + g:i + g + 1, :] = r[k:k + 1, g * cols:(g + 1) * cols]


def head_bias(ids, pair, w, step=32, group=4):
    rows, cols, cz = pair.shape
    heads = w.shape[0]
    return pl.pallas_call(
        functools.partial(head_bias_kernel, group),
        out_shape=(jax.ShapeDtypeStruct((rows, cols), F32),) * heads,
        grid_spec=pltpu.PrefetchScalarGridSpec(
            num_scalar_prefetch=1,
            grid=(rows // step,),
            in_specs=[pl.BlockSpec((step, cols, cz), lambda i, _: (i, 0, 0)), whole(w)],
            out_specs=(pl.BlockSpec((step, cols), lambda i, _: (i, 0)),) * heads,
            scratch_shapes=[pltpu.VMEM((2 * heads, 2 * cz), BF16)],
        ),
        compiler_params=PARAMS,
        name="head_bias",
    )(ids, pair, w)


def head_project_kernel(heads, scale, ids_ref, x_ref, wq_ref, wk_ref, wv_ref, wg_ref, bg_ref, *refs):
    qkv_refs, (gate_ref, w_t, b_p, w_hi, w_lo) = refs[:heads], refs[heads:]
    ch = x_ref.shape[-1]
    hw = ch // heads

    @pl.when(pl.program_id(0) == 0)
    def _():
        me = own_head(ids_ref)
        for t, (ref, f) in enumerate(((wq_ref, scale), (wk_ref, 1.0), (wv_ref, 1.0), (wg_ref, 1.0))):
            w_t[...] = ref[...].T * f
            for k in range(heads):
                src = pl.ds(pl.multiple_of((me ^ k) * hw, hw), hw)
                hi, lo = split(w_t[src, :])
                at = slice(t * ch + k * hw, t * ch + (k + 1) * hw)
                w_hi[at, :] = hi
                w_lo[at, :] = lo
                if t == 3:
                    b_p[k * hw:(k + 1) * hw, :] = bg_ref[src, :]

    yh, yl = split(norm_rows(x_ref[0]))
    r = mm_nt(w_hi[...], yh) + mm_nt(w_hi[...], yl) + mm_nt(w_lo[...], yh)
    for t in range(3):
        for k in range(heads):
            lo = t * ch + k * hw
            qkv_refs[k][t, 0] = r[lo:lo + hw]
    gate_ref[0] = jax.nn.sigmoid(r[3 * ch:] + b_p[...])


def head_project(me, x, wq, wk, wv, wg, bg, heads):
    seqs, span, ch = x.shape
    hw = ch // heads
    bg = bg.reshape(ch, 1)
    return pl.pallas_call(
        functools.partial(head_project_kernel, heads, 1.0 / math.sqrt(hw)),
        out_shape=(jax.ShapeDtypeStruct((3, seqs, hw, span), F32),) * heads
        + (jax.ShapeDtypeStruct((seqs, ch, span), F32),),
        grid_spec=pltpu.PrefetchScalarGridSpec(
            num_scalar_prefetch=1,
            grid=(seqs,),
            in_specs=[pl.BlockSpec((1, span, ch), lambda s, _: (s, 0, 0))]
            + [whole(a) for a in (wq, wk, wv, wg, bg)],
            out_specs=(pl.BlockSpec((3, 1, hw, span), lambda s, _: (0, s, 0, 0)),) * heads
            + (pl.BlockSpec((1, ch, span), lambda s, _: (s, 0, 0)),),
            scratch_shapes=[
                pltpu.VMEM((ch, ch), F32),
                pltpu.VMEM((ch, 1), F32),
                pltpu.VMEM((4 * ch, ch), BF16),
                pltpu.VMEM((4 * ch, ch), BF16),
            ],
        ),
        compiler_params=PARAMS,
        name="head_project",
    )(me, x, wq, wk, wv, wg, bg)


def stage_kernel(n_ref, *refs):
    pieces, (q_ref, k_ref, v_ref) = refs[:-3], refs[-3:]
    _, _, hw, span = pieces[0].shape
    for p, ref in enumerate(pieces):
        part, core = divmod(p, CORES)
        at = slice(part * span, (part + 1) * span)
        q = ref[0, 0]
        qh = q.astype(BF16).astype(F32)
        q_ref[core, 0, (n_ref[0] - 1) ^ part] = (
            jnp.concatenate([qh, qh, q - qh, jnp.zeros_like(q)], axis=0).T.astype(BF16)
        )
        hi, lo = split(ref[1, 0])
        k_ref[core, 0, 0:hw, at] = hi
        k_ref[core, 0, hw:2 * hw, at] = lo
        k_ref[core, 0, 2 * hw:3 * hw, at] = hi
        k_ref[core, 0, 3 * hw:4 * hw, at] = jnp.zeros_like(hi)
        v = ref[2, 0]
        vh = v.astype(BF16).astype(F32)
        st = jnp.concatenate([vh, v - vh, jnp.ones((hw, span), F32), jnp.zeros((hw, span), F32)], axis=0)
        v_ref[core, 0, at, :] = st.T.astype(BF16)


def stage(n, pieces, parts):
    _, seqs, hw, span = pieces[0].shape
    return pl.pallas_call(
        stage_kernel,
        out_shape=(
            jax.ShapeDtypeStruct((CORES, seqs, parts, span, 4 * hw), BF16),
            jax.ShapeDtypeStruct((CORES, seqs, 4 * hw, parts * span), BF16),
            jax.ShapeDtypeStruct((CORES, seqs, parts * span, 4 * hw), BF16),
        ),
        grid_spec=pltpu.PrefetchScalarGridSpec(
            num_scalar_prefetch=1,
            grid=(seqs,),
            in_specs=[pl.BlockSpec((3, 1, hw, span), lambda s, _: (0, s, 0, 0)) for _ in pieces],
            out_specs=(
                pl.BlockSpec((CORES, 1, parts, span, 4 * hw), lambda s, _: (0, s, 0, 0, 0)),
                pl.BlockSpec((CORES, 1, 4 * hw, parts * span), lambda s, _: (0, s, 0, 0)),
                pl.BlockSpec((CORES, 1, parts * span, 4 * hw), lambda s, _: (0, s, 0, 0)),
            ),
        ),
        compiler_params=PARAMS,
        name="stage",
    )(n, *pieces)


def head_attention_kernel(hw, turn, tiles, at_ref, q_ref, k_ref, v_ref, *refs):
    bias_refs, out_ref = refs[:tiles], refs[-1]
    parts = bias_refs[0].shape[1]
    cores, seqs = q_ref.shape[:2]
    core = at_ref[3 * turn + 2]
    bias = jnp.concatenate(
        [
            jnp.concatenate([sum(b[h ^ core, n] for b in bias_refs) for n in range(parts)], axis=1)
            for h in range(CORES)
        ],
        axis=0,
    )
    for g in range(cores):
        for s in range(seqs):
            scores = mm(q_ref[g, s, 0], k_ref[g, s]) + bias
            top = jnp.max(scores, axis=1, keepdims=True)
            ph, plo = split(jnp.exp(scores - top))
            t = (mm(ph, v_ref[g, s]) + mm(plo, v_ref[g, s])).T
            out_ref[0, g, s] = (t[0:hw] + t[hw:2 * hw]) / t[2 * hw:2 * hw + 1]


def head_attention(at, turn, q, k, v, tiles, prev, hw, step=2):
    cores, seqs, parts, span, _ = q.shape
    before = () if prev is None else (prev,)
    return pl.pallas_call(
        functools.partial(head_attention_kernel, hw, turn, len(tiles)),
        out_shape=jax.ShapeDtypeStruct((parts, cores, seqs, hw, span), F32),
        grid_spec=pltpu.PrefetchScalarGridSpec(
            num_scalar_prefetch=1,
            grid=(seqs // step,),
            in_specs=[
                pl.BlockSpec((cores, step, 1, span, 4 * hw), lambda s, at: (0, s, at[3 * turn], 0, 0)),
                pl.BlockSpec((cores, step, 4 * hw, parts * span), lambda s, at: (0, s, 0, 0)),
                pl.BlockSpec((cores, step, parts * span, 4 * hw), lambda s, at: (0, s, 0, 0)),
            ]
            + [whole(b) for b in tiles]
            + [pl.BlockSpec(memory_space=pl.ANY) for _ in before],
            out_specs=pl.BlockSpec((1, cores, step, hw, span), lambda s, at: (at[3 * turn + 1], 0, s, 0, 0)),
        ),
        input_output_aliases={4 + len(tiles): 0} if before else {},
        compiler_params=PARAMS,
        name="head_attention",
    )(at, q, k, v, *tiles, *before)


def head_merge_kernel(heads, ids_ref, *refs):
    pieces = refs[:heads]
    gate_ref, x_ref, wm_ref, bm_ref, f1_ref, f2_ref = refs[heads:heads + 6]
    next_ref, left_refs, right_ref = refs[heads + 6], refs[heads + 7:heads + 9], refs[heads + 9]
    m_hi, m_lo, f_st = refs[heads + 10:]
    _, hw, span = pieces[0].shape
    hid = f1_ref.shape[0]
    rows = span // CORES

    @pl.when(pl.program_id(0) == 0)
    def _():
        for k in range(heads):
            hi, lo = split(wm_ref[pl.ds(pl.multiple_of((own_head(ids_ref) ^ k) * hw, hw), hw), :])
            m_hi[k * hw:(k + 1) * hw, :] = hi
            m_lo[k * hw:(k + 1) * hw, :] = lo
        hi, lo = split(jnp.concatenate([f1_ref[...], f2_ref[...]], axis=0))
        f_st[0:2 * hid, :] = hi
        f_st[2 * hid:4 * hid, :] = lo

    a = jnp.concatenate([p[0] for p in pieces], axis=0)
    ah, al = split((a * gate_ref[0]).T)
    y = x_ref[0] + (mm(ah, m_hi[...]) + mm(al, m_hi[...]) + mm(ah, m_lo[...])) + bm_ref[...]
    next_ref[0] = y
    zh, zl = split(norm_rows(y))
    p = mm_nt(f_st[...], zh)
    p = p[:2 * hid] + p[2 * hid:] + mm_nt(f_st[0:2 * hid, :], zl)
    swap = ids_ref[0] % CORES == 1
    left_refs[0][0] = jnp.where(swap, p[:hid, rows:], p[:hid, :rows])
    left_refs[1][0] = jnp.where(swap, p[:hid, :rows], p[:hid, rows:])
    right_ref[0] = p[hid:]


def head_merge(me, pieces, gate, x, wm, bm, f1, f2):
    seqs, span, ch = x.shape
    heads = len(pieces)
    hw = ch // heads
    hid = f1.shape[0]
    rows = span // CORES
    bm = bm.reshape(1, ch)
    return pl.pallas_call(
        functools.partial(head_merge_kernel, heads),
        out_shape=(jax.ShapeDtypeStruct(x.shape, F32),)
        + (jax.ShapeDtypeStruct((seqs, hid, rows), F32),) * CORES
        + (jax.ShapeDtypeStruct((seqs, hid, span), F32),),
        grid_spec=pltpu.PrefetchScalarGridSpec(
            num_scalar_prefetch=1,
            grid=(seqs,),
            in_specs=[pl.BlockSpec((1, hw, span), lambda s, _: (s, 0, 0)) for _ in pieces]
            + [
                pl.BlockSpec((1, ch, span), lambda s, _: (s, 0, 0)),
                pl.BlockSpec((1, span, ch), lambda s, _: (s, 0, 0)),
            ]
            + [whole(a) for a in (wm, bm, f1, f2)],
            out_specs=(pl.BlockSpec((1, span, ch), lambda s, _: (s, 0, 0)),)
            + (pl.BlockSpec((1, hid, rows), lambda s, _: (s, 0, 0)),) * CORES
            + (pl.BlockSpec((1, hid, span), lambda s, _: (s, 0, 0)),),
            scratch_shapes=[
                pltpu.VMEM((ch, ch), BF16),
                pltpu.VMEM((ch, ch), BF16),
                pltpu.VMEM((4 * hid, ch), BF16),
            ],
        ),
        compiler_params=PARAMS,
        name="head_merge",
    )(me, *pieces, gate, x, wm, bm, f1, f2)


def pack_kernel(slots_ref, *refs):
    left_refs, (own_ref, sib_ref, lr_ref, rc_ref, right) = refs[:-5], refs[-5:]
    cores, seqs, hid, rows = left_refs[0].shape
    slots = len(left_refs) * cores
    for i in range(own_ref.shape[0]):
        at = slots_ref[i] * cores
        for t, ref in enumerate((own_ref, sib_ref)):
            right[pl.ds((at + t) * seqs, seqs)] = ref[i]
    rt = jnp.concatenate([right[:, d, :] for d in range(hid)], axis=0)
    rc_ref[...] = rt.T
    for p, ref in enumerate(left_refs):
        for t in range(cores):
            for s in range(seqs):
                at = (p * cores + t) * seqs + s
                lr_ref[pl.ds(at, rows, stride=slots * seqs), :] = ref[t, s].T


def pack(slots, lefts, own, sib):
    cores, seqs, hid, rows = lefts[0].shape
    planes, _, _, cols = own.shape
    total = planes * cores * seqs
    return pl.pallas_call(
        pack_kernel,
        out_shape=(
            jax.ShapeDtypeStruct((rows * total, hid), F32),
            jax.ShapeDtypeStruct((cols, hid * total), F32),
        ),
        in_specs=[pl.BlockSpec(memory_space=pltpu.SMEM)]
        + [pl.BlockSpec(memory_space=pltpu.VMEM)] * (len(lefts) + 2),
        out_specs=(pl.BlockSpec(memory_space=pltpu.VMEM),) * 2,
        scratch_shapes=[pltpu.VMEM((total, hid, cols), F32)],
        compiler_params=PARAMS,
        name="pack",
    )(slots, *lefts, own, sib)


def after(x, *deps):
    return lax.optimization_barrier((x, deps))[0]


def per_head(
    parts,
    homolog_embedding,
    pair_state,
    probe_projector,
    lookup_projector,
    content_projector,
    sigmoid_projector,
    sigmoid_offset,
    pair_bias_weight,
    mixing_projector,
    mixing_offset,
    first_factor_projector,
    second_factor_projector,
    outer_product_weight,
    outer_product_bias,
    up_weight,
    expand_bias,
    down_weight,
):
    _, _, ch = homolog_embedding.shape
    _, _, cz = pair_state.shape
    heads = pair_bias_weight.shape[1]
    hw = ch // heads
    hid = first_factor_projector.shape[1]
    ids = jnp.stack([lax.axis_index("wide"), lax.axis_index("narrow")])
    tiles = head_bias(ids, pair_state, pair_bias_weight.T)
    late = after(ids, tiles[0])
    z, c, n = late[0] // CORES, late[0] % CORES, late[1]
    order = jnp.asarray(ORDER, jnp.int32)[z]
    at = jnp.stack([order, order ^ n, jnp.full_like(order, c)], axis=1).reshape(-1)
    slots = (jnp.arange(PLANES, dtype=jnp.int32) ^ z) ^ n
    *qkv, gate = head_project(
        ids, after(homolog_embedding, tiles[0], at, slots), probe_projector, lookup_projector, content_projector,
        sigmoid_projector, sigmoid_offset, heads,
    )
    tiles = after(exchange(tiles, parts), gate)
    bias = jnp.stack(
        [jnp.stack([tiles[p * CORES + r] for p in range(parts)]) for r in range(CORES)]
    )
    near, second, third = line_gather(bias, parts)
    qkv = exchange(after(qkv, bias), parts)
    marked = after(n[None], near, second[0]) + 1
    q, k, v = stage(marked, after(qkv, near, second[0]), parts)
    bias = after(bias, second[1], third[0])
    att = None
    for i, tile in enumerate(((bias,), (near,), second, third)):
        att = head_attention(at, i, q, k, v, tile, att, hw)
    pieces = exchange([att[p, r] for p in range(parts) for r in range(CORES)], parts)
    alignment_state_next, left_a, left_b, right = head_merge(
        ids, pieces, gate, homolog_embedding, mixing_projector, mixing_offset,
        first_factor_projector.T, second_factor_projector.T,
    )
    turn = lambda z0, c0, n0: (n0, c0, z0)
    left_b, left_a = send(left_b, parts, turn), send(left_a, parts, turn)
    sibling = lambda z0, c0, n0: (z0, c0 ^ 1, n0)
    left = jnp.stack([left_a, send(left_b, parts, sibling)])
    rights = [right] + [send(right, parts, lambda z0, c0, n0, d=d: (z0 ^ d, c0, n0)) for d in range(1, PLANES)]
    lefts = [left] + [send(left, parts, lambda z0, c0, n0, d=d: (z0, c0, n0 ^ d)) for d in range(1, parts)]
    own = jnp.stack(rights)
    left_rows, right_cols = pack(slots, lefts, own, send(own, parts, sibling))
    pair_state_next = pair_update(
        left_rows, right_cols, outer_product_weight.reshape(hid, hid * cz), pair_state,
        outer_product_bias, up_weight, expand_bias, down_weight,
    )
    return (alignment_state_next, pair_state_next)


def lines(mesh):
    return mesh.shape["wide"] == PLANES * CORES and mesh.shape["narrow"] == PLANES


def step(mesh, *args):
    parts = mesh.shape["narrow"]
    heads = args[7].shape[1]
    if lines(mesh) and heads == CORES * parts:
        return per_head(parts, *args)
    return spread_heads(parts, *args)


def solution(mesh):
    placed = (P("wide", "narrow", None), P("wide", "narrow", None)) + (P(),) * 15
    return jax.shard_map(
        functools.partial(step, mesh),
        mesh=mesh,
        in_specs=placed,
        out_specs=(P("wide", "narrow", None), P("wide", "narrow", None)),
        check_vma=False,
    )
```

```python
import functools
import math

import jax
import jax.numpy as jnp
from jax import lax
from jax.experimental import pallas as pl
from jax.experimental.pallas import tpu as pltpu
from jax.sharding import PartitionSpec as P


F32, BF16 = jnp.float32, jnp.bfloat16
PARAMS = pltpu.CompilerParams(vmem_limit_bytes=60 * 2**20)


def split(x):
    hi = x.astype(BF16)
    lo = (x - hi.astype(F32)).astype(BF16)
    return hi, lo


def mm(a, b):
    return jnp.dot(a, b, preferred_element_type=F32)


def mm_nt(a, b):
    return lax.dot_general(a, b, (((1,), (1,)), ((), ())), preferred_element_type=F32)


def norm_rows(x):
    mean = jnp.mean(x, axis=-1, keepdims=True)
    c = x - mean
    var = jnp.mean(c * c, axis=-1, keepdims=True)
    return c * lax.rsqrt(var + 1e-05)


def whole(a):
    return pl.BlockSpec(a.shape, lambda *_: (0,) * a.ndim, pipeline_mode=pl.Buffered(1))


def bias_kernel(pair_ref, w_ref, out_ref):
    rows, _, _ = pair_ref.shape
    heads = w_ref.shape[1]
    wh, wl = split(w_ref[...].T)
    lhs = jnp.concatenate(
        [jnp.concatenate([wh, wh], axis=1), jnp.concatenate([wl, wl], axis=1)], axis=0
    )
    for i in range(rows):
        yh, yl = split(norm_rows(pair_ref[i]))
        r = mm_nt(lhs, jnp.concatenate([yh, yl], axis=1))
        out_ref[:, i, :] = r[:heads] + r[heads:]


def bias_tile(pair, w, step=8):
    rows, cols, cz = pair.shape
    heads = w.shape[1]
    return pl.pallas_call(
        bias_kernel,
        out_shape=jax.ShapeDtypeStruct((heads, rows, cols), F32),
        grid=(rows // step,),
        in_specs=[pl.BlockSpec((step, cols, cz), lambda i: (i, 0, 0)), whole(w)],
        out_specs=pl.BlockSpec((heads, step, cols), lambda i: (0, i, 0)),
        compiler_params=PARAMS,
        name="bias_tile",
    )(pair, w)


def project_kernel(parts, scale, x_ref, wq_ref, wk_ref, wv_ref, wg_ref, bg_ref, qkv_ref, gate_ref, w_hi, w_lo):
    ch = x_ref.shape[-1]
    own = ch // parts

    @pl.when(pl.program_id(0) == 0)
    def _():
        for t, (ref, f) in enumerate(((wq_ref, scale), (wk_ref, 1.0), (wv_ref, 1.0), (wg_ref, 1.0))):
            hi, lo = split(ref[...].T * f)
            w_hi[t * ch:(t + 1) * ch, :] = hi
            w_lo[t * ch:(t + 1) * ch, :] = lo

    yh, yl = split(norm_rows(x_ref[0]))
    r = mm_nt(w_hi[...], yh) + mm_nt(w_hi[...], yl) + mm_nt(w_lo[...], yh)
    for t in range(3):
        for n in range(parts):
            lo = t * ch + n * own
            qkv_ref[n, t, 0] = r[lo:lo + own]
    gate_ref[0] = jax.nn.sigmoid(r[3 * ch:] + bg_ref[...])


def project(x, wq, wk, wv, wg, bg, parts, head_width):
    seqs, span, ch = x.shape
    own = ch // parts
    bg = bg.reshape(ch, 1)
    return pl.pallas_call(
        functools.partial(project_kernel, parts, 1.0 / math.sqrt(head_width)),
        out_shape=(
            jax.ShapeDtypeStruct((parts, 3, seqs, own, span), F32),
            jax.ShapeDtypeStruct((seqs, ch, span), F32),
        ),
        grid=(seqs,),
        in_specs=[pl.BlockSpec((1, span, ch), lambda s: (s, 0, 0))] + [whole(a) for a in (wq, wk, wv, wg, bg)],
        out_specs=(
            pl.BlockSpec((parts, 3, 1, own, span), lambda s: (0, 0, s, 0, 0)),
            pl.BlockSpec((1, ch, span), lambda s: (s, 0, 0)),
        ),
        scratch_shapes=[pltpu.VMEM((4 * ch, ch), BF16), pltpu.VMEM((4 * ch, ch), BF16)],
        compiler_params=PARAMS,
        name="project",
    )(x, wq, wk, wv, wg, bg)


def attention_kernel(hw, q_ref, k_ref, v_ref, bias_ref, out_ref, ks, vs):
    parts = k_ref.shape[0]
    span = k_ref.shape[-1]
    s = pl.program_id(1)

    @pl.when(pl.program_id(0) == 0)
    def _():
        for n in range(parts):
            at = slice(n * span, (n + 1) * span)
            hi, lo = split(k_ref[n, 0, 0])
            ks[s, 0:hw, at] = hi
            ks[s, hw:2 * hw, at] = lo
            ks[s, 2 * hw:3 * hw, at] = hi
            v = v_ref[n, 0, 0]
            vh = v.astype(BF16).astype(F32)
            st = jnp.concatenate([vh, v - vh, jnp.ones((hw, span), F32), jnp.zeros((hw, span), F32)], axis=0)
            vs[s, at, :] = st.T.astype(BF16)

    q = q_ref[0, 0, 0]
    qh = q.astype(BF16).astype(F32)
    qst = jnp.concatenate([qh, qh, q - qh, jnp.zeros_like(q)], axis=0).T[:, :3 * hw].astype(BF16)
    bias = jnp.concatenate(
        [
            jnp.concatenate([bias_ref[w, n] for n in range(parts)], axis=1)
            for w in range(bias_ref.shape[0])
        ],
        axis=0,
    )
    scores = mm(qst, ks[s]) + bias
    top = jnp.max(scores, axis=1, keepdims=True)
    ph, plo = split(jnp.exp(scores - top))
    t = (mm(ph, vs[s]) + mm(plo, vs[s])).T
    out_ref[0, 0] = (t[0:hw] + t[hw:2 * hw]) / t[2 * hw:2 * hw + 1]


def attention(qkv, bias, head, hw):
    parts, _, seqs, _, span = qkv.shape
    _, _, rows, _ = bias.shape
    per = span // rows
    return pl.pallas_call(
        functools.partial(attention_kernel, hw),
        out_shape=jax.ShapeDtypeStruct((parts, seqs, hw, span), F32),
        grid=(parts, seqs),
        in_specs=[
            pl.BlockSpec((1, 1, 1, hw, span), lambda b, s: (b, 0, s, head, 0)),
            pl.BlockSpec((parts, 1, 1, hw, span), lambda b, s: (0, 1, s, head, 0)),
            pl.BlockSpec((parts, 1, 1, hw, span), lambda b, s: (0, 2, s, head, 0)),
            pl.BlockSpec((per, parts, rows, span), lambda b, s: (b, 0, 0, 0)),
        ],
        out_specs=pl.BlockSpec((1, 1, hw, span), lambda b, s: (b, s, 0, 0)),
        scratch_shapes=[
            pltpu.VMEM((seqs, 3 * hw, parts * span), BF16),
            pltpu.VMEM((seqs, parts * span, 4 * hw), BF16),
        ],
        compiler_params=PARAMS,
        name="attention",
    )(qkv, qkv, qkv, bias)


def merge_kernel(*refs):
    heads = len(refs) - 12
    att = refs[:heads]
    gate_ref, x_ref, wm_ref, bm_ref, f1_ref, f2_ref, next_ref, left_ref, right_ref, m_hi, m_lo, f_st = refs[heads:]
    parts, _, _, _ = att[0].shape
    hid = f1_ref.shape[1]
    blocks, _, _, rows = left_ref.shape

    @pl.when(pl.program_id(0) == 0)
    def _():
        hi, lo = split(wm_ref[...])
        m_hi[...] = hi
        m_lo[...] = lo
        hi, lo = split(jnp.concatenate([f1_ref[...], f2_ref[...]], axis=1).T)
        f_st[0:2 * hid, :] = hi
        f_st[2 * hid:4 * hid, :] = lo

    a = jnp.concatenate([att[h][n, 0] for n in range(parts) for h in range(heads)], axis=0)
    ah, al = split((a * gate_ref[0]).T)
    y = x_ref[0] + (mm(ah, m_hi[...]) + mm(al, m_hi[...]) + mm(ah, m_lo[...])) + bm_ref[...]
    next_ref[0] = y
    zh, zl = split(norm_rows(y))
    p = mm_nt(f_st[...], zh)
    p = p[:2 * hid] + p[2 * hid:] + mm_nt(f_st[0:2 * hid, :], zl)
    for b in range(blocks):
        left_ref[b, 0] = p[:hid, b * rows:(b + 1) * rows]
    right_ref[0] = p[hid:]


def merge(att, gate, x, wm, bm, f1, f2, rows):
    seqs, span, ch = x.shape
    parts, _, hw, _ = att[0].shape
    hid = f1.shape[1]
    bm = bm.reshape(1, ch)
    blocks = span // rows
    return pl.pallas_call(
        merge_kernel,
        out_shape=(
            jax.ShapeDtypeStruct(x.shape, F32),
            jax.ShapeDtypeStruct((blocks, seqs, hid, rows), F32),
            jax.ShapeDtypeStruct((seqs, hid, span), F32),
        ),
        grid=(seqs,),
        in_specs=[pl.BlockSpec((parts, 1, hw, span), lambda s: (0, s, 0, 0)) for _ in att]
        + [
            pl.BlockSpec((1, ch, span), lambda s: (s, 0, 0)),
            pl.BlockSpec((1, span, ch), lambda s: (s, 0, 0)),
        ]
        + [whole(a) for a in (wm, bm, f1, f2)],
        out_specs=(
            pl.BlockSpec((1, span, ch), lambda s: (s, 0, 0)),
            pl.BlockSpec((blocks, 1, hid, rows), lambda s: (0, s, 0, 0)),
            pl.BlockSpec((1, hid, span), lambda s: (s, 0, 0)),
        ),
        scratch_shapes=[
            pltpu.VMEM((ch, ch), BF16),
            pltpu.VMEM((ch, ch), BF16),
            pltpu.VMEM((4 * hid, ch), BF16),
        ],
        compiler_params=PARAMS,
        name="merge",
    )(*att, gate, x, wm, bm, f1, f2)


def pair_kernel(
    step_rows, group, seqs, left_ref, right_ref, w_ref, pair_ref, ob_ref, up_ref, eb_ref, dn_ref,
    out_ref, r_hi, r_lo, w_st, up_st, dn_st,
):
    _, cols, cz = pair_ref.shape
    c_n = w_ref.shape[0]
    d_n = w_ref.shape[1] // cz

    @pl.when(pl.program_id(0) == 0)
    def _():
        hi, lo = split(right_ref[...])
        r_hi[...] = hi
        r_lo[...] = lo
        hi, lo = split(w_ref[...])
        w_st[0:c_n, :] = hi
        w_st[c_n:2 * c_n, :] = lo
        w_st[2 * c_n:3 * c_n, :] = hi
        hi, lo = split(up_ref[...])
        up_st[0:cz, :] = hi
        up_st[cz:2 * cz, :] = hi
        up_st[2 * cz:3 * cz, :] = lo
        hi, lo = split(dn_ref[...])
        dn_st[:, 0:cz] = hi
        dn_st[:, cz:2 * cz] = lo

    def body(p, carry):
        lrow = left_ref[pl.ds(pl.multiple_of(p * group * seqs, group * seqs), group * seqs), :]
        lhi = lrow.astype(BF16).astype(F32)
        u = mm(jnp.concatenate([lhi, lhi, lrow - lhi], axis=1).astype(BF16), w_st[...])
        his, los = [], []
        for q in range(group):
            sub = u[q * seqs:(q + 1) * seqs, :]
            hi, lo = split(jnp.concatenate([sub[:, d * cz:(d + 1) * cz] for d in range(d_n)], axis=0))
            his.append(hi)
            los.append(lo)
        mids = []
        for q in range(0, group, 2):
            cross = mm(r_lo[...], jnp.concatenate(his[q:q + 2], axis=1))
            for i in range(2):
                a = mm(r_hi[...], jnp.concatenate([his[q + i], los[q + i]], axis=1))
                o = a[:, :cz] + a[:, cz:] + cross[:, i * cz:(i + 1) * cz]
                mids.append(pair_ref[group * p + q + i] + o / seqs + ob_ref[...])
        for q in range(0, group, 2):
            mid = jnp.concatenate(mids[q:q + 2], axis=0)
            yh, yl = split(norm_rows(mid))
            h = mm(jnp.concatenate([yh, yl, yh], axis=1), up_st[...])
            hh, hl = split(jnp.maximum(h + eb_ref[...], 0.0))
            a = mm(hh, dn_st[...])
            o = mid + (a[:, :cz] + a[:, cz:] + mm(hl, dn_st[:, 0:cz]))
            for i in range(2):
                out_ref[group * p + q + i] = o[i * cols:(i + 1) * cols]
        return carry

    lax.fori_loop(0, step_rows // group, body, 0)


def pair_update(left_rows, right_cols, w2, pair, ob, up, eb, dn, step_rows=8, group=4):
    rows, cols, cz = pair.shape
    seqs = left_rows.shape[0] // rows
    c_n = w2.shape[0]
    ob = ob.reshape(1, -1)
    eb = eb.reshape(1, -1)
    return pl.pallas_call(
        functools.partial(pair_kernel, step_rows, group, seqs),
        out_shape=jax.ShapeDtypeStruct(pair.shape, F32),
        grid=(rows // step_rows,),
        in_specs=[
            pl.BlockSpec((step_rows * seqs, left_rows.shape[1]), lambda i: (i, 0)),
            whole(right_cols), whole(w2),
            pl.BlockSpec((step_rows, cols, cz), lambda i: (i, 0, 0)),
            whole(ob), whole(up), whole(eb), whole(dn),
        ],
        out_specs=pl.BlockSpec((step_rows, cols, cz), lambda i: (i, 0, 0)),
        scratch_shapes=[
            pltpu.VMEM(right_cols.shape, BF16),
            pltpu.VMEM(right_cols.shape, BF16),
            pltpu.VMEM((3 * c_n, w2.shape[1]), BF16),
            pltpu.VMEM((3 * cz, up.shape[1]), BF16),
            pltpu.VMEM((up.shape[1], 2 * cz), BF16),
        ],
        compiler_params=PARAMS,
        name="pair_update",
    )(left_rows, right_cols, w2, pair, ob, up, eb, dn)


def spread_heads(
    parts,
    homolog_embedding,
    pair_state,
    probe_projector,
    lookup_projector,
    content_projector,
    sigmoid_projector,
    sigmoid_offset,
    pair_bias_weight,
    mixing_projector,
    mixing_offset,
    first_factor_projector,
    second_factor_projector,
    outer_product_weight,
    outer_product_bias,
    up_weight,
    expand_bias,
    down_weight,
):
    _, _, ch = homolog_embedding.shape
    rows, cols, cz = pair_state.shape
    heads = pair_bias_weight.shape[1]
    hw = ch // heads
    own_heads = heads // parts
    hid = first_factor_projector.shape[1]

    bias = bias_tile(pair_state, pair_bias_weight).reshape(parts, own_heads, rows, cols)
    bias = lax.all_to_all(bias, "narrow", 0, 0, tiled=True)
    gathered = [
        lax.all_gather(bias[:, h], "wide", axis=0, tiled=False) for h in range(own_heads)
    ]
    qkv, gate = project(
        homolog_embedding, probe_projector, lookup_projector, content_projector, sigmoid_projector,
        sigmoid_offset, parts, hw,
    )
    qkv = lax.all_to_all(qkv, "narrow", 0, 0, tiled=True)
    att = [
        lax.all_to_all(attention(qkv, gathered[h], h, hw), "narrow", 0, 0, tiled=True)
        for h in range(own_heads)
    ]
    alignment_state_next, left, right = merge(
        att, gate, homolog_embedding, mixing_projector, mixing_offset,
        first_factor_projector, second_factor_projector, rows,
    )
    left = lax.all_gather(left, "narrow", axis=0, tiled=True)
    left = lax.all_to_all(left, "wide", 0, 0, tiled=True)
    right = lax.all_gather(right, "wide", axis=0, tiled=True)
    left = left.reshape(-1, hid, rows)
    all_seqs = left.shape[0]
    left_rows = jnp.transpose(left, (2, 0, 1)).reshape(rows * all_seqs, hid)
    right_cols = jnp.transpose(right, (2, 1, 0)).reshape(cols, hid * all_seqs)
    pair_state_next = pair_update(
        left_rows, right_cols, outer_product_weight.reshape(hid, hid * cz), pair_state,
        outer_product_bias, up_weight, expand_bias, down_weight,
    )
    return (alignment_state_next, pair_state_next)


AXES = ("wide", "narrow")
PLANES, CORES = 4, 2
PARTNER = {1: 2, 2: 1}
OUTWARD = {1: 0, 2: 3}
ORDER = ((0, 1, 2, 3), (1, 0, 2, 3), (2, 3, 1, 0), (3, 2, 1, 0))


def send(x, parts, route):
    pairs = []
    for z in range(PLANES):
        for c in range(CORES):
            for n in range(parts):
                to = route(z, c, n)
                if to is not None:
                    pairs.append(((z * CORES + c) * parts + n, (to[0] * CORES + to[1]) * parts + to[2]))
    return lax.ppermute(x, AXES, pairs)


def exchange(blocks, parts):
    out = [blocks[0]]
    for k in range(1, len(blocks)):
        dn, dc = divmod(k, CORES)
        out.append(send(blocks[k], parts, lambda z, c, n: (z, c ^ dc, n ^ dn)))
    return out


def line_gather(x, parts):
    middle = lambda table: lambda z, c, n: (table[z], c, n) if z in table else None
    near = send(x, parts, lambda z, c, n: (z ^ 1, c, n))
    across = send(x, parts, middle(PARTNER))
    out2 = send(across, parts, middle(OUTWARD))
    far = send(near, parts, middle(PARTNER))
    out3 = send(far, parts, middle(OUTWARD))
    return near, (across, out2), (far, out3)


def own_head(ids_ref):
    return ids_ref[1] * CORES + ids_ref[0] % CORES


def head_bias_kernel(group, ids_ref, pair_ref, w_ref, *refs):
    out_refs, lhs = refs[:-1], refs[-1]
    rows, cols, cz = pair_ref.shape
    heads = w_ref.shape[0]

    @pl.when(pl.program_id(0) == 0)
    def _():
        me = own_head(ids_ref)
        own = jnp.concatenate([w_ref[pl.ds(me ^ k, 1), :] for k in range(heads)], axis=0)
        hi = own.astype(BF16).astype(F32)
        both = jnp.concatenate([hi, own - hi], axis=0)
        lhs[...] = jnp.concatenate([both, both], axis=1).astype(BF16)

    for i in range(0, rows, group):
        yh, yl = split(norm_rows(pair_ref[i:i + group].reshape(group * cols, cz)))
        r = mm_nt(lhs[...], jnp.concatenate([yh, yl], axis=1))
        r = r[:heads] + r[heads:]
        for g in range(group):
            for k in range(heads):
                out_refs[k][i + g:i + g + 1, :] = r[k:k + 1, g * cols:(g + 1) * cols]


def head_bias(ids, pair, w, step=32, group=4):
    rows, cols, cz = pair.shape
    heads = w.shape[0]
    return pl.pallas_call(
        functools.partial(head_bias_kernel, group),
        out_shape=(jax.ShapeDtypeStruct((rows, cols), F32),) * heads,
        grid_spec=pltpu.PrefetchScalarGridSpec(
            num_scalar_prefetch=1,
            grid=(rows // step,),
            in_specs=[pl.BlockSpec((step, cols, cz), lambda i, _: (i, 0, 0)), whole(w)],
            out_specs=(pl.BlockSpec((step, cols), lambda i, _: (i, 0)),) * heads,
            scratch_shapes=[pltpu.VMEM((2 * heads, 2 * cz), BF16)],
        ),
        compiler_params=PARAMS,
        name="head_bias",
    )(ids, pair, w)


def head_project_kernel(heads, scale, ids_ref, x_ref, wq_ref, wk_ref, wv_ref, wg_ref, bg_ref, *refs):
    qkv_refs, (gate_ref, w_t, b_p, w_hi, w_lo) = refs[:heads], refs[heads:]
    ch = x_ref.shape[-1]
    hw = ch // heads

    @pl.when(pl.program_id(0) == 0)
    def _():
        me = own_head(ids_ref)
        for t, (ref, f) in enumerate(((wq_ref, scale), (wk_ref, 1.0), (wv_ref, 1.0), (wg_ref, 1.0))):
            w_t[...] = ref[...].T * f
            for k in range(heads):
                src = pl.ds(pl.multiple_of((me ^ k) * hw, hw), hw)
                hi, lo = split(w_t[src, :])
                at = slice(t * ch + k * hw, t * ch + (k + 1) * hw)
                w_hi[at, :] = hi
                w_lo[at, :] = lo
                if t == 3:
                    b_p[k * hw:(k + 1) * hw, :] = bg_ref[src, :]

    yh, yl = split(norm_rows(x_ref[0]))
    r = mm_nt(w_hi[...], yh) + mm_nt(w_hi[...], yl) + mm_nt(w_lo[...], yh)
    for t in range(3):
        for k in range(heads):
            lo = t * ch + k * hw
            qkv_refs[k][t, 0] = r[lo:lo + hw]
    gate_ref[0] = jax.nn.sigmoid(r[3 * ch:] + b_p[...])


def head_project(me, x, wq, wk, wv, wg, bg, heads):
    seqs, span, ch = x.shape
    hw = ch // heads
    bg = bg.reshape(ch, 1)
    return pl.pallas_call(
        functools.partial(head_project_kernel, heads, 1.0 / math.sqrt(hw)),
        out_shape=(jax.ShapeDtypeStruct((3, seqs, hw, span), F32),) * heads
        + (jax.ShapeDtypeStruct((seqs, ch, span), F32),),
        grid_spec=pltpu.PrefetchScalarGridSpec(
            num_scalar_prefetch=1,
            grid=(seqs,),
            in_specs=[pl.BlockSpec((1, span, ch), lambda s, _: (s, 0, 0))]
            + [whole(a) for a in (wq, wk, wv, wg, bg)],
            out_specs=(pl.BlockSpec((3, 1, hw, span), lambda s, _: (0, s, 0, 0)),) * heads
            + (pl.BlockSpec((1, ch, span), lambda s, _: (s, 0, 0)),),
            scratch_shapes=[
                pltpu.VMEM((ch, ch), F32),
                pltpu.VMEM((ch, 1), F32),
                pltpu.VMEM((4 * ch, ch), BF16),
                pltpu.VMEM((4 * ch, ch), BF16),
            ],
        ),
        compiler_params=PARAMS,
        name="head_project",
    )(me, x, wq, wk, wv, wg, bg)


def stage_kernel(n_ref, *refs):
    pieces, (q_ref, k_ref, v_ref) = refs[:-3], refs[-3:]
    _, _, hw, span = pieces[0].shape
    for p, ref in enumerate(pieces):
        part, core = divmod(p, CORES)
        at = slice(part * span, (part + 1) * span)
        q = ref[0, 0]
        qh = q.astype(BF16).astype(F32)
        q_ref[core, 0, (n_ref[0] - 1) ^ part] = (
            jnp.concatenate([qh, qh, q - qh, jnp.zeros_like(q)], axis=0).T.astype(BF16)
        )
        hi, lo = split(ref[1, 0])
        k_ref[core, 0, 0:hw, at] = hi
        k_ref[core, 0, hw:2 * hw, at] = lo
        k_ref[core, 0, 2 * hw:3 * hw, at] = hi
        k_ref[core, 0, 3 * hw:4 * hw, at] = jnp.zeros_like(hi)
        v = ref[2, 0]
        vh = v.astype(BF16).astype(F32)
        st = jnp.concatenate([vh, v - vh, jnp.ones((hw, span), F32), jnp.zeros((hw, span), F32)], axis=0)
        v_ref[core, 0, at, :] = st.T.astype(BF16)


def stage(n, pieces, parts):
    _, seqs, hw, span = pieces[0].shape
    return pl.pallas_call(
        stage_kernel,
        out_shape=(
            jax.ShapeDtypeStruct((CORES, seqs, parts, span, 4 * hw), BF16),
            jax.ShapeDtypeStruct((CORES, seqs, 4 * hw, parts * span), BF16),
            jax.ShapeDtypeStruct((CORES, seqs, parts * span, 4 * hw), BF16),
        ),
        grid_spec=pltpu.PrefetchScalarGridSpec(
            num_scalar_prefetch=1,
            grid=(seqs,),
            in_specs=[pl.BlockSpec((3, 1, hw, span), lambda s, _: (0, s, 0, 0)) for _ in pieces],
            out_specs=(
                pl.BlockSpec((CORES, 1, parts, span, 4 * hw), lambda s, _: (0, s, 0, 0, 0)),
                pl.BlockSpec((CORES, 1, 4 * hw, parts * span), lambda s, _: (0, s, 0, 0)),
                pl.BlockSpec((CORES, 1, parts * span, 4 * hw), lambda s, _: (0, s, 0, 0)),
            ),
        ),
        compiler_params=PARAMS,
        name="stage",
    )(n, *pieces)


def head_attention_kernel(hw, turn, tiles, at_ref, q_ref, k_ref, v_ref, *refs):
    bias_refs, out_ref = refs[:tiles], refs[-1]
    parts = bias_refs[0].shape[1]
    cores, seqs = q_ref.shape[:2]
    core = at_ref[3 * turn + 2]
    bias = jnp.concatenate(
        [
            jnp.concatenate([sum(b[h ^ core, n] for b in bias_refs) for n in range(parts)], axis=1)
            for h in range(CORES)
        ],
        axis=0,
    )
    score = lambda g, s: mm(q_ref[g, s, 0], k_ref[g, s]) + bias
    items = [(g, s) for s in range(seqs) for g in range(cores)]
    ahead = score(*items[0])
    for i, (g, s) in enumerate(items):
        scores = ahead
        if i + 1 < len(items):
            ahead = score(*items[i + 1])
        top = jnp.max(scores, axis=1, keepdims=True)
        ph, plo = split(jnp.exp(scores - top))
        t = (mm(ph, v_ref[g, s]) + mm(plo, v_ref[g, s])).T
        out_ref[0, g, s] = (t[0:hw] + t[hw:2 * hw]) / t[2 * hw:2 * hw + 1]


def head_attention(at, turn, q, k, v, tiles, prev, hw, step=2):
    cores, seqs, parts, span, _ = q.shape
    before = () if prev is None else (prev,)
    return pl.pallas_call(
        functools.partial(head_attention_kernel, hw, turn, len(tiles)),
        out_shape=jax.ShapeDtypeStruct((parts, cores, seqs, hw, span), F32),
        grid_spec=pltpu.PrefetchScalarGridSpec(
            num_scalar_prefetch=1,
            grid=(seqs // step,),
            in_specs=[
                pl.BlockSpec((cores, step, 1, span, 4 * hw), lambda s, at: (0, s, at[3 * turn], 0, 0)),
                pl.BlockSpec((cores, step, 4 * hw, parts * span), lambda s, at: (0, s, 0, 0)),
                pl.BlockSpec((cores, step, parts * span, 4 * hw), lambda s, at: (0, s, 0, 0)),
            ]
            + [whole(b) for b in tiles]
            + [pl.BlockSpec(memory_space=pl.ANY) for _ in before],
            out_specs=pl.BlockSpec((1, cores, step, hw, span), lambda s, at: (at[3 * turn + 1], 0, s, 0, 0)),
        ),
        input_output_aliases={4 + len(tiles): 0} if before else {},
        compiler_params=PARAMS,
        name="head_attention",
    )(at, q, k, v, *tiles, *before)


def head_merge_kernel(heads, ids_ref, *refs):
    pieces = refs[:heads]
    gate_ref, x_ref, wm_ref, bm_ref, f1_ref, f2_ref = refs[heads:heads + 6]
    next_ref, left_ref, right_ref, m_hi, m_lo, f_st = refs[heads + 6:]
    _, hw, span = pieces[0].shape
    hid = f1_ref.shape[0]
    rows = span // CORES

    @pl.when(pl.program_id(0) == 0)
    def _():
        for k in range(heads):
            hi, lo = split(wm_ref[pl.ds(pl.multiple_of((own_head(ids_ref) ^ k) * hw, hw), hw), :])
            m_hi[k * hw:(k + 1) * hw, :] = hi
            m_lo[k * hw:(k + 1) * hw, :] = lo
        hi, lo = split(jnp.concatenate([f1_ref[...], f2_ref[...]], axis=0))
        f_st[0:2 * hid, :] = hi
        f_st[2 * hid:4 * hid, :] = lo

    swap = ids_ref[0] % CORES == 1
    for s in range(x_ref.shape[0]):
        a = jnp.concatenate([p[s] for p in pieces], axis=0)
        ah, al = split((a * gate_ref[s]).T)
        y = x_ref[s] + (mm(ah, m_hi[...]) + mm(al, m_hi[...]) + mm(ah, m_lo[...])) + bm_ref[...]
        next_ref[s] = y
        zh, zl = split(norm_rows(y))
        p = mm_nt(f_st[...], zh)
        p = p[:2 * hid] + p[2 * hid:] + mm_nt(f_st[0:2 * hid, :], zl)
        left_ref[0, s] = jnp.where(swap, p[:hid, rows:], p[:hid, :rows])
        left_ref[1, s] = jnp.where(swap, p[:hid, :rows], p[:hid, rows:])
        right_ref[s] = p[hid:]


def head_merge(me, pieces, gate, x, wm, bm, f1, f2, step=2):
    seqs, span, ch = x.shape
    heads = len(pieces)
    hw = ch // heads
    hid = f1.shape[0]
    rows = span // CORES
    bm = bm.reshape(1, ch)
    return pl.pallas_call(
        functools.partial(head_merge_kernel, heads),
        out_shape=(jax.ShapeDtypeStruct(x.shape, F32),)
        + (jax.ShapeDtypeStruct((CORES, seqs, hid, rows), F32),)
        + (jax.ShapeDtypeStruct((seqs, hid, span), F32),),
        grid_spec=pltpu.PrefetchScalarGridSpec(
            num_scalar_prefetch=1,
            grid=(seqs // step,),
            in_specs=[pl.BlockSpec((step, hw, span), lambda s, _: (s, 0, 0)) for _ in pieces]
            + [
                pl.BlockSpec((step, ch, span), lambda s, _: (s, 0, 0)),
                pl.BlockSpec((step, span, ch), lambda s, _: (s, 0, 0)),
            ]
            + [whole(a) for a in (wm, bm, f1, f2)],
            out_specs=(
                pl.BlockSpec((step, span, ch), lambda s, _: (s, 0, 0)),
                pl.BlockSpec((CORES, step, hid, rows), lambda s, _: (0, s, 0, 0)),
                pl.BlockSpec((step, hid, span), lambda s, _: (s, 0, 0)),
            ),
            scratch_shapes=[
                pltpu.VMEM((ch, ch), BF16),
                pltpu.VMEM((ch, ch), BF16),
                pltpu.VMEM((4 * hid, ch), BF16),
            ],
        ),
        compiler_params=PARAMS,
        name="head_merge",
    )(me, *pieces, gate, x, wm, bm, f1, f2)


def pack_kernel(slots_ref, *refs):
    left_refs, (own_ref, sib_ref, lr_ref, rc_ref, right) = refs[:-5], refs[-5:]
    cores, seqs, hid, rows = left_refs[0].shape
    slots = len(left_refs) * cores
    for i in range(own_ref.shape[0]):
        at = slots_ref[i] * cores
        for t, ref in enumerate((own_ref, sib_ref)):
            right[pl.ds((at + t) * seqs, seqs)] = ref[i]
    rt = jnp.concatenate([right[:, d, :] for d in range(hid)], axis=0)
    rc_ref[...] = rt.T
    for p, ref in enumerate(left_refs):
        for t in range(cores):
            for s in range(seqs):
                at = (p * cores + t) * seqs + s
                lr_ref[pl.ds(at, rows, stride=slots * seqs), :] = ref[t, s].T


def pack(slots, lefts, own, sib):
    cores, seqs, hid, rows = lefts[0].shape
    planes, _, _, cols = own.shape
    total = planes * cores * seqs
    return pl.pallas_call(
        pack_kernel,
        out_shape=(
            jax.ShapeDtypeStruct((rows * total, hid), F32),
            jax.ShapeDtypeStruct((cols, hid * total), F32),
        ),
        in_specs=[pl.BlockSpec(memory_space=pltpu.SMEM)]
        + [pl.BlockSpec(memory_space=pltpu.VMEM)] * (len(lefts) + 2),
        out_specs=(pl.BlockSpec(memory_space=pltpu.VMEM),) * 2,
        scratch_shapes=[pltpu.VMEM((total, hid, cols), F32)],
        compiler_params=PARAMS,
        name="pack",
    )(slots, *lefts, own, sib)


def after(x, *deps):
    return lax.optimization_barrier((x, deps))[0]


def per_head(
    parts,
    homolog_embedding,
    pair_state,
    probe_projector,
    lookup_projector,
    content_projector,
    sigmoid_projector,
    sigmoid_offset,
    pair_bias_weight,
    mixing_projector,
    mixing_offset,
    first_factor_projector,
    second_factor_projector,
    outer_product_weight,
    outer_product_bias,
    up_weight,
    expand_bias,
    down_weight,
):
    _, _, ch = homolog_embedding.shape
    _, _, cz = pair_state.shape
    heads = pair_bias_weight.shape[1]
    hw = ch // heads
    hid = first_factor_projector.shape[1]
    ids = jnp.stack([lax.axis_index("wide"), lax.axis_index("narrow")])
    tiles = head_bias(ids, pair_state, pair_bias_weight.T)
    late = after(ids, tiles[0])
    z, c, n = late[0] // CORES, late[0] % CORES, late[1]
    order = jnp.asarray(ORDER, jnp.int32)[z]
    at = jnp.stack([order, order ^ n, jnp.full_like(order, c)], axis=1).reshape(-1)
    slots = (jnp.arange(PLANES, dtype=jnp.int32) ^ z) ^ n
    *qkv, gate = head_project(
        ids, after(homolog_embedding, tiles[0], at, slots), probe_projector, lookup_projector, content_projector,
        sigmoid_projector, sigmoid_offset, heads,
    )
    tiles = after(exchange(tiles, parts), gate)
    bias = jnp.stack(
        [jnp.stack([tiles[p * CORES + r] for p in range(parts)]) for r in range(CORES)]
    )
    near, second, third = line_gather(bias, parts)
    qkv = exchange(after(qkv, bias), parts)
    marked = after(n[None], near, second[0]) + 1
    q, k, v = stage(marked, after(qkv, near, second[0]), parts)
    bias = after(bias, second[1], third[0])
    att = None
    for i, tile in enumerate(((bias,), (near,), second, third)):
        att = head_attention(at, i, q, k, v, tile, att, hw)
    pieces = exchange([att[p, r] for p in range(parts) for r in range(CORES)], parts)
    alignment_state_next, left, right = head_merge(
        ids, pieces, gate, homolog_embedding, mixing_projector, mixing_offset,
        first_factor_projector.T, second_factor_projector.T,
    )
    turn = lambda z0, c0, n0: (n0, c0, z0)
    left = send(left, parts, turn)
    sibling = lambda z0, c0, n0: (z0, c0 ^ 1, n0)
    left = jnp.stack([left[0], send(left[1], parts, sibling)])
    rights = [right] + [send(right, parts, lambda z0, c0, n0, d=d: (z0 ^ d, c0, n0)) for d in range(1, PLANES)]
    lefts = [left] + [send(left, parts, lambda z0, c0, n0, d=d: (z0, c0, n0 ^ d)) for d in range(1, parts)]
    own = jnp.stack(rights)
    left_rows, right_cols = pack(slots, lefts, own, send(own, parts, sibling))
    pair_state_next = pair_update(
        left_rows, right_cols, outer_product_weight.reshape(hid, hid * cz), pair_state,
        outer_product_bias, up_weight, expand_bias, down_weight,
    )
    return (alignment_state_next, pair_state_next)


def lines(mesh):
    return mesh.shape["wide"] == PLANES * CORES and mesh.shape["narrow"] == PLANES


def step(mesh, *args):
    parts = mesh.shape["narrow"]
    heads = args[7].shape[1]
    if lines(mesh) and heads == CORES * parts:
        return per_head(parts, *args)
    return spread_heads(parts, *args)


def solution(mesh):
    placed = (P("wide", "narrow", None), P("wide", "narrow", None)) + (P(),) * 15
    return jax.shard_map(
        functools.partial(step, mesh),
        mesh=mesh,
        in_specs=placed,
        out_specs=(P("wide", "narrow", None), P("wide", "narrow", None)),
        check_vma=False,
    )
```

```python
import functools
import math

import jax
import jax.numpy as jnp
from jax import lax
from jax.experimental import pallas as pl
from jax.experimental.pallas import tpu as pltpu
from jax.sharding import PartitionSpec as P


F32, BF16 = jnp.float32, jnp.bfloat16
PARAMS = pltpu.CompilerParams(vmem_limit_bytes=60 * 2**20)


def split(x):
    hi = x.astype(BF16)
    lo = (x - hi.astype(F32)).astype(BF16)
    return hi, lo


def mm(a, b):
    return jnp.dot(a, b, preferred_element_type=F32)


def mm_nt(a, b):
    return lax.dot_general(a, b, (((1,), (1,)), ((), ())), preferred_element_type=F32)


def norm_rows(x):
    mean = jnp.mean(x, axis=-1, keepdims=True)
    c = x - mean
    var = jnp.mean(c * c, axis=-1, keepdims=True)
    return c * lax.rsqrt(var + 1e-05)


def whole(a):
    return pl.BlockSpec(a.shape, lambda *_: (0,) * a.ndim, pipeline_mode=pl.Buffered(1))


def bias_kernel(pair_ref, w_ref, out_ref):
    rows, _, _ = pair_ref.shape
    heads = w_ref.shape[1]
    wh, wl = split(w_ref[...].T)
    lhs = jnp.concatenate(
        [jnp.concatenate([wh, wh], axis=1), jnp.concatenate([wl, wl], axis=1)], axis=0
    )
    for i in range(rows):
        yh, yl = split(norm_rows(pair_ref[i]))
        r = mm_nt(lhs, jnp.concatenate([yh, yl], axis=1))
        out_ref[:, i, :] = r[:heads] + r[heads:]


def bias_tile(pair, w, step=8):
    rows, cols, cz = pair.shape
    heads = w.shape[1]
    return pl.pallas_call(
        bias_kernel,
        out_shape=jax.ShapeDtypeStruct((heads, rows, cols), F32),
        grid=(rows // step,),
        in_specs=[pl.BlockSpec((step, cols, cz), lambda i: (i, 0, 0)), whole(w)],
        out_specs=pl.BlockSpec((heads, step, cols), lambda i: (0, i, 0)),
        compiler_params=PARAMS,
        name="bias_tile",
    )(pair, w)


def project_kernel(parts, scale, x_ref, wq_ref, wk_ref, wv_ref, wg_ref, bg_ref, qkv_ref, gate_ref, w_hi, w_lo):
    ch = x_ref.shape[-1]
    own = ch // parts

    @pl.when(pl.program_id(0) == 0)
    def _():
        for t, (ref, f) in enumerate(((wq_ref, scale), (wk_ref, 1.0), (wv_ref, 1.0), (wg_ref, 1.0))):
            hi, lo = split(ref[...].T * f)
            w_hi[t * ch:(t + 1) * ch, :] = hi
            w_lo[t * ch:(t + 1) * ch, :] = lo

    yh, yl = split(norm_rows(x_ref[0]))
    r = mm_nt(w_hi[...], yh) + mm_nt(w_hi[...], yl) + mm_nt(w_lo[...], yh)
    for t in range(3):
        for n in range(parts):
            lo = t * ch + n * own
            qkv_ref[n, t, 0] = r[lo:lo + own]
    gate_ref[0] = jax.nn.sigmoid(r[3 * ch:] + bg_ref[...])


def project(x, wq, wk, wv, wg, bg, parts, head_width):
    seqs, span, ch = x.shape
    own = ch // parts
    bg = bg.reshape(ch, 1)
    return pl.pallas_call(
        functools.partial(project_kernel, parts, 1.0 / math.sqrt(head_width)),
        out_shape=(
            jax.ShapeDtypeStruct((parts, 3, seqs, own, span), F32),
            jax.ShapeDtypeStruct((seqs, ch, span), F32),
        ),
        grid=(seqs,),
        in_specs=[pl.BlockSpec((1, span, ch), lambda s: (s, 0, 0))] + [whole(a) for a in (wq, wk, wv, wg, bg)],
        out_specs=(
            pl.BlockSpec((parts, 3, 1, own, span), lambda s: (0, 0, s, 0, 0)),
            pl.BlockSpec((1, ch, span), lambda s: (s, 0, 0)),
        ),
        scratch_shapes=[pltpu.VMEM((4 * ch, ch), BF16), pltpu.VMEM((4 * ch, ch), BF16)],
        compiler_params=PARAMS,
        name="project",
    )(x, wq, wk, wv, wg, bg)


def attention_kernel(hw, q_ref, k_ref, v_ref, bias_ref, out_ref, ks, vs):
    parts = k_ref.shape[0]
    span = k_ref.shape[-1]
    s = pl.program_id(1)

    @pl.when(pl.program_id(0) == 0)
    def _():
        for n in range(parts):
            at = slice(n * span, (n + 1) * span)
            hi, lo = split(k_ref[n, 0, 0])
            ks[s, 0:hw, at] = hi
            ks[s, hw:2 * hw, at] = lo
            ks[s, 2 * hw:3 * hw, at] = hi
            v = v_ref[n, 0, 0]
            vh = v.astype(BF16).astype(F32)
            st = jnp.concatenate([vh, v - vh, jnp.ones((hw, span), F32), jnp.zeros((hw, span), F32)], axis=0)
            vs[s, at, :] = st.T.astype(BF16)

    q = q_ref[0, 0, 0]
    qh = q.astype(BF16).astype(F32)
    qst = jnp.concatenate([qh, qh, q - qh, jnp.zeros_like(q)], axis=0).T[:, :3 * hw].astype(BF16)
    bias = jnp.concatenate(
        [
            jnp.concatenate([bias_ref[w, n] for n in range(parts)], axis=1)
            for w in range(bias_ref.shape[0])
        ],
        axis=0,
    )
    scores = mm(qst, ks[s]) + bias
    top = jnp.max(scores, axis=1, keepdims=True)
    ph, plo = split(jnp.exp(scores - top))
    t = (mm(ph, vs[s]) + mm(plo, vs[s])).T
    out_ref[0, 0] = (t[0:hw] + t[hw:2 * hw]) / t[2 * hw:2 * hw + 1]


def attention(qkv, bias, head, hw):
    parts, _, seqs, _, span = qkv.shape
    _, _, rows, _ = bias.shape
    per = span // rows
    return pl.pallas_call(
        functools.partial(attention_kernel, hw),
        out_shape=jax.ShapeDtypeStruct((parts, seqs, hw, span), F32),
        grid=(parts, seqs),
        in_specs=[
            pl.BlockSpec((1, 1, 1, hw, span), lambda b, s: (b, 0, s, head, 0)),
            pl.BlockSpec((parts, 1, 1, hw, span), lambda b, s: (0, 1, s, head, 0)),
            pl.BlockSpec((parts, 1, 1, hw, span), lambda b, s: (0, 2, s, head, 0)),
            pl.BlockSpec((per, parts, rows, span), lambda b, s: (b, 0, 0, 0)),
        ],
        out_specs=pl.BlockSpec((1, 1, hw, span), lambda b, s: (b, s, 0, 0)),
        scratch_shapes=[
            pltpu.VMEM((seqs, 3 * hw, parts * span), BF16),
            pltpu.VMEM((seqs, parts * span, 4 * hw), BF16),
        ],
        compiler_params=PARAMS,
        name="attention",
    )(qkv, qkv, qkv, bias)


def merge_kernel(*refs):
    heads = len(refs) - 12
    att = refs[:heads]
    gate_ref, x_ref, wm_ref, bm_ref, f1_ref, f2_ref, next_ref, left_ref, right_ref, m_hi, m_lo, f_st = refs[heads:]
    parts, _, _, _ = att[0].shape
    hid = f1_ref.shape[1]
    blocks, _, _, rows = left_ref.shape

    @pl.when(pl.program_id(0) == 0)
    def _():
        hi, lo = split(wm_ref[...])
        m_hi[...] = hi
        m_lo[...] = lo
        hi, lo = split(jnp.concatenate([f1_ref[...], f2_ref[...]], axis=1).T)
        f_st[0:2 * hid, :] = hi
        f_st[2 * hid:4 * hid, :] = lo

    a = jnp.concatenate([att[h][n, 0] for n in range(parts) for h in range(heads)], axis=0)
    ah, al = split((a * gate_ref[0]).T)
    y = x_ref[0] + (mm(ah, m_hi[...]) + mm(al, m_hi[...]) + mm(ah, m_lo[...])) + bm_ref[...]
    next_ref[0] = y
    zh, zl = split(norm_rows(y))
    p = mm_nt(f_st[...], zh)
    p = p[:2 * hid] + p[2 * hid:] + mm_nt(f_st[0:2 * hid, :], zl)
    for b in range(blocks):
        left_ref[b, 0] = p[:hid, b * rows:(b + 1) * rows]
    right_ref[0] = p[hid:]


def merge(att, gate, x, wm, bm, f1, f2, rows):
    seqs, span, ch = x.shape
    parts, _, hw, _ = att[0].shape
    hid = f1.shape[1]
    bm = bm.reshape(1, ch)
    blocks = span // rows
    return pl.pallas_call(
        merge_kernel,
        out_shape=(
            jax.ShapeDtypeStruct(x.shape, F32),
            jax.ShapeDtypeStruct((blocks, seqs, hid, rows), F32),
            jax.ShapeDtypeStruct((seqs, hid, span), F32),
        ),
        grid=(seqs,),
        in_specs=[pl.BlockSpec((parts, 1, hw, span), lambda s: (0, s, 0, 0)) for _ in att]
        + [
            pl.BlockSpec((1, ch, span), lambda s: (s, 0, 0)),
            pl.BlockSpec((1, span, ch), lambda s: (s, 0, 0)),
        ]
        + [whole(a) for a in (wm, bm, f1, f2)],
        out_specs=(
            pl.BlockSpec((1, span, ch), lambda s: (s, 0, 0)),
            pl.BlockSpec((blocks, 1, hid, rows), lambda s: (0, s, 0, 0)),
            pl.BlockSpec((1, hid, span), lambda s: (s, 0, 0)),
        ),
        scratch_shapes=[
            pltpu.VMEM((ch, ch), BF16),
            pltpu.VMEM((ch, ch), BF16),
            pltpu.VMEM((4 * hid, ch), BF16),
        ],
        compiler_params=PARAMS,
        name="merge",
    )(*att, gate, x, wm, bm, f1, f2)


def pair_rows(
    step_rows, group, seqs, first, left_ref, pair_ref, ob_ref, eb_ref, out_ref, r_hi, r_lo, w_st, up_st, dn_st
):
    _, cols, cz = pair_ref.shape
    d_n = w_st.shape[1] // cz

    def body(p, carry):
        lrow = left_ref[pl.ds(pl.multiple_of((first + p * group) * seqs, group * seqs), group * seqs), :]
        lhi = lrow.astype(BF16).astype(F32)
        u = mm(jnp.concatenate([lhi, lhi, lrow - lhi], axis=1).astype(BF16), w_st[...])
        his, los = [], []
        for q in range(group):
            sub = u[q * seqs:(q + 1) * seqs, :]
            hi, lo = split(jnp.concatenate([sub[:, d * cz:(d + 1) * cz] for d in range(d_n)], axis=0))
            his.append(hi)
            los.append(lo)
        mids = []
        for q in range(0, group, 2):
            cross = mm(r_lo[...], jnp.concatenate(his[q:q + 2], axis=1))
            for i in range(2):
                a = mm(r_hi[...], jnp.concatenate([his[q + i], los[q + i]], axis=1))
                o = a[:, :cz] + a[:, cz:] + cross[:, i * cz:(i + 1) * cz]
                mids.append(pair_ref[group * p + q + i] + o / seqs + ob_ref[...])
        for q in range(0, group, 2):
            mid = jnp.concatenate(mids[q:q + 2], axis=0)
            yh, yl = split(norm_rows(mid))
            h = mm(jnp.concatenate([yh, yl, yh], axis=1), up_st[...])
            hh, hl = split(jnp.maximum(h + eb_ref[...], 0.0))
            a = mm(hh, dn_st[...])
            o = mid + (a[:, :cz] + a[:, cz:] + mm(hl, dn_st[:, 0:cz]))
            for i in range(2):
                out_ref[group * p + q + i] = o[i * cols:(i + 1) * cols]
        return carry

    lax.fori_loop(0, step_rows // group, body, 0)


def pair_weights(w_ref, up_ref, dn_ref, w_st, up_st, dn_st):
    c_n = w_ref.shape[0]
    cz = up_ref.shape[0]
    hi, lo = split(w_ref[...])
    w_st[0:c_n, :] = hi
    w_st[c_n:2 * c_n, :] = lo
    w_st[2 * c_n:3 * c_n, :] = hi
    hi, lo = split(up_ref[...])
    up_st[0:cz, :] = hi
    up_st[cz:2 * cz, :] = hi
    up_st[2 * cz:3 * cz, :] = lo
    hi, lo = split(dn_ref[...])
    dn_st[:, 0:cz] = hi
    dn_st[:, cz:2 * cz] = lo


def pair_kernel(
    step_rows, group, seqs, left_ref, right_ref, w_ref, pair_ref, ob_ref, up_ref, eb_ref, dn_ref,
    out_ref, r_hi, r_lo, w_st, up_st, dn_st,
):
    @pl.when(pl.program_id(0) == 0)
    def _():
        r_hi[...], r_lo[...] = split(right_ref[...])
        pair_weights(w_ref, up_ref, dn_ref, w_st, up_st, dn_st)

    pair_rows(
        step_rows, group, seqs, 0, left_ref, pair_ref, ob_ref, eb_ref, out_ref, r_hi, r_lo, w_st, up_st, dn_st
    )


def pair_update(left_rows, right_cols, w2, pair, ob, up, eb, dn, step_rows=8, group=4):
    rows, cols, cz = pair.shape
    seqs = left_rows.shape[0] // rows
    c_n = w2.shape[0]
    ob = ob.reshape(1, -1)
    eb = eb.reshape(1, -1)
    return pl.pallas_call(
        functools.partial(pair_kernel, step_rows, group, seqs),
        out_shape=jax.ShapeDtypeStruct(pair.shape, F32),
        grid=(rows // step_rows,),
        in_specs=[
            pl.BlockSpec((step_rows * seqs, left_rows.shape[1]), lambda i: (i, 0)),
            whole(right_cols), whole(w2),
            pl.BlockSpec((step_rows, cols, cz), lambda i: (i, 0, 0)),
            whole(ob), whole(up), whole(eb), whole(dn),
        ],
        out_specs=pl.BlockSpec((step_rows, cols, cz), lambda i: (i, 0, 0)),
        scratch_shapes=[
            pltpu.VMEM(right_cols.shape, BF16),
            pltpu.VMEM(right_cols.shape, BF16),
            pltpu.VMEM((3 * c_n, w2.shape[1]), BF16),
            pltpu.VMEM((3 * cz, up.shape[1]), BF16),
            pltpu.VMEM((up.shape[1], 2 * cz), BF16),
        ],
        compiler_params=PARAMS,
        name="pair_update",
    )(left_rows, right_cols, w2, pair, ob, up, eb, dn)


def spread_heads(
    parts,
    homolog_embedding,
    pair_state,
    probe_projector,
    lookup_projector,
    content_projector,
    sigmoid_projector,
    sigmoid_offset,
    pair_bias_weight,
    mixing_projector,
    mixing_offset,
    first_factor_projector,
    second_factor_projector,
    outer_product_weight,
    outer_product_bias,
    up_weight,
    expand_bias,
    down_weight,
):
    _, _, ch = homolog_embedding.shape
    rows, cols, cz = pair_state.shape
    heads = pair_bias_weight.shape[1]
    hw = ch // heads
    own_heads = heads // parts
    hid = first_factor_projector.shape[1]

    bias = bias_tile(pair_state, pair_bias_weight).reshape(parts, own_heads, rows, cols)
    bias = lax.all_to_all(bias, "narrow", 0, 0, tiled=True)
    gathered = [
        lax.all_gather(bias[:, h], "wide", axis=0, tiled=False) for h in range(own_heads)
    ]
    qkv, gate = project(
        homolog_embedding, probe_projector, lookup_projector, content_projector, sigmoid_projector,
        sigmoid_offset, parts, hw,
    )
    qkv = lax.all_to_all(qkv, "narrow", 0, 0, tiled=True)
    att = [
        lax.all_to_all(attention(qkv, gathered[h], h, hw), "narrow", 0, 0, tiled=True)
        for h in range(own_heads)
    ]
    alignment_state_next, left, right = merge(
        att, gate, homolog_embedding, mixing_projector, mixing_offset,
        first_factor_projector, second_factor_projector, rows,
    )
    left = lax.all_gather(left, "narrow", axis=0, tiled=True)
    left = lax.all_to_all(left, "wide", 0, 0, tiled=True)
    right = lax.all_gather(right, "wide", axis=0, tiled=True)
    left = left.reshape(-1, hid, rows)
    all_seqs = left.shape[0]
    left_rows = jnp.transpose(left, (2, 0, 1)).reshape(rows * all_seqs, hid)
    right_cols = jnp.transpose(right, (2, 1, 0)).reshape(cols, hid * all_seqs)
    pair_state_next = pair_update(
        left_rows, right_cols, outer_product_weight.reshape(hid, hid * cz), pair_state,
        outer_product_bias, up_weight, expand_bias, down_weight,
    )
    return (alignment_state_next, pair_state_next)


AXES = ("wide", "narrow")
PLANES, CORES = 4, 2
PARTNER = {1: 2, 2: 1}
OUTWARD = {1: 0, 2: 3}
ORDER = ((0, 1, 2, 3), (1, 0, 2, 3), (2, 3, 1, 0), (3, 2, 1, 0))


def send(x, parts, route):
    pairs = []
    for z in range(PLANES):
        for c in range(CORES):
            for n in range(parts):
                to = route(z, c, n)
                if to is not None:
                    pairs.append(((z * CORES + c) * parts + n, (to[0] * CORES + to[1]) * parts + to[2]))
    return lax.ppermute(x, AXES, pairs)


def exchange(blocks, parts):
    out = [blocks[0]]
    for k in range(1, len(blocks)):
        dn, dc = divmod(k, CORES)
        out.append(send(blocks[k], parts, lambda z, c, n: (z, c ^ dc, n ^ dn)))
    return out


def line_gather(x, parts):
    middle = lambda table: lambda z, c, n: (table[z], c, n) if z in table else None
    near = send(x, parts, lambda z, c, n: (z ^ 1, c, n))
    across = send(x, parts, middle(PARTNER))
    out2 = send(across, parts, middle(OUTWARD))
    far = send(near, parts, middle(PARTNER))
    out3 = send(far, parts, middle(OUTWARD))
    return near, (across, out2), (far, out3)


def own_head(ids_ref):
    return ids_ref[1] * CORES + ids_ref[0] % CORES


def head_bias_kernel(group, ids_ref, pair_ref, w_ref, *refs):
    out_refs, lhs = refs[:-1], refs[-1]
    rows, cols, cz = pair_ref.shape
    heads = w_ref.shape[0]

    @pl.when(pl.program_id(0) == 0)
    def _():
        me = own_head(ids_ref)
        own = jnp.concatenate([w_ref[pl.ds(me ^ k, 1), :] for k in range(heads)], axis=0)
        hi = own.astype(BF16).astype(F32)
        both = jnp.concatenate([hi, own - hi], axis=0)
        lhs[...] = jnp.concatenate([both, both], axis=1).astype(BF16)

    for i in range(0, rows, group):
        yh, yl = split(norm_rows(pair_ref[i:i + group].reshape(group * cols, cz)))
        r = mm_nt(lhs[...], jnp.concatenate([yh, yl], axis=1))
        r = r[:heads] + r[heads:]
        for g in range(group):
            for k in range(heads):
                out_refs[k][i + g:i + g + 1, :] = r[k:k + 1, g * cols:(g + 1) * cols]


def head_bias(ids, pair, w, step=32, group=4):
    rows, cols, cz = pair.shape
    heads = w.shape[0]
    return pl.pallas_call(
        functools.partial(head_bias_kernel, group),
        out_shape=(jax.ShapeDtypeStruct((rows, cols), F32),) * heads,
        grid_spec=pltpu.PrefetchScalarGridSpec(
            num_scalar_prefetch=1,
            grid=(rows // step,),
            in_specs=[pl.BlockSpec((step, cols, cz), lambda i, _: (i, 0, 0)), whole(w)],
            out_specs=(pl.BlockSpec((step, cols), lambda i, _: (i, 0)),) * heads,
            scratch_shapes=[pltpu.VMEM((2 * heads, 2 * cz), BF16)],
        ),
        compiler_params=PARAMS,
        name="head_bias",
    )(ids, pair, w)


def head_project_kernel(heads, scale, ids_ref, x_ref, wq_ref, wk_ref, wv_ref, wg_ref, bg_ref, *refs):
    qkv_refs, (gate_ref, w_t, b_p, w_hi, w_lo) = refs[:heads], refs[heads:]
    ch = x_ref.shape[-1]
    hw = ch // heads

    @pl.when(pl.program_id(0) == 0)
    def _():
        me = own_head(ids_ref)
        for t, (ref, f) in enumerate(((wq_ref, scale), (wk_ref, 1.0), (wv_ref, 1.0), (wg_ref, 1.0))):
            w_t[...] = ref[...].T * f
            for k in range(heads):
                src = pl.ds(pl.multiple_of((me ^ k) * hw, hw), hw)
                hi, lo = split(w_t[src, :])
                at = slice(t * ch + k * hw, t * ch + (k + 1) * hw)
                w_hi[at, :] = hi
                w_lo[at, :] = lo
                if t == 3:
                    b_p[k * hw:(k + 1) * hw, :] = bg_ref[src, :]

    yh, yl = split(norm_rows(x_ref[0]))
    r = mm_nt(w_hi[...], yh) + mm_nt(w_hi[...], yl) + mm_nt(w_lo[...], yh)
    for t in range(3):
        for k in range(heads):
            lo = t * ch + k * hw
            qkv_refs[k][t, 0] = r[lo:lo + hw]
    gate_ref[0] = jax.nn.sigmoid(r[3 * ch:] + b_p[...])


def head_project(me, x, wq, wk, wv, wg, bg, heads):
    seqs, span, ch = x.shape
    hw = ch // heads
    bg = bg.reshape(ch, 1)
    return pl.pallas_call(
        functools.partial(head_project_kernel, heads, 1.0 / math.sqrt(hw)),
        out_shape=(jax.ShapeDtypeStruct((3, seqs, hw, span), F32),) * heads
        + (jax.ShapeDtypeStruct((seqs, ch, span), F32),),
        grid_spec=pltpu.PrefetchScalarGridSpec(
            num_scalar_prefetch=1,
            grid=(seqs,),
            in_specs=[pl.BlockSpec((1, span, ch), lambda s, _: (s, 0, 0))]
            + [whole(a) for a in (wq, wk, wv, wg, bg)],
            out_specs=(pl.BlockSpec((3, 1, hw, span), lambda s, _: (0, s, 0, 0)),) * heads
            + (pl.BlockSpec((1, ch, span), lambda s, _: (s, 0, 0)),),
            scratch_shapes=[
                pltpu.VMEM((ch, ch), F32),
                pltpu.VMEM((ch, 1), F32),
                pltpu.VMEM((4 * ch, ch), BF16),
                pltpu.VMEM((4 * ch, ch), BF16),
            ],
        ),
        compiler_params=PARAMS,
        name="head_project",
    )(me, x, wq, wk, wv, wg, bg)


def stage_kernel(n_ref, *refs):
    pieces, (q_ref, k_ref, v_ref) = refs[:-3], refs[-3:]
    _, _, hw, span = pieces[0].shape
    for p, ref in enumerate(pieces):
        part, core = divmod(p, CORES)
        at = slice(part * span, (part + 1) * span)
        q = ref[0, 0]
        qh = q.astype(BF16).astype(F32)
        q_ref[core, 0, (n_ref[0] - 1) ^ part] = (
            jnp.concatenate([qh, qh, q - qh, jnp.zeros_like(q)], axis=0).T.astype(BF16)
        )
        hi, lo = split(ref[1, 0])
        k_ref[core, 0, 0:hw, at] = hi
        k_ref[core, 0, hw:2 * hw, at] = lo
        k_ref[core, 0, 2 * hw:3 * hw, at] = hi
        k_ref[core, 0, 3 * hw:4 * hw, at] = jnp.zeros_like(hi)
        v = ref[2, 0]
        vh = v.astype(BF16).astype(F32)
        st = jnp.concatenate([vh, v - vh, jnp.ones((hw, span), F32), jnp.zeros((hw, span), F32)], axis=0)
        v_ref[core, 0, at, :] = st.T.astype(BF16)


def stage(n, pieces, parts):
    _, seqs, hw, span = pieces[0].shape
    return pl.pallas_call(
        stage_kernel,
        out_shape=(
            jax.ShapeDtypeStruct((CORES, seqs, parts, span, 4 * hw), BF16),
            jax.ShapeDtypeStruct((CORES, seqs, 4 * hw, parts * span), BF16),
            jax.ShapeDtypeStruct((CORES, seqs, parts * span, 4 * hw), BF16),
        ),
        grid_spec=pltpu.PrefetchScalarGridSpec(
            num_scalar_prefetch=1,
            grid=(seqs,),
            in_specs=[pl.BlockSpec((3, 1, hw, span), lambda s, _: (0, s, 0, 0)) for _ in pieces],
            out_specs=(
                pl.BlockSpec((CORES, 1, parts, span, 4 * hw), lambda s, _: (0, s, 0, 0, 0)),
                pl.BlockSpec((CORES, 1, 4 * hw, parts * span), lambda s, _: (0, s, 0, 0)),
                pl.BlockSpec((CORES, 1, parts * span, 4 * hw), lambda s, _: (0, s, 0, 0)),
            ),
        ),
        compiler_params=PARAMS,
        name="stage",
    )(n, *pieces)


def head_attention_kernel(hw, turn, tiles, at_ref, q_ref, k_ref, v_ref, *refs):
    bias_refs, out_ref = refs[:tiles], refs[-1]
    parts = bias_refs[0].shape[1]
    cores, seqs = q_ref.shape[:2]
    core = at_ref[3 * turn + 2]
    bias = jnp.concatenate(
        [
            jnp.concatenate([sum(b[h ^ core, n] for b in bias_refs) for n in range(parts)], axis=1)
            for h in range(CORES)
        ],
        axis=0,
    )
    score = lambda g, s: mm(q_ref[g, s, 0], k_ref[g, s]) + bias
    items = [(g, s) for s in range(seqs) for g in range(cores)]
    ahead = score(*items[0])
    for i, (g, s) in enumerate(items):
        scores = ahead
        if i + 1 < len(items):
            ahead = score(*items[i + 1])
        top = jnp.max(scores, axis=1, keepdims=True)
        ph, plo = split(jnp.exp(scores - top))
        t = (mm(ph, v_ref[g, s]) + mm(plo, v_ref[g, s])).T
        out_ref[0, g, s] = (t[0:hw] + t[hw:2 * hw]) / t[2 * hw:2 * hw + 1]


def head_attention(at, turn, q, k, v, tiles, prev, hw, step=2):
    cores, seqs, parts, span, _ = q.shape
    before = () if prev is None else (prev,)
    return pl.pallas_call(
        functools.partial(head_attention_kernel, hw, turn, len(tiles)),
        out_shape=jax.ShapeDtypeStruct((parts, cores, seqs, hw, span), F32),
        grid_spec=pltpu.PrefetchScalarGridSpec(
            num_scalar_prefetch=1,
            grid=(seqs // step,),
            in_specs=[
                pl.BlockSpec((cores, step, 1, span, 4 * hw), lambda s, at: (0, s, at[3 * turn], 0, 0)),
                pl.BlockSpec((cores, step, 4 * hw, parts * span), lambda s, at: (0, s, 0, 0)),
                pl.BlockSpec((cores, step, parts * span, 4 * hw), lambda s, at: (0, s, 0, 0)),
            ]
            + [whole(b) for b in tiles]
            + [pl.BlockSpec(memory_space=pl.ANY) for _ in before],
            out_specs=pl.BlockSpec((1, cores, step, hw, span), lambda s, at: (at[3 * turn + 1], 0, s, 0, 0)),
        ),
        input_output_aliases={4 + len(tiles): 0} if before else {},
        compiler_params=PARAMS,
        name="head_attention",
    )(at, q, k, v, *tiles, *before)


def head_merge_kernel(heads, ids_ref, *refs):
    pieces = refs[:heads]
    gate_ref, x_ref, wm_ref, bm_ref, f1_ref, f2_ref = refs[heads:heads + 6]
    next_ref, left_a, left_b, right_ref, m_hi, m_lo, f_st = refs[heads + 6:]
    _, hw, span = pieces[0].shape
    hid = f1_ref.shape[0]
    rows = span // CORES

    @pl.when(pl.program_id(0) == 0)
    def _():
        for k in range(heads):
            hi, lo = split(wm_ref[pl.ds(pl.multiple_of((own_head(ids_ref) ^ k) * hw, hw), hw), :])
            m_hi[k * hw:(k + 1) * hw, :] = hi
            m_lo[k * hw:(k + 1) * hw, :] = lo
        hi, lo = split(jnp.concatenate([f1_ref[...], f2_ref[...]], axis=0))
        f_st[0:2 * hid, :] = hi
        f_st[2 * hid:4 * hid, :] = lo

    swap = ids_ref[0] % CORES == 1
    for s in range(x_ref.shape[0]):
        a = jnp.concatenate([p[s] for p in pieces], axis=0)
        ah, al = split((a * gate_ref[s]).T)
        y = x_ref[s] + (mm(ah, m_hi[...]) + mm(al, m_hi[...]) + mm(ah, m_lo[...])) + bm_ref[...]
        next_ref[s] = y
        zh, zl = split(norm_rows(y))
        p = mm_nt(f_st[...], zh)
        p = p[:2 * hid] + p[2 * hid:] + mm_nt(f_st[0:2 * hid, :], zl)
        left_a[s] = jnp.where(swap, p[:hid, rows:], p[:hid, :rows])
        left_b[s] = jnp.where(swap, p[:hid, :rows], p[:hid, rows:])
        right_ref[s] = p[hid:]


def head_merge(me, pieces, gate, x, wm, bm, f1, f2, step=2):
    seqs, span, ch = x.shape
    heads = len(pieces)
    hw = ch // heads
    hid = f1.shape[0]
    rows = span // CORES
    bm = bm.reshape(1, ch)
    return pl.pallas_call(
        functools.partial(head_merge_kernel, heads),
        out_shape=(jax.ShapeDtypeStruct(x.shape, F32),)
        + (jax.ShapeDtypeStruct((seqs, hid, rows), F32),) * CORES
        + (jax.ShapeDtypeStruct((seqs, hid, span), F32),),
        grid_spec=pltpu.PrefetchScalarGridSpec(
            num_scalar_prefetch=1,
            grid=(seqs // step,),
            in_specs=[pl.BlockSpec((step, hw, span), lambda s, _: (s, 0, 0)) for _ in pieces]
            + [
                pl.BlockSpec((step, ch, span), lambda s, _: (s, 0, 0)),
                pl.BlockSpec((step, span, ch), lambda s, _: (s, 0, 0)),
            ]
            + [whole(a) for a in (wm, bm, f1, f2)],
            out_specs=(
                pl.BlockSpec((step, span, ch), lambda s, _: (s, 0, 0)),
                pl.BlockSpec((step, hid, rows), lambda s, _: (s, 0, 0)),
                pl.BlockSpec((step, hid, rows), lambda s, _: (s, 0, 0)),
                pl.BlockSpec((step, hid, span), lambda s, _: (s, 0, 0)),
            ),
            scratch_shapes=[
                pltpu.VMEM((ch, ch), BF16),
                pltpu.VMEM((ch, ch), BF16),
                pltpu.VMEM((4 * hid, ch), BF16),
            ],
        ),
        compiler_params=PARAMS,
        name="head_merge",
    )(me, *pieces, gate, x, wm, bm, f1, f2)


def packed_pair_kernel(step_rows, group, lefts, slots_ref, *refs):
    left_refs, (own_ref, sib_ref, w_ref, pair_ref, ob_ref, up_ref, eb_ref, dn_ref) = refs[:lefts], refs[lefts:lefts + 8]
    out_ref, r_hi, r_lo, w_st, up_st, dn_st, left, right = refs[lefts + 8:]
    cores, seqs, hid, rows = left_refs[0].shape
    total = lefts * cores * seqs

    @pl.when(pl.program_id(0) == 0)
    def _():
        pair_weights(w_ref, up_ref, dn_ref, w_st, up_st, dn_st)
        for i in range(own_ref.shape[0]):
            at = slots_ref[i] * cores
            for t, ref in enumerate((own_ref, sib_ref)):
                right[pl.ds((at + t) * seqs, seqs)] = ref[i]
        r_hi[...], r_lo[...] = split(jnp.concatenate([right[:, d, :] for d in range(hid)], axis=0).T)
        for p, ref in enumerate(left_refs):
            for t in range(cores):
                for s in range(seqs):
                    at = (p * cores + t) * seqs + s
                    left[pl.ds(at, rows, stride=total), :] = ref[t, s].T

    pair_rows(
        step_rows, group, total, pl.program_id(0) * step_rows, left, pair_ref, ob_ref, eb_ref, out_ref,
        r_hi, r_lo, w_st, up_st, dn_st,
    )


def packed_pair_update(slots, lefts, own, sib, w2, pair, ob, up, eb, dn, step_rows=8, group=4):
    rows, cols, cz = pair.shape
    cores, seqs, hid, _ = lefts[0].shape
    total = len(lefts) * cores * seqs
    ob = ob.reshape(1, -1)
    eb = eb.reshape(1, -1)
    tile = pl.BlockSpec((step_rows, cols, cz), lambda i, _: (i, 0, 0))
    return pl.pallas_call(
        functools.partial(packed_pair_kernel, step_rows, group, len(lefts)),
        out_shape=jax.ShapeDtypeStruct(pair.shape, F32),
        grid_spec=pltpu.PrefetchScalarGridSpec(
            num_scalar_prefetch=1,
            grid=(rows // step_rows,),
            in_specs=[whole(a) for a in (*lefts, own, sib, w2)] + [tile] + [whole(a) for a in (ob, up, eb, dn)],
            out_specs=tile,
            scratch_shapes=[
                pltpu.VMEM((cols, hid * total), BF16),
                pltpu.VMEM((cols, hid * total), BF16),
                pltpu.VMEM((3 * hid, w2.shape[1]), BF16),
                pltpu.VMEM((3 * cz, up.shape[1]), BF16),
                pltpu.VMEM((up.shape[1], 2 * cz), BF16),
                pltpu.VMEM((rows * total, hid), F32),
                pltpu.VMEM((total, hid, cols), F32),
            ],
        ),
        compiler_params=PARAMS,
        name="packed_pair_update",
    )(slots, *lefts, own, sib, w2, pair, ob, up, eb, dn)


def after(x, *deps):
    return lax.optimization_barrier((x, deps))[0]


def per_head(
    parts,
    homolog_embedding,
    pair_state,
    probe_projector,
    lookup_projector,
    content_projector,
    sigmoid_projector,
    sigmoid_offset,
    pair_bias_weight,
    mixing_projector,
    mixing_offset,
    first_factor_projector,
    second_factor_projector,
    outer_product_weight,
    outer_product_bias,
    up_weight,
    expand_bias,
    down_weight,
):
    _, _, ch = homolog_embedding.shape
    _, _, cz = pair_state.shape
    heads = pair_bias_weight.shape[1]
    hw = ch // heads
    hid = first_factor_projector.shape[1]
    ids = jnp.stack([lax.axis_index("wide"), lax.axis_index("narrow")])
    tiles = head_bias(ids, pair_state, pair_bias_weight.T)
    late = after(ids, tiles[0])
    z, c, n = late[0] // CORES, late[0] % CORES, late[1]
    order = jnp.asarray(ORDER, jnp.int32)[z]
    at = jnp.stack([order, order ^ n, jnp.full_like(order, c)], axis=1).reshape(-1)
    slots = (jnp.arange(PLANES, dtype=jnp.int32) ^ z) ^ n
    *qkv, gate = head_project(
        ids, after(homolog_embedding, tiles[0], at, slots), probe_projector, lookup_projector, content_projector,
        sigmoid_projector, sigmoid_offset, heads,
    )
    tiles = after(exchange(tiles, parts), gate)
    bias = jnp.stack(
        [jnp.stack([tiles[p * CORES + r] for p in range(parts)]) for r in range(CORES)]
    )
    near, second, third = line_gather(bias, parts)
    qkv = exchange(after(qkv, bias), parts)
    marked = after(n[None], near, second[0]) + 1
    q, k, v = stage(marked, after(qkv, near, second[0]), parts)
    bias = after(bias, third[0])
    att = None
    for i, tile in enumerate(((bias,), (near,), second, third)):
        att = head_attention(at, i, q, k, v, tile, att, hw)
    pieces = exchange([att[p, r] for p in range(parts) for r in range(CORES)], parts)
    alignment_state_next, left_a, left_b, right = head_merge(
        ids, pieces, gate, homolog_embedding, mixing_projector, mixing_offset,
        first_factor_projector.T, second_factor_projector.T,
    )
    turn = lambda z0, c0, n0: (n0, c0, z0)
    left_b, left_a = send(left_b, parts, turn), send(left_a, parts, turn)
    sibling = lambda z0, c0, n0: (z0, c0 ^ 1, n0)
    left_b = send(left_b, parts, sibling)
    left = jnp.stack([left_a, left_b])
    rights = [right] + [send(right, parts, lambda z0, c0, n0, d=d: (z0 ^ d, c0, n0)) for d in range(1, PLANES)]
    lefts = [left] + [send(left, parts, lambda z0, c0, n0, d=d: (z0, c0, n0 ^ d)) for d in range(1, parts)]
    own = jnp.stack(rights)
    pair_state_next = packed_pair_update(
        slots, lefts, own, send(own, parts, sibling),
        outer_product_weight.reshape(hid, hid * cz), pair_state,
        outer_product_bias, up_weight, expand_bias, down_weight,
    )
    return (alignment_state_next, pair_state_next)


def lines(mesh):
    return mesh.shape["wide"] == PLANES * CORES and mesh.shape["narrow"] == PLANES


def step(mesh, *args):
    parts = mesh.shape["narrow"]
    heads = args[7].shape[1]
    if lines(mesh) and heads == CORES * parts:
        return per_head(parts, *args)
    return spread_heads(parts, *args)


def solution(mesh):
    placed = (P("wide", "narrow", None), P("wide", "narrow", None)) + (P(),) * 15
    return jax.shard_map(
        functools.partial(step, mesh),
        mesh=mesh,
        in_specs=placed,
        out_specs=(P("wide", "narrow", None), P("wide", "narrow", None)),
        check_vma=False,
    )
```

```python
import functools
import math

import jax
import jax.numpy as jnp
from jax import lax
from jax.experimental import pallas as pl
from jax.experimental.pallas import tpu as pltpu
from jax.sharding import PartitionSpec as P


F32, BF16 = jnp.float32, jnp.bfloat16
PARAMS = pltpu.CompilerParams(vmem_limit_bytes=60 * 2**20)


def split(x):
    hi = x.astype(BF16)
    lo = (x - hi.astype(F32)).astype(BF16)
    return hi, lo


def mm(a, b):
    return jnp.dot(a, b, preferred_element_type=F32)


def mm_nt(a, b):
    return lax.dot_general(a, b, (((1,), (1,)), ((), ())), preferred_element_type=F32)


def norm_rows(x):
    mean = jnp.mean(x, axis=-1, keepdims=True)
    c = x - mean
    var = jnp.mean(c * c, axis=-1, keepdims=True)
    return c * lax.rsqrt(var + 1e-05)


def whole(a):
    return pl.BlockSpec(a.shape, lambda *_: (0,) * a.ndim, pipeline_mode=pl.Buffered(1))


def bias_kernel(pair_ref, w_ref, out_ref):
    rows, _, _ = pair_ref.shape
    heads = w_ref.shape[1]
    wh, wl = split(w_ref[...].T)
    lhs = jnp.concatenate(
        [jnp.concatenate([wh, wh], axis=1), jnp.concatenate([wl, wl], axis=1)], axis=0
    )
    for i in range(rows):
        yh, yl = split(norm_rows(pair_ref[i]))
        r = mm_nt(lhs, jnp.concatenate([yh, yl], axis=1))
        out_ref[:, i, :] = r[:heads] + r[heads:]


def bias_tile(pair, w, step=8):
    rows, cols, cz = pair.shape
    heads = w.shape[1]
    return pl.pallas_call(
        bias_kernel,
        out_shape=jax.ShapeDtypeStruct((heads, rows, cols), F32),
        grid=(rows // step,),
        in_specs=[pl.BlockSpec((step, cols, cz), lambda i: (i, 0, 0)), whole(w)],
        out_specs=pl.BlockSpec((heads, step, cols), lambda i: (0, i, 0)),
        compiler_params=PARAMS,
        name="bias_tile",
    )(pair, w)


def project_kernel(parts, scale, x_ref, wq_ref, wk_ref, wv_ref, wg_ref, bg_ref, qkv_ref, gate_ref, w_hi, w_lo):
    ch = x_ref.shape[-1]
    own = ch // parts

    @pl.when(pl.program_id(0) == 0)
    def _():
        for t, (ref, f) in enumerate(((wq_ref, scale), (wk_ref, 1.0), (wv_ref, 1.0), (wg_ref, 1.0))):
            hi, lo = split(ref[...].T * f)
            w_hi[t * ch:(t + 1) * ch, :] = hi
            w_lo[t * ch:(t + 1) * ch, :] = lo

    yh, yl = split(norm_rows(x_ref[0]))
    r = mm_nt(w_hi[...], yh) + mm_nt(w_hi[...], yl) + mm_nt(w_lo[...], yh)
    for t in range(3):
        for n in range(parts):
            lo = t * ch + n * own
            qkv_ref[n, t, 0] = r[lo:lo + own]
    gate_ref[0] = jax.nn.sigmoid(r[3 * ch:] + bg_ref[...])


def project(x, wq, wk, wv, wg, bg, parts, head_width):
    seqs, span, ch = x.shape
    own = ch // parts
    bg = bg.reshape(ch, 1)
    return pl.pallas_call(
        functools.partial(project_kernel, parts, 1.0 / math.sqrt(head_width)),
        out_shape=(
            jax.ShapeDtypeStruct((parts, 3, seqs, own, span), F32),
            jax.ShapeDtypeStruct((seqs, ch, span), F32),
        ),
        grid=(seqs,),
        in_specs=[pl.BlockSpec((1, span, ch), lambda s: (s, 0, 0))] + [whole(a) for a in (wq, wk, wv, wg, bg)],
        out_specs=(
            pl.BlockSpec((parts, 3, 1, own, span), lambda s: (0, 0, s, 0, 0)),
            pl.BlockSpec((1, ch, span), lambda s: (s, 0, 0)),
        ),
        scratch_shapes=[pltpu.VMEM((4 * ch, ch), BF16), pltpu.VMEM((4 * ch, ch), BF16)],
        compiler_params=PARAMS,
        name="project",
    )(x, wq, wk, wv, wg, bg)


def attention_kernel(hw, q_ref, k_ref, v_ref, bias_ref, out_ref, ks, vs):
    parts = k_ref.shape[0]
    span = k_ref.shape[-1]
    s = pl.program_id(1)

    @pl.when(pl.program_id(0) == 0)
    def _():
        for n in range(parts):
            at = slice(n * span, (n + 1) * span)
            hi, lo = split(k_ref[n, 0, 0])
            ks[s, 0:hw, at] = hi
            ks[s, hw:2 * hw, at] = lo
            ks[s, 2 * hw:3 * hw, at] = hi
            v = v_ref[n, 0, 0]
            vh = v.astype(BF16).astype(F32)
            st = jnp.concatenate([vh, v - vh, jnp.ones((hw, span), F32), jnp.zeros((hw, span), F32)], axis=0)
            vs[s, at, :] = st.T.astype(BF16)

    q = q_ref[0, 0, 0]
    qh = q.astype(BF16).astype(F32)
    qst = jnp.concatenate([qh, qh, q - qh, jnp.zeros_like(q)], axis=0).T[:, :3 * hw].astype(BF16)
    bias = jnp.concatenate(
        [
            jnp.concatenate([bias_ref[w, n] for n in range(parts)], axis=1)
            for w in range(bias_ref.shape[0])
        ],
        axis=0,
    )
    scores = mm(qst, ks[s]) + bias
    top = jnp.max(scores, axis=1, keepdims=True)
    ph, plo = split(jnp.exp(scores - top))
    t = (mm(ph, vs[s]) + mm(plo, vs[s])).T
    out_ref[0, 0] = (t[0:hw] + t[hw:2 * hw]) / t[2 * hw:2 * hw + 1]


def attention(qkv, bias, head, hw):
    parts, _, seqs, _, span = qkv.shape
    _, _, rows, _ = bias.shape
    per = span // rows
    return pl.pallas_call(
        functools.partial(attention_kernel, hw),
        out_shape=jax.ShapeDtypeStruct((parts, seqs, hw, span), F32),
        grid=(parts, seqs),
        in_specs=[
            pl.BlockSpec((1, 1, 1, hw, span), lambda b, s: (b, 0, s, head, 0)),
            pl.BlockSpec((parts, 1, 1, hw, span), lambda b, s: (0, 1, s, head, 0)),
            pl.BlockSpec((parts, 1, 1, hw, span), lambda b, s: (0, 2, s, head, 0)),
            pl.BlockSpec((per, parts, rows, span), lambda b, s: (b, 0, 0, 0)),
        ],
        out_specs=pl.BlockSpec((1, 1, hw, span), lambda b, s: (b, s, 0, 0)),
        scratch_shapes=[
            pltpu.VMEM((seqs, 3 * hw, parts * span), BF16),
            pltpu.VMEM((seqs, parts * span, 4 * hw), BF16),
        ],
        compiler_params=PARAMS,
        name="attention",
    )(qkv, qkv, qkv, bias)


def merge_kernel(*refs):
    heads = len(refs) - 12
    att = refs[:heads]
    gate_ref, x_ref, wm_ref, bm_ref, f1_ref, f2_ref, next_ref, left_ref, right_ref, m_hi, m_lo, f_st = refs[heads:]
    parts, _, _, _ = att[0].shape
    hid = f1_ref.shape[1]
    blocks, _, _, rows = left_ref.shape

    @pl.when(pl.program_id(0) == 0)
    def _():
        hi, lo = split(wm_ref[...])
        m_hi[...] = hi
        m_lo[...] = lo
        hi, lo = split(jnp.concatenate([f1_ref[...], f2_ref[...]], axis=1).T)
        f_st[0:2 * hid, :] = hi
        f_st[2 * hid:4 * hid, :] = lo

    a = jnp.concatenate([att[h][n, 0] for n in range(parts) for h in range(heads)], axis=0)
    ah, al = split((a * gate_ref[0]).T)
    y = x_ref[0] + (mm(ah, m_hi[...]) + mm(al, m_hi[...]) + mm(ah, m_lo[...])) + bm_ref[...]
    next_ref[0] = y
    zh, zl = split(norm_rows(y))
    p = mm_nt(f_st[...], zh)
    p = p[:2 * hid] + p[2 * hid:] + mm_nt(f_st[0:2 * hid, :], zl)
    for b in range(blocks):
        left_ref[b, 0] = p[:hid, b * rows:(b + 1) * rows]
    right_ref[0] = p[hid:]


def merge(att, gate, x, wm, bm, f1, f2, rows):
    seqs, span, ch = x.shape
    parts, _, hw, _ = att[0].shape
    hid = f1.shape[1]
    bm = bm.reshape(1, ch)
    blocks = span // rows
    return pl.pallas_call(
        merge_kernel,
        out_shape=(
            jax.ShapeDtypeStruct(x.shape, F32),
            jax.ShapeDtypeStruct((blocks, seqs, hid, rows), F32),
            jax.ShapeDtypeStruct((seqs, hid, span), F32),
        ),
        grid=(seqs,),
        in_specs=[pl.BlockSpec((parts, 1, hw, span), lambda s: (0, s, 0, 0)) for _ in att]
        + [
            pl.BlockSpec((1, ch, span), lambda s: (s, 0, 0)),
            pl.BlockSpec((1, span, ch), lambda s: (s, 0, 0)),
        ]
        + [whole(a) for a in (wm, bm, f1, f2)],
        out_specs=(
            pl.BlockSpec((1, span, ch), lambda s: (s, 0, 0)),
            pl.BlockSpec((blocks, 1, hid, rows), lambda s: (0, s, 0, 0)),
            pl.BlockSpec((1, hid, span), lambda s: (s, 0, 0)),
        ),
        scratch_shapes=[
            pltpu.VMEM((ch, ch), BF16),
            pltpu.VMEM((ch, ch), BF16),
            pltpu.VMEM((4 * hid, ch), BF16),
        ],
        compiler_params=PARAMS,
        name="merge",
    )(*att, gate, x, wm, bm, f1, f2)


def pair_rows(
    step_rows, group, seqs, first, left_ref, pair_ref, ob_ref, eb_ref, out_ref, r_hi, r_lo, w_st, up_st, dn_st
):
    _, cols, cz = pair_ref.shape
    d_n = w_st.shape[1] // cz

    def body(p, carry):
        lrow = left_ref[pl.ds(pl.multiple_of((first + p * group) * seqs, group * seqs), group * seqs), :]
        lhi = lrow.astype(BF16).astype(F32)
        u = mm(jnp.concatenate([lhi, lhi, lrow - lhi], axis=1).astype(BF16), w_st[...])
        his, los = [], []
        for q in range(group):
            sub = u[q * seqs:(q + 1) * seqs, :]
            hi, lo = split(jnp.concatenate([sub[:, d * cz:(d + 1) * cz] for d in range(d_n)], axis=0))
            his.append(hi)
            los.append(lo)
        mids = []
        for q in range(0, group, 2):
            cross = mm(r_lo[...], jnp.concatenate(his[q:q + 2], axis=1))
            for i in range(2):
                a = mm(r_hi[...], jnp.concatenate([his[q + i], los[q + i]], axis=1))
                o = a[:, :cz] + a[:, cz:] + cross[:, i * cz:(i + 1) * cz]
                mids.append(pair_ref[group * p + q + i] + o / seqs + ob_ref[...])
        for q in range(0, group, 2):
            mid = jnp.concatenate(mids[q:q + 2], axis=0)
            yh, yl = split(norm_rows(mid))
            h = mm(jnp.concatenate([yh, yl, yh], axis=1), up_st[...])
            hh, hl = split(jnp.maximum(h + eb_ref[...], 0.0))
            a = mm(hh, dn_st[...])
            o = mid + (a[:, :cz] + a[:, cz:] + mm(hl, dn_st[:, 0:cz]))
            for i in range(2):
                out_ref[group * p + q + i] = o[i * cols:(i + 1) * cols]
        return carry

    lax.fori_loop(0, step_rows // group, body, 0)


def pair_weights(w_ref, up_ref, dn_ref, w_st, up_st, dn_st):
    c_n = w_ref.shape[0]
    cz = up_ref.shape[0]
    hi, lo = split(w_ref[...])
    w_st[0:c_n, :] = hi
    w_st[c_n:2 * c_n, :] = lo
    w_st[2 * c_n:3 * c_n, :] = hi
    hi, lo = split(up_ref[...])
    up_st[0:cz, :] = hi
    up_st[cz:2 * cz, :] = hi
    up_st[2 * cz:3 * cz, :] = lo
    hi, lo = split(dn_ref[...])
    dn_st[:, 0:cz] = hi
    dn_st[:, cz:2 * cz] = lo


def pair_kernel(
    step_rows, group, seqs, left_ref, right_ref, w_ref, pair_ref, ob_ref, up_ref, eb_ref, dn_ref,
    out_ref, r_hi, r_lo, w_st, up_st, dn_st,
):
    @pl.when(pl.program_id(0) == 0)
    def _():
        r_hi[...], r_lo[...] = split(right_ref[...])
        pair_weights(w_ref, up_ref, dn_ref, w_st, up_st, dn_st)

    pair_rows(
        step_rows, group, seqs, 0, left_ref, pair_ref, ob_ref, eb_ref, out_ref, r_hi, r_lo, w_st, up_st, dn_st
    )


def pair_update(left_rows, right_cols, w2, pair, ob, up, eb, dn, step_rows=8, group=4):
    rows, cols, cz = pair.shape
    seqs = left_rows.shape[0] // rows
    c_n = w2.shape[0]
    ob = ob.reshape(1, -1)
    eb = eb.reshape(1, -1)
    return pl.pallas_call(
        functools.partial(pair_kernel, step_rows, group, seqs),
        out_shape=jax.ShapeDtypeStruct(pair.shape, F32),
        grid=(rows // step_rows,),
        in_specs=[
            pl.BlockSpec((step_rows * seqs, left_rows.shape[1]), lambda i: (i, 0)),
            whole(right_cols), whole(w2),
            pl.BlockSpec((step_rows, cols, cz), lambda i: (i, 0, 0)),
            whole(ob), whole(up), whole(eb), whole(dn),
        ],
        out_specs=pl.BlockSpec((step_rows, cols, cz), lambda i: (i, 0, 0)),
        scratch_shapes=[
            pltpu.VMEM(right_cols.shape, BF16),
            pltpu.VMEM(right_cols.shape, BF16),
            pltpu.VMEM((3 * c_n, w2.shape[1]), BF16),
            pltpu.VMEM((3 * cz, up.shape[1]), BF16),
            pltpu.VMEM((up.shape[1], 2 * cz), BF16),
        ],
        compiler_params=PARAMS,
        name="pair_update",
    )(left_rows, right_cols, w2, pair, ob, up, eb, dn)


def spread_heads(
    parts,
    homolog_embedding,
    pair_state,
    probe_projector,
    lookup_projector,
    content_projector,
    sigmoid_projector,
    sigmoid_offset,
    pair_bias_weight,
    mixing_projector,
    mixing_offset,
    first_factor_projector,
    second_factor_projector,
    outer_product_weight,
    outer_product_bias,
    up_weight,
    expand_bias,
    down_weight,
):
    _, _, ch = homolog_embedding.shape
    rows, cols, cz = pair_state.shape
    heads = pair_bias_weight.shape[1]
    hw = ch // heads
    own_heads = heads // parts
    hid = first_factor_projector.shape[1]

    bias = bias_tile(pair_state, pair_bias_weight).reshape(parts, own_heads, rows, cols)
    bias = lax.all_to_all(bias, "narrow", 0, 0, tiled=True)
    gathered = [
        lax.all_gather(bias[:, h], "wide", axis=0, tiled=False) for h in range(own_heads)
    ]
    qkv, gate = project(
        homolog_embedding, probe_projector, lookup_projector, content_projector, sigmoid_projector,
        sigmoid_offset, parts, hw,
    )
    qkv = lax.all_to_all(qkv, "narrow", 0, 0, tiled=True)
    att = [
        lax.all_to_all(attention(qkv, gathered[h], h, hw), "narrow", 0, 0, tiled=True)
        for h in range(own_heads)
    ]
    alignment_state_next, left, right = merge(
        att, gate, homolog_embedding, mixing_projector, mixing_offset,
        first_factor_projector, second_factor_projector, rows,
    )
    left = lax.all_gather(left, "narrow", axis=0, tiled=True)
    left = lax.all_to_all(left, "wide", 0, 0, tiled=True)
    right = lax.all_gather(right, "wide", axis=0, tiled=True)
    left = left.reshape(-1, hid, rows)
    all_seqs = left.shape[0]
    left_rows = jnp.transpose(left, (2, 0, 1)).reshape(rows * all_seqs, hid)
    right_cols = jnp.transpose(right, (2, 1, 0)).reshape(cols, hid * all_seqs)
    pair_state_next = pair_update(
        left_rows, right_cols, outer_product_weight.reshape(hid, hid * cz), pair_state,
        outer_product_bias, up_weight, expand_bias, down_weight,
    )
    return (alignment_state_next, pair_state_next)


AXES = ("wide", "narrow")
PLANES, CORES = 4, 2
PARTNER = {1: 2, 2: 1}
OUTWARD = {1: 0, 2: 3}
ORDER = ((0, 1, 2, 3), (1, 0, 2, 3), (2, 3, 1, 0), (3, 2, 1, 0))


def send(x, parts, route):
    pairs = []
    for z in range(PLANES):
        for c in range(CORES):
            for n in range(parts):
                to = route(z, c, n)
                if to is not None:
                    pairs.append(((z * CORES + c) * parts + n, (to[0] * CORES + to[1]) * parts + to[2]))
    return lax.ppermute(x, AXES, pairs)


def exchange(blocks, parts):
    out = [blocks[0]]
    for k in range(1, len(blocks)):
        dn, dc = divmod(k, CORES)
        out.append(send(blocks[k], parts, lambda z, c, n: (z, c ^ dc, n ^ dn)))
    return out


def line_gather(x, parts):
    middle = lambda table: lambda z, c, n: (table[z], c, n) if z in table else None
    near = send(x, parts, lambda z, c, n: (z ^ 1, c, n))
    across = send(x, parts, middle(PARTNER))
    out2 = send(across, parts, middle(OUTWARD))
    far = send(near, parts, middle(PARTNER))
    out3 = send(far, parts, middle(OUTWARD))
    return near, (across, out2), (far, out3)


def own_head(ids_ref):
    return ids_ref[1] * CORES + ids_ref[0] % CORES


def head_bias_kernel(group, ids_ref, pair_ref, w_ref, *refs):
    out_refs, lhs = refs[:-1], refs[-1]
    rows, cols, cz = pair_ref.shape
    heads = w_ref.shape[0]

    @pl.when(pl.program_id(0) == 0)
    def _():
        me = own_head(ids_ref)
        own = jnp.concatenate([w_ref[pl.ds(me ^ k, 1), :] for k in range(heads)], axis=0)
        hi = own.astype(BF16).astype(F32)
        both = jnp.concatenate([hi, own - hi], axis=0)
        lhs[...] = jnp.concatenate([both, both], axis=1).astype(BF16)

    for i in range(0, rows, group):
        yh, yl = split(norm_rows(pair_ref[i:i + group].reshape(group * cols, cz)))
        r = mm_nt(lhs[...], jnp.concatenate([yh, yl], axis=1))
        r = r[:heads] + r[heads:]
        for g in range(group):
            for k in range(heads):
                out_refs[k][i + g:i + g + 1, :] = r[k:k + 1, g * cols:(g + 1) * cols]


def head_bias(ids, pair, w, step=32, group=4):
    rows, cols, cz = pair.shape
    heads = w.shape[0]
    return pl.pallas_call(
        functools.partial(head_bias_kernel, group),
        out_shape=(jax.ShapeDtypeStruct((rows, cols), F32),) * heads,
        grid_spec=pltpu.PrefetchScalarGridSpec(
            num_scalar_prefetch=1,
            grid=(rows // step,),
            in_specs=[pl.BlockSpec((step, cols, cz), lambda i, _: (i, 0, 0)), whole(w)],
            out_specs=(pl.BlockSpec((step, cols), lambda i, _: (i, 0)),) * heads,
            scratch_shapes=[pltpu.VMEM((2 * heads, 2 * cz), BF16)],
        ),
        compiler_params=PARAMS,
        name="head_bias",
    )(ids, pair, w)


def head_project_kernel(heads, scale, ids_ref, x_ref, wq_ref, wk_ref, wv_ref, wg_ref, bg_ref, *refs):
    qkv_refs, (gate_ref, w_t, b_p, w_hi, w_lo) = refs[:heads], refs[heads:]
    ch = x_ref.shape[-1]
    hw = ch // heads

    @pl.when(pl.program_id(0) == 0)
    def _():
        me = own_head(ids_ref)
        for t, (ref, f) in enumerate(((wq_ref, scale), (wk_ref, 1.0), (wv_ref, 1.0), (wg_ref, 1.0))):
            w_t[...] = ref[...].T * f
            for k in range(heads):
                src = pl.ds(pl.multiple_of((me ^ k) * hw, hw), hw)
                hi, lo = split(w_t[src, :])
                at = slice(t * ch + k * hw, t * ch + (k + 1) * hw)
                w_hi[at, :] = hi
                w_lo[at, :] = lo
                if t == 3:
                    b_p[k * hw:(k + 1) * hw, :] = bg_ref[src, :]

    yh, yl = split(norm_rows(x_ref[0]))
    r = mm_nt(w_hi[...], yh) + mm_nt(w_hi[...], yl) + mm_nt(w_lo[...], yh)
    for t in range(3):
        for k in range(heads):
            lo = t * ch + k * hw
            qkv_refs[k][t, 0] = r[lo:lo + hw]
    gate_ref[0] = jax.nn.sigmoid(r[3 * ch:] + b_p[...])


def head_project(me, x, wq, wk, wv, wg, bg, heads):
    seqs, span, ch = x.shape
    hw = ch // heads
    bg = bg.reshape(ch, 1)
    return pl.pallas_call(
        functools.partial(head_project_kernel, heads, 1.0 / math.sqrt(hw)),
        out_shape=(jax.ShapeDtypeStruct((3, seqs, hw, span), F32),) * heads
        + (jax.ShapeDtypeStruct((seqs, ch, span), F32),),
        grid_spec=pltpu.PrefetchScalarGridSpec(
            num_scalar_prefetch=1,
            grid=(seqs,),
            in_specs=[pl.BlockSpec((1, span, ch), lambda s, _: (s, 0, 0))]
            + [whole(a) for a in (wq, wk, wv, wg, bg)],
            out_specs=(pl.BlockSpec((3, 1, hw, span), lambda s, _: (0, s, 0, 0)),) * heads
            + (pl.BlockSpec((1, ch, span), lambda s, _: (s, 0, 0)),),
            scratch_shapes=[
                pltpu.VMEM((ch, ch), F32),
                pltpu.VMEM((ch, 1), F32),
                pltpu.VMEM((4 * ch, ch), BF16),
                pltpu.VMEM((4 * ch, ch), BF16),
            ],
        ),
        compiler_params=PARAMS,
        name="head_project",
    )(me, x, wq, wk, wv, wg, bg)


def stage_kernel(n_ref, *refs):
    pieces, (q_ref, k_ref, v_ref) = refs[:-3], refs[-3:]
    _, _, hw, span = pieces[0].shape
    for p, ref in enumerate(pieces):
        part, core = divmod(p, CORES)
        at = slice(part * span, (part + 1) * span)
        q = ref[0, 0]
        qh = q.astype(BF16).astype(F32)
        q_ref[core, 0, (n_ref[0] - 1) ^ part] = (
            jnp.concatenate([qh, qh, q - qh, jnp.zeros_like(q)], axis=0).T.astype(BF16)
        )
        hi, lo = split(ref[1, 0])
        k_ref[core, 0, 0:hw, at] = hi
        k_ref[core, 0, hw:2 * hw, at] = lo
        k_ref[core, 0, 2 * hw:3 * hw, at] = hi
        k_ref[core, 0, 3 * hw:4 * hw, at] = jnp.zeros_like(hi)
        v = ref[2, 0]
        vh = v.astype(BF16).astype(F32)
        st = jnp.concatenate([vh, v - vh, jnp.ones((hw, span), F32), jnp.zeros((hw, span), F32)], axis=0)
        v_ref[core, 0, at, :] = st.T.astype(BF16)


def stage(n, pieces, parts):
    _, seqs, hw, span = pieces[0].shape
    return pl.pallas_call(
        stage_kernel,
        out_shape=(
            jax.ShapeDtypeStruct((CORES, seqs, parts, span, 4 * hw), BF16),
            jax.ShapeDtypeStruct((CORES, seqs, 4 * hw, parts * span), BF16),
            jax.ShapeDtypeStruct((CORES, seqs, parts * span, 4 * hw), BF16),
        ),
        grid_spec=pltpu.PrefetchScalarGridSpec(
            num_scalar_prefetch=1,
            grid=(seqs,),
            in_specs=[pl.BlockSpec((3, 1, hw, span), lambda s, _: (0, s, 0, 0)) for _ in pieces],
            out_specs=(
                pl.BlockSpec((CORES, 1, parts, span, 4 * hw), lambda s, _: (0, s, 0, 0, 0)),
                pl.BlockSpec((CORES, 1, 4 * hw, parts * span), lambda s, _: (0, s, 0, 0)),
                pl.BlockSpec((CORES, 1, parts * span, 4 * hw), lambda s, _: (0, s, 0, 0)),
            ),
        ),
        compiler_params=PARAMS,
        name="stage",
    )(n, *pieces)


def attend_tile(hw, core, q_ref, k_ref, v_ref, bias_refs, store):
    parts = bias_refs[0].shape[1]
    cores, seqs = q_ref.shape[:2]
    bias = jnp.concatenate(
        [
            jnp.concatenate([sum(b[h ^ core, n] for b in bias_refs) for n in range(parts)], axis=1)
            for h in range(CORES)
        ],
        axis=0,
    )
    score = lambda g, s: mm(q_ref[g, s, 0], k_ref[g, s]) + bias
    items = [(g, s) for s in range(seqs) for g in range(cores)]
    ahead = score(*items[0])
    for i, (g, s) in enumerate(items):
        scores = ahead
        if i + 1 < len(items):
            ahead = score(*items[i + 1])
        top = jnp.max(scores, axis=1, keepdims=True)
        ph, plo = split(jnp.exp(scores - top))
        t = (mm(ph, v_ref[g, s]) + mm(plo, v_ref[g, s])).T
        store(g, s, (t[0:hw] + t[hw:2 * hw]) / t[2 * hw:2 * hw + 1])


def head_attention_kernel(hw, turn, tiles, at_ref, q_ref, k_ref, v_ref, *refs):
    bias_refs, out_ref = refs[:tiles], refs[-1]

    def store(g, s, value):
        out_ref[0, g, s] = value

    attend_tile(hw, at_ref[3 * turn + 2], q_ref, k_ref, v_ref, bias_refs, store)


def last_attention_kernel(hw, turn, tiles, at_ref, q_ref, k_ref, v_ref, *refs):
    bias_refs, prev_ref, out_refs, tile = refs[:tiles], refs[tiles], refs[tiles + 1:-1], refs[-1]
    cores = q_ref.shape[0]

    def store(g, s, value):
        tile[g, s] = value

    attend_tile(hw, at_ref[3 * turn + 2], q_ref, k_ref, v_ref, bias_refs, store)
    for k, out_ref in enumerate(out_refs):
        p, g = divmod(k, cores)
        mine = at_ref[3 * turn + 1] == p

        @pl.when(mine)
        def _():
            out_ref[...] = tile[g]

        @pl.when(jnp.logical_not(mine))
        def _():
            out_ref[...] = prev_ref[p, g]


def last_attention(at, turn, q, k, v, tiles, prev, hw, step=2):
    cores, seqs, parts, span, _ = q.shape
    return pl.pallas_call(
        functools.partial(last_attention_kernel, hw, turn, len(tiles)),
        out_shape=(jax.ShapeDtypeStruct((seqs, hw, span), F32),) * (parts * cores),
        grid_spec=pltpu.PrefetchScalarGridSpec(
            num_scalar_prefetch=1,
            grid=(seqs // step,),
            in_specs=[
                pl.BlockSpec((cores, step, 1, span, 4 * hw), lambda s, at: (0, s, at[3 * turn], 0, 0)),
                pl.BlockSpec((cores, step, 4 * hw, parts * span), lambda s, at: (0, s, 0, 0)),
                pl.BlockSpec((cores, step, parts * span, 4 * hw), lambda s, at: (0, s, 0, 0)),
            ]
            + [whole(b) for b in tiles]
            + [pl.BlockSpec((parts, cores, step, hw, span), lambda s, at: (0, 0, s, 0, 0))],
            out_specs=(pl.BlockSpec((step, hw, span), lambda s, at: (s, 0, 0)),) * (parts * cores),
            scratch_shapes=[pltpu.VMEM((cores, step, hw, span), F32)],
        ),
        compiler_params=PARAMS,
        name="last_attention",
    )(at, q, k, v, *tiles, prev)


def head_attention(at, turn, q, k, v, tiles, prev, hw, step=2):
    cores, seqs, parts, span, _ = q.shape
    before = () if prev is None else (prev,)
    return pl.pallas_call(
        functools.partial(head_attention_kernel, hw, turn, len(tiles)),
        out_shape=jax.ShapeDtypeStruct((parts, cores, seqs, hw, span), F32),
        grid_spec=pltpu.PrefetchScalarGridSpec(
            num_scalar_prefetch=1,
            grid=(seqs // step,),
            in_specs=[
                pl.BlockSpec((cores, step, 1, span, 4 * hw), lambda s, at: (0, s, at[3 * turn], 0, 0)),
                pl.BlockSpec((cores, step, 4 * hw, parts * span), lambda s, at: (0, s, 0, 0)),
                pl.BlockSpec((cores, step, parts * span, 4 * hw), lambda s, at: (0, s, 0, 0)),
            ]
            + [whole(b) for b in tiles]
            + [pl.BlockSpec(memory_space=pl.ANY) for _ in before],
            out_specs=pl.BlockSpec((1, cores, step, hw, span), lambda s, at: (at[3 * turn + 1], 0, s, 0, 0)),
        ),
        input_output_aliases={4 + len(tiles): 0} if before else {},
        compiler_params=PARAMS,
        name="head_attention",
    )(at, q, k, v, *tiles, *before)


def head_merge_kernel(heads, ids_ref, *refs):
    pieces = refs[:heads]
    gate_ref, x_ref, wm_ref, bm_ref, f1_ref, f2_ref = refs[heads:heads + 6]
    next_ref, left_a, left_b, right_ref, m_hi, m_lo, f_st = refs[heads + 6:]
    _, hw, span = pieces[0].shape
    hid = f1_ref.shape[0]
    rows = span // CORES

    @pl.when(pl.program_id(0) == 0)
    def _():
        for k in range(heads):
            hi, lo = split(wm_ref[pl.ds(pl.multiple_of((own_head(ids_ref) ^ k) * hw, hw), hw), :])
            m_hi[k * hw:(k + 1) * hw, :] = hi
            m_lo[k * hw:(k + 1) * hw, :] = lo
        hi, lo = split(jnp.concatenate([f1_ref[...], f2_ref[...]], axis=0))
        f_st[0:2 * hid, :] = hi
        f_st[2 * hid:4 * hid, :] = lo

    swap = ids_ref[0] % CORES == 1
    for s in range(x_ref.shape[0]):
        a = jnp.concatenate([p[s] for p in pieces], axis=0)
        ah, al = split((a * gate_ref[s]).T)
        y = x_ref[s] + (mm(ah, m_hi[...]) + mm(al, m_hi[...]) + mm(ah, m_lo[...])) + bm_ref[...]
        next_ref[s] = y
        zh, zl = split(norm_rows(y))
        p = mm_nt(f_st[...], zh)
        p = p[:2 * hid] + p[2 * hid:] + mm_nt(f_st[0:2 * hid, :], zl)
        left_a[s] = jnp.where(swap, p[:hid, rows:], p[:hid, :rows])
        left_b[s] = jnp.where(swap, p[:hid, :rows], p[:hid, rows:])
        right_ref[s] = p[hid:]


def head_merge(me, pieces, gate, x, wm, bm, f1, f2, step=2):
    seqs, span, ch = x.shape
    heads = len(pieces)
    hw = ch // heads
    hid = f1.shape[0]
    rows = span // CORES
    bm = bm.reshape(1, ch)
    return pl.pallas_call(
        functools.partial(head_merge_kernel, heads),
        out_shape=(jax.ShapeDtypeStruct(x.shape, F32),)
        + (jax.ShapeDtypeStruct((seqs, hid, rows), F32),) * CORES
        + (jax.ShapeDtypeStruct((seqs, hid, span), F32),),
        grid_spec=pltpu.PrefetchScalarGridSpec(
            num_scalar_prefetch=1,
            grid=(seqs // step,),
            in_specs=[pl.BlockSpec((step, hw, span), lambda s, _: (s, 0, 0)) for _ in pieces]
            + [
                pl.BlockSpec((step, ch, span), lambda s, _: (s, 0, 0)),
                pl.BlockSpec((step, span, ch), lambda s, _: (s, 0, 0)),
            ]
            + [whole(a) for a in (wm, bm, f1, f2)],
            out_specs=(
                pl.BlockSpec((step, span, ch), lambda s, _: (s, 0, 0)),
                pl.BlockSpec((step, hid, rows), lambda s, _: (s, 0, 0)),
                pl.BlockSpec((step, hid, rows), lambda s, _: (s, 0, 0)),
                pl.BlockSpec((step, hid, span), lambda s, _: (s, 0, 0)),
            ),
            scratch_shapes=[
                pltpu.VMEM((ch, ch), BF16),
                pltpu.VMEM((ch, ch), BF16),
                pltpu.VMEM((4 * hid, ch), BF16),
            ],
        ),
        compiler_params=PARAMS,
        name="head_merge",
    )(me, *pieces, gate, x, wm, bm, f1, f2)


def packed_pair_kernel(step_rows, group, lefts, slots_ref, *refs):
    left_refs, refs = refs[:lefts], refs[lefts:]
    cores, seqs, hid, rows = left_refs[0].shape
    right_refs, refs = refs[:lefts * cores], refs[lefts * cores:]
    w_ref, pair_ref, ob_ref, up_ref, eb_ref, dn_ref = refs[:6]
    out_ref, r_hi, r_lo, w_st, up_st, dn_st, left, right = refs[6:]
    total = lefts * cores * seqs

    @pl.when(pl.program_id(0) == 0)
    def _():
        pair_weights(w_ref, up_ref, dn_ref, w_st, up_st, dn_st)
        for i, ref in enumerate(right_refs):
            core, plane = divmod(i, lefts)
            right[pl.ds((slots_ref[plane] * cores + core) * seqs, seqs)] = ref[...]
        r_hi[...], r_lo[...] = split(jnp.concatenate([right[:, d, :] for d in range(hid)], axis=0).T)
        for p, ref in enumerate(left_refs):
            for t in range(cores):
                for s in range(seqs):
                    at = (p * cores + t) * seqs + s
                    left[pl.ds(at, rows, stride=total), :] = ref[t, s].T

    pair_rows(
        step_rows, group, total, pl.program_id(0) * step_rows, left, pair_ref, ob_ref, eb_ref, out_ref,
        r_hi, r_lo, w_st, up_st, dn_st,
    )


def packed_pair_update(slots, lefts, rights, w2, pair, ob, up, eb, dn, step_rows=8, group=4):
    rows, cols, cz = pair.shape
    cores, seqs, hid, _ = lefts[0].shape
    total = len(lefts) * cores * seqs
    ob = ob.reshape(1, -1)
    eb = eb.reshape(1, -1)
    tile = pl.BlockSpec((step_rows, cols, cz), lambda i, _: (i, 0, 0))
    return pl.pallas_call(
        functools.partial(packed_pair_kernel, step_rows, group, len(lefts)),
        out_shape=jax.ShapeDtypeStruct(pair.shape, F32),
        grid_spec=pltpu.PrefetchScalarGridSpec(
            num_scalar_prefetch=1,
            grid=(rows // step_rows,),
            in_specs=[whole(a) for a in (*lefts, *rights, w2)] + [tile] + [whole(a) for a in (ob, up, eb, dn)],
            out_specs=tile,
            scratch_shapes=[
                pltpu.VMEM((cols, hid * total), BF16),
                pltpu.VMEM((cols, hid * total), BF16),
                pltpu.VMEM((3 * hid, w2.shape[1]), BF16),
                pltpu.VMEM((3 * cz, up.shape[1]), BF16),
                pltpu.VMEM((up.shape[1], 2 * cz), BF16),
                pltpu.VMEM((rows * total, hid), F32),
                pltpu.VMEM((total, hid, cols), F32),
            ],
        ),
        compiler_params=PARAMS,
        name="packed_pair_update",
    )(slots, *lefts, *rights, w2, pair, ob, up, eb, dn)


def after(x, *deps):
    return lax.optimization_barrier((x, deps))[0]


def per_head(
    parts,
    homolog_embedding,
    pair_state,
    probe_projector,
    lookup_projector,
    content_projector,
    sigmoid_projector,
    sigmoid_offset,
    pair_bias_weight,
    mixing_projector,
    mixing_offset,
    first_factor_projector,
    second_factor_projector,
    outer_product_weight,
    outer_product_bias,
    up_weight,
    expand_bias,
    down_weight,
):
    _, _, ch = homolog_embedding.shape
    _, _, cz = pair_state.shape
    heads = pair_bias_weight.shape[1]
    hw = ch // heads
    hid = first_factor_projector.shape[1]
    ids = jnp.stack([lax.axis_index("wide"), lax.axis_index("narrow")])
    tiles = head_bias(ids, pair_state, pair_bias_weight.T)
    late = after(ids, tiles[0])
    z, c, n = late[0] // CORES, late[0] % CORES, late[1]
    order = jnp.asarray(ORDER, jnp.int32)[z]
    at = jnp.stack([order, order ^ n, jnp.full_like(order, c)], axis=1).reshape(-1)
    slots = (jnp.arange(PLANES, dtype=jnp.int32) ^ z) ^ n
    *qkv, gate = head_project(
        ids, after(homolog_embedding, tiles[0], at, slots), probe_projector, lookup_projector, content_projector,
        sigmoid_projector, sigmoid_offset, heads,
    )
    tiles = after(exchange(tiles, parts), gate)
    bias = jnp.stack(
        [jnp.stack([tiles[p * CORES + r] for p in range(parts)]) for r in range(CORES)]
    )
    near, second, third = line_gather(bias, parts)
    qkv = exchange(after(qkv, bias), parts)
    marked = after(n[None], near, second[0]) + 1
    w2 = outer_product_weight.reshape(hid, hid * cz)
    q, k, v = stage(marked, after(qkv, near, second[0], w2), parts)
    bias = after(bias, third[0])
    att = None
    for i, tile in enumerate(((bias,), (near,), second)):
        att = head_attention(at, i, q, k, v, tile, att, hw)
    pieces = exchange(last_attention(at, PLANES - 1, q, k, v, third, att, hw), parts)
    alignment_state_next, left_a, left_b, right = head_merge(
        ids, pieces, gate, homolog_embedding, mixing_projector, mixing_offset,
        first_factor_projector.T, second_factor_projector.T,
    )
    left_b = send(left_b, parts, lambda z0, c0, n0: (n0, c0 ^ 1, z0))
    left_a = send(left_a, parts, lambda z0, c0, n0: (n0, c0, z0))
    left = jnp.stack([left_a, left_b])
    rights = [right] + [send(right, parts, lambda z0, c0, n0, d=d: (z0 ^ d, c0, n0)) for d in range(1, PLANES)]
    lefts = [left] + [send(left, parts, lambda z0, c0, n0, d=d: (z0, c0, n0 ^ d)) for d in range(1, parts)]
    rights += [send(a, parts, lambda z0, c0, n0: (z0, c0 ^ 1, n0)) for a in rights]
    pair_state_next = packed_pair_update(
        slots, lefts, rights, w2, pair_state,
        outer_product_bias, up_weight, expand_bias, down_weight,
    )
    return (alignment_state_next, pair_state_next)


def lines(mesh):
    return mesh.shape["wide"] == PLANES * CORES and mesh.shape["narrow"] == PLANES


def step(mesh, *args):
    parts = mesh.shape["narrow"]
    heads = args[7].shape[1]
    if lines(mesh) and heads == CORES * parts:
        return per_head(parts, *args)
    return spread_heads(parts, *args)


def solution(mesh):
    placed = (P("wide", "narrow", None), P("wide", "narrow", None)) + (P(),) * 15
    return jax.shard_map(
        functools.partial(step, mesh),
        mesh=mesh,
        in_specs=placed,
        out_specs=(P("wide", "narrow", None), P("wide", "narrow", None)),
        check_vma=False,
    )
```

```python
import functools
import math

import jax
import jax.numpy as jnp
from jax import lax
from jax.experimental import pallas as pl
from jax.experimental.pallas import tpu as pltpu
from jax.sharding import PartitionSpec as P


F32, BF16 = jnp.float32, jnp.bfloat16
PARAMS = pltpu.CompilerParams(vmem_limit_bytes=60 * 2**20)


def split(x):
    hi = x.astype(BF16)
    lo = (x - hi.astype(F32)).astype(BF16)
    return hi, lo


def mm(a, b):
    return jnp.dot(a, b, preferred_element_type=F32)


def mm_nt(a, b):
    return lax.dot_general(a, b, (((1,), (1,)), ((), ())), preferred_element_type=F32)


def norm_rows(x):
    mean = jnp.mean(x, axis=-1, keepdims=True)
    c = x - mean
    var = jnp.mean(c * c, axis=-1, keepdims=True)
    return c * lax.rsqrt(var + 1e-05)


def whole(a):
    return pl.BlockSpec(a.shape, lambda *_: (0,) * a.ndim, pipeline_mode=pl.Buffered(1))


def bias_kernel(pair_ref, w_ref, out_ref):
    rows, _, _ = pair_ref.shape
    heads = w_ref.shape[1]
    wh, wl = split(w_ref[...].T)
    lhs = jnp.concatenate(
        [jnp.concatenate([wh, wh], axis=1), jnp.concatenate([wl, wl], axis=1)], axis=0
    )
    for i in range(rows):
        yh, yl = split(norm_rows(pair_ref[i]))
        r = mm_nt(lhs, jnp.concatenate([yh, yl], axis=1))
        out_ref[:, i, :] = r[:heads] + r[heads:]


def bias_tile(pair, w, step=8):
    rows, cols, cz = pair.shape
    heads = w.shape[1]
    return pl.pallas_call(
        bias_kernel,
        out_shape=jax.ShapeDtypeStruct((heads, rows, cols), F32),
        grid=(rows // step,),
        in_specs=[pl.BlockSpec((step, cols, cz), lambda i: (i, 0, 0)), whole(w)],
        out_specs=pl.BlockSpec((heads, step, cols), lambda i: (0, i, 0)),
        compiler_params=PARAMS,
        name="bias_tile",
    )(pair, w)


def project_kernel(parts, scale, x_ref, wq_ref, wk_ref, wv_ref, wg_ref, bg_ref, qkv_ref, gate_ref, w_hi, w_lo):
    ch = x_ref.shape[-1]
    own = ch // parts

    @pl.when(pl.program_id(0) == 0)
    def _():
        for t, (ref, f) in enumerate(((wq_ref, scale), (wk_ref, 1.0), (wv_ref, 1.0), (wg_ref, 1.0))):
            hi, lo = split(ref[...].T * f)
            w_hi[t * ch:(t + 1) * ch, :] = hi
            w_lo[t * ch:(t + 1) * ch, :] = lo

    yh, yl = split(norm_rows(x_ref[0]))
    r = mm_nt(w_hi[...], yh) + mm_nt(w_hi[...], yl) + mm_nt(w_lo[...], yh)
    for t in range(3):
        for n in range(parts):
            lo = t * ch + n * own
            qkv_ref[n, t, 0] = r[lo:lo + own]
    gate_ref[0] = jax.nn.sigmoid(r[3 * ch:] + bg_ref[...])


def project(x, wq, wk, wv, wg, bg, parts, head_width):
    seqs, span, ch = x.shape
    own = ch // parts
    bg = bg.reshape(ch, 1)
    return pl.pallas_call(
        functools.partial(project_kernel, parts, 1.0 / math.sqrt(head_width)),
        out_shape=(
            jax.ShapeDtypeStruct((parts, 3, seqs, own, span), F32),
            jax.ShapeDtypeStruct((seqs, ch, span), F32),
        ),
        grid=(seqs,),
        in_specs=[pl.BlockSpec((1, span, ch), lambda s: (s, 0, 0))] + [whole(a) for a in (wq, wk, wv, wg, bg)],
        out_specs=(
            pl.BlockSpec((parts, 3, 1, own, span), lambda s: (0, 0, s, 0, 0)),
            pl.BlockSpec((1, ch, span), lambda s: (s, 0, 0)),
        ),
        scratch_shapes=[pltpu.VMEM((4 * ch, ch), BF16), pltpu.VMEM((4 * ch, ch), BF16)],
        compiler_params=PARAMS,
        name="project",
    )(x, wq, wk, wv, wg, bg)


def attention_kernel(hw, q_ref, k_ref, v_ref, bias_ref, out_ref, ks, vs):
    parts = k_ref.shape[0]
    span = k_ref.shape[-1]
    s = pl.program_id(1)

    @pl.when(pl.program_id(0) == 0)
    def _():
        for n in range(parts):
            at = slice(n * span, (n + 1) * span)
            hi, lo = split(k_ref[n, 0, 0])
            ks[s, 0:hw, at] = hi
            ks[s, hw:2 * hw, at] = lo
            ks[s, 2 * hw:3 * hw, at] = hi
            v = v_ref[n, 0, 0]
            vh = v.astype(BF16).astype(F32)
            st = jnp.concatenate([vh, v - vh, jnp.ones((hw, span), F32), jnp.zeros((hw, span), F32)], axis=0)
            vs[s, at, :] = st.T.astype(BF16)

    q = q_ref[0, 0, 0]
    qh = q.astype(BF16).astype(F32)
    qst = jnp.concatenate([qh, qh, q - qh, jnp.zeros_like(q)], axis=0).T[:, :3 * hw].astype(BF16)
    bias = jnp.concatenate(
        [
            jnp.concatenate([bias_ref[w, n] for n in range(parts)], axis=1)
            for w in range(bias_ref.shape[0])
        ],
        axis=0,
    )
    scores = mm(qst, ks[s]) + bias
    top = jnp.max(scores, axis=1, keepdims=True)
    ph, plo = split(jnp.exp(scores - top))
    t = (mm(ph, vs[s]) + mm(plo, vs[s])).T
    out_ref[0, 0] = (t[0:hw] + t[hw:2 * hw]) / t[2 * hw:2 * hw + 1]


def attention(qkv, bias, head, hw):
    parts, _, seqs, _, span = qkv.shape
    _, _, rows, _ = bias.shape
    per = span // rows
    return pl.pallas_call(
        functools.partial(attention_kernel, hw),
        out_shape=jax.ShapeDtypeStruct((parts, seqs, hw, span), F32),
        grid=(parts, seqs),
        in_specs=[
            pl.BlockSpec((1, 1, 1, hw, span), lambda b, s: (b, 0, s, head, 0)),
            pl.BlockSpec((parts, 1, 1, hw, span), lambda b, s: (0, 1, s, head, 0)),
            pl.BlockSpec((parts, 1, 1, hw, span), lambda b, s: (0, 2, s, head, 0)),
            pl.BlockSpec((per, parts, rows, span), lambda b, s: (b, 0, 0, 0)),
        ],
        out_specs=pl.BlockSpec((1, 1, hw, span), lambda b, s: (b, s, 0, 0)),
        scratch_shapes=[
            pltpu.VMEM((seqs, 3 * hw, parts * span), BF16),
            pltpu.VMEM((seqs, parts * span, 4 * hw), BF16),
        ],
        compiler_params=PARAMS,
        name="attention",
    )(qkv, qkv, qkv, bias)


def merge_kernel(*refs):
    heads = len(refs) - 12
    att = refs[:heads]
    gate_ref, x_ref, wm_ref, bm_ref, f1_ref, f2_ref, next_ref, left_ref, right_ref, m_hi, m_lo, f_st = refs[heads:]
    parts, _, _, _ = att[0].shape
    hid = f1_ref.shape[1]
    blocks, _, _, rows = left_ref.shape

    @pl.when(pl.program_id(0) == 0)
    def _():
        hi, lo = split(wm_ref[...])
        m_hi[...] = hi
        m_lo[...] = lo
        hi, lo = split(jnp.concatenate([f1_ref[...], f2_ref[...]], axis=1).T)
        f_st[0:2 * hid, :] = hi
        f_st[2 * hid:4 * hid, :] = lo

    a = jnp.concatenate([att[h][n, 0] for n in range(parts) for h in range(heads)], axis=0)
    ah, al = split((a * gate_ref[0]).T)
    y = x_ref[0] + (mm(ah, m_hi[...]) + mm(al, m_hi[...]) + mm(ah, m_lo[...])) + bm_ref[...]
    next_ref[0] = y
    zh, zl = split(norm_rows(y))
    p = mm_nt(f_st[...], zh)
    p = p[:2 * hid] + p[2 * hid:] + mm_nt(f_st[0:2 * hid, :], zl)
    for b in range(blocks):
        left_ref[b, 0] = p[:hid, b * rows:(b + 1) * rows]
    right_ref[0] = p[hid:]


def merge(att, gate, x, wm, bm, f1, f2, rows):
    seqs, span, ch = x.shape
    parts, _, hw, _ = att[0].shape
    hid = f1.shape[1]
    bm = bm.reshape(1, ch)
    blocks = span // rows
    return pl.pallas_call(
        merge_kernel,
        out_shape=(
            jax.ShapeDtypeStruct(x.shape, F32),
            jax.ShapeDtypeStruct((blocks, seqs, hid, rows), F32),
            jax.ShapeDtypeStruct((seqs, hid, span), F32),
        ),
        grid=(seqs,),
        in_specs=[pl.BlockSpec((parts, 1, hw, span), lambda s: (0, s, 0, 0)) for _ in att]
        + [
            pl.BlockSpec((1, ch, span), lambda s: (s, 0, 0)),
            pl.BlockSpec((1, span, ch), lambda s: (s, 0, 0)),
        ]
        + [whole(a) for a in (wm, bm, f1, f2)],
        out_specs=(
            pl.BlockSpec((1, span, ch), lambda s: (s, 0, 0)),
            pl.BlockSpec((blocks, 1, hid, rows), lambda s: (0, s, 0, 0)),
            pl.BlockSpec((1, hid, span), lambda s: (s, 0, 0)),
        ),
        scratch_shapes=[
            pltpu.VMEM((ch, ch), BF16),
            pltpu.VMEM((ch, ch), BF16),
            pltpu.VMEM((4 * hid, ch), BF16),
        ],
        compiler_params=PARAMS,
        name="merge",
    )(*att, gate, x, wm, bm, f1, f2)


def pair_rows(
    step_rows, group, seqs, first, left_ref, pair_ref, ob_ref, eb_ref, out_ref, r_hi, r_lo, w_st, up_st, dn_st
):
    _, cols, cz = pair_ref.shape
    d_n = w_st.shape[1] // cz

    def body(p, carry):
        lrow = left_ref[pl.ds(pl.multiple_of((first + p * group) * seqs, group * seqs), group * seqs), :]
        lhi = lrow.astype(BF16).astype(F32)
        u = mm(jnp.concatenate([lhi, lhi, lrow - lhi], axis=1).astype(BF16), w_st[...])
        his, los = [], []
        for q in range(group):
            sub = u[q * seqs:(q + 1) * seqs, :]
            hi, lo = split(jnp.concatenate([sub[:, d * cz:(d + 1) * cz] for d in range(d_n)], axis=0))
            his.append(hi)
            los.append(lo)
        mids = []
        for q in range(0, group, 2):
            cross = mm(r_lo[...], jnp.concatenate(his[q:q + 2], axis=1))
            for i in range(2):
                a = mm(r_hi[...], jnp.concatenate([his[q + i], los[q + i]], axis=1))
                o = a[:, :cz] + a[:, cz:] + cross[:, i * cz:(i + 1) * cz]
                mids.append(pair_ref[group * p + q + i] + o / seqs + ob_ref[...])
        for q in range(0, group, 2):
            mid = jnp.concatenate(mids[q:q + 2], axis=0)
            yh, yl = split(norm_rows(mid))
            h = mm(jnp.concatenate([yh, yl, yh], axis=1), up_st[...])
            hh, hl = split(jnp.maximum(h + eb_ref[...], 0.0))
            a = mm(hh, dn_st[...])
            o = mid + (a[:, :cz] + a[:, cz:] + mm(hl, dn_st[:, 0:cz]))
            for i in range(2):
                out_ref[group * p + q + i] = o[i * cols:(i + 1) * cols]
        return carry

    lax.fori_loop(0, step_rows // group, body, 0)


def pair_weights(w_ref, up_ref, dn_ref, w_st, up_st, dn_st):
    c_n = w_ref.shape[0]
    cz = up_ref.shape[0]
    hi, lo = split(w_ref[...])
    w_st[0:c_n, :] = hi
    w_st[c_n:2 * c_n, :] = lo
    w_st[2 * c_n:3 * c_n, :] = hi
    hi, lo = split(up_ref[...])
    up_st[0:cz, :] = hi
    up_st[cz:2 * cz, :] = hi
    up_st[2 * cz:3 * cz, :] = lo
    hi, lo = split(dn_ref[...])
    dn_st[:, 0:cz] = hi
    dn_st[:, cz:2 * cz] = lo


def pair_kernel(
    step_rows, group, seqs, left_ref, right_ref, w_ref, pair_ref, ob_ref, up_ref, eb_ref, dn_ref,
    out_ref, r_hi, r_lo, w_st, up_st, dn_st,
):
    @pl.when(pl.program_id(0) == 0)
    def _():
        r_hi[...], r_lo[...] = split(right_ref[...])
        pair_weights(w_ref, up_ref, dn_ref, w_st, up_st, dn_st)

    pair_rows(
        step_rows, group, seqs, 0, left_ref, pair_ref, ob_ref, eb_ref, out_ref, r_hi, r_lo, w_st, up_st, dn_st
    )


def pair_update(left_rows, right_cols, w2, pair, ob, up, eb, dn, step_rows=8, group=4):
    rows, cols, cz = pair.shape
    seqs = left_rows.shape[0] // rows
    c_n = w2.shape[0]
    ob = ob.reshape(1, -1)
    eb = eb.reshape(1, -1)
    return pl.pallas_call(
        functools.partial(pair_kernel, step_rows, group, seqs),
        out_shape=jax.ShapeDtypeStruct(pair.shape, F32),
        grid=(rows // step_rows,),
        in_specs=[
            pl.BlockSpec((step_rows * seqs, left_rows.shape[1]), lambda i: (i, 0)),
            whole(right_cols), whole(w2),
            pl.BlockSpec((step_rows, cols, cz), lambda i: (i, 0, 0)),
            whole(ob), whole(up), whole(eb), whole(dn),
        ],
        out_specs=pl.BlockSpec((step_rows, cols, cz), lambda i: (i, 0, 0)),
        scratch_shapes=[
            pltpu.VMEM(right_cols.shape, BF16),
            pltpu.VMEM(right_cols.shape, BF16),
            pltpu.VMEM((3 * c_n, w2.shape[1]), BF16),
            pltpu.VMEM((3 * cz, up.shape[1]), BF16),
            pltpu.VMEM((up.shape[1], 2 * cz), BF16),
        ],
        compiler_params=PARAMS,
        name="pair_update",
    )(left_rows, right_cols, w2, pair, ob, up, eb, dn)


def spread_heads(
    parts,
    homolog_embedding,
    pair_state,
    probe_projector,
    lookup_projector,
    content_projector,
    sigmoid_projector,
    sigmoid_offset,
    pair_bias_weight,
    mixing_projector,
    mixing_offset,
    first_factor_projector,
    second_factor_projector,
    outer_product_weight,
    outer_product_bias,
    up_weight,
    expand_bias,
    down_weight,
):
    _, _, ch = homolog_embedding.shape
    rows, cols, cz = pair_state.shape
    heads = pair_bias_weight.shape[1]
    hw = ch // heads
    own_heads = heads // parts
    hid = first_factor_projector.shape[1]

    bias = bias_tile(pair_state, pair_bias_weight).reshape(parts, own_heads, rows, cols)
    bias = lax.all_to_all(bias, "narrow", 0, 0, tiled=True)
    gathered = [
        lax.all_gather(bias[:, h], "wide", axis=0, tiled=False) for h in range(own_heads)
    ]
    qkv, gate = project(
        homolog_embedding, probe_projector, lookup_projector, content_projector, sigmoid_projector,
        sigmoid_offset, parts, hw,
    )
    qkv = lax.all_to_all(qkv, "narrow", 0, 0, tiled=True)
    att = [
        lax.all_to_all(attention(qkv, gathered[h], h, hw), "narrow", 0, 0, tiled=True)
        for h in range(own_heads)
    ]
    alignment_state_next, left, right = merge(
        att, gate, homolog_embedding, mixing_projector, mixing_offset,
        first_factor_projector, second_factor_projector, rows,
    )
    left = lax.all_gather(left, "narrow", axis=0, tiled=True)
    left = lax.all_to_all(left, "wide", 0, 0, tiled=True)
    right = lax.all_gather(right, "wide", axis=0, tiled=True)
    left = left.reshape(-1, hid, rows)
    all_seqs = left.shape[0]
    left_rows = jnp.transpose(left, (2, 0, 1)).reshape(rows * all_seqs, hid)
    right_cols = jnp.transpose(right, (2, 1, 0)).reshape(cols, hid * all_seqs)
    pair_state_next = pair_update(
        left_rows, right_cols, outer_product_weight.reshape(hid, hid * cz), pair_state,
        outer_product_bias, up_weight, expand_bias, down_weight,
    )
    return (alignment_state_next, pair_state_next)


AXES = ("wide", "narrow")
PLANES, CORES = 4, 2
PARTNER = {1: 2, 2: 1}
OUTWARD = {1: 0, 2: 3}
ORDER = ((0, 1, 2, 3), (1, 0, 2, 3), (2, 3, 1, 0), (3, 2, 1, 0))


def send(x, parts, route):
    pairs = []
    for z in range(PLANES):
        for c in range(CORES):
            for n in range(parts):
                to = route(z, c, n)
                if to is not None:
                    pairs.append(((z * CORES + c) * parts + n, (to[0] * CORES + to[1]) * parts + to[2]))
    return lax.ppermute(x, AXES, pairs)


def exchange(blocks, parts):
    out = [blocks[0]]
    for k in range(1, len(blocks)):
        dn, dc = divmod(k, CORES)
        out.append(send(blocks[k], parts, lambda z, c, n: (z, c ^ dc, n ^ dn)))
    return out


def line_gather(x, parts):
    middle = lambda table: lambda z, c, n: (table[z], c, n) if z in table else None
    near = send(x, parts, lambda z, c, n: (z ^ 1, c, n))
    across = send(x, parts, middle(PARTNER))
    out2 = send(across, parts, middle(OUTWARD))
    far = send(near, parts, middle(PARTNER))
    out3 = send(far, parts, middle(OUTWARD))
    return near, (across, out2), (far, out3)


def own_head(ids_ref):
    return ids_ref[1] * CORES + ids_ref[0] % CORES


def head_bias_kernel(group, ids_ref, pair_ref, w_ref, *refs):
    out_refs, lhs = refs[:-1], refs[-1]
    rows, cols, cz = pair_ref.shape
    heads = w_ref.shape[0]

    @pl.when(pl.program_id(0) == 0)
    def _():
        me = own_head(ids_ref)
        own = jnp.concatenate([w_ref[pl.ds(me ^ k, 1), :] for k in range(heads)], axis=0)
        hi = own.astype(BF16).astype(F32)
        both = jnp.concatenate([hi, own - hi], axis=0)
        lhs[...] = jnp.concatenate([both, both], axis=1).astype(BF16)

    for i in range(0, rows, group):
        yh, yl = split(norm_rows(pair_ref[i:i + group].reshape(group * cols, cz)))
        r = mm_nt(lhs[...], jnp.concatenate([yh, yl], axis=1))
        r = r[:heads] + r[heads:]
        for g in range(group):
            for k in range(heads):
                out_refs[k][i + g:i + g + 1, :] = r[k:k + 1, g * cols:(g + 1) * cols]


def head_bias(ids, pair, w, step=32, group=4):
    rows, cols, cz = pair.shape
    heads = w.shape[0]
    return pl.pallas_call(
        functools.partial(head_bias_kernel, group),
        out_shape=(jax.ShapeDtypeStruct((rows, cols), F32),) * heads,
        grid_spec=pltpu.PrefetchScalarGridSpec(
            num_scalar_prefetch=1,
            grid=(rows // step,),
            in_specs=[pl.BlockSpec((step, cols, cz), lambda i, _: (i, 0, 0)), whole(w)],
            out_specs=(pl.BlockSpec((step, cols), lambda i, _: (i, 0)),) * heads,
            scratch_shapes=[pltpu.VMEM((2 * heads, 2 * cz), BF16)],
        ),
        compiler_params=PARAMS,
        name="head_bias",
    )(ids, pair, w)


def head_project_kernel(heads, scale, ids_ref, x_ref, wq_ref, wk_ref, wv_ref, wg_ref, bg_ref, *refs):
    qkv_refs, (gate_ref, w_t, b_p, w_hi, w_lo) = refs[:heads], refs[heads:]
    ch = x_ref.shape[-1]
    hw = ch // heads

    @pl.when(pl.program_id(0) == 0)
    def _():
        me = own_head(ids_ref)
        for t, (ref, f) in enumerate(((wq_ref, scale), (wk_ref, 1.0), (wv_ref, 1.0), (wg_ref, 1.0))):
            w_t[...] = ref[...].T * f
            for k in range(heads):
                src = pl.ds(pl.multiple_of((me ^ k) * hw, hw), hw)
                hi, lo = split(w_t[src, :])
                at = slice(t * ch + k * hw, t * ch + (k + 1) * hw)
                w_hi[at, :] = hi
                w_lo[at, :] = lo
                if t == 3:
                    b_p[k * hw:(k + 1) * hw, :] = bg_ref[src, :]

    yh, yl = split(norm_rows(x_ref[0]))
    r = mm_nt(w_hi[...], yh) + mm_nt(w_hi[...], yl) + mm_nt(w_lo[...], yh)
    for t in range(3):
        for k in range(heads):
            lo = t * ch + k * hw
            qkv_refs[k][t, 0] = r[lo:lo + hw]
    gate_ref[0] = jax.nn.sigmoid(r[3 * ch:] + b_p[...])


def head_project(me, x, wq, wk, wv, wg, bg, heads):
    seqs, span, ch = x.shape
    hw = ch // heads
    bg = bg.reshape(ch, 1)
    return pl.pallas_call(
        functools.partial(head_project_kernel, heads, 1.0 / math.sqrt(hw)),
        out_shape=(jax.ShapeDtypeStruct((3, seqs, hw, span), F32),) * heads
        + (jax.ShapeDtypeStruct((seqs, ch, span), F32),),
        grid_spec=pltpu.PrefetchScalarGridSpec(
            num_scalar_prefetch=1,
            grid=(seqs,),
            in_specs=[pl.BlockSpec((1, span, ch), lambda s, _: (s, 0, 0))]
            + [whole(a) for a in (wq, wk, wv, wg, bg)],
            out_specs=(pl.BlockSpec((3, 1, hw, span), lambda s, _: (0, s, 0, 0)),) * heads
            + (pl.BlockSpec((1, ch, span), lambda s, _: (s, 0, 0)),),
            scratch_shapes=[
                pltpu.VMEM((ch, ch), F32),
                pltpu.VMEM((ch, 1), F32),
                pltpu.VMEM((4 * ch, ch), BF16),
                pltpu.VMEM((4 * ch, ch), BF16),
            ],
        ),
        compiler_params=PARAMS,
        name="head_project",
    )(me, x, wq, wk, wv, wg, bg)


def stage_kernel(n_ref, *refs):
    pieces, (q_ref, k_ref, v_ref) = refs[:-3], refs[-3:]
    _, _, hw, span = pieces[0].shape
    for p, ref in enumerate(pieces):
        part, core = divmod(p, CORES)
        at = slice(part * span, (part + 1) * span)
        q = ref[0, 0]
        qh = q.astype(BF16).astype(F32)
        q_ref[core, 0, (n_ref[0] - 1) ^ part] = (
            jnp.concatenate([qh, qh, q - qh, jnp.zeros_like(q)], axis=0).T.astype(BF16)
        )
        hi, lo = split(ref[1, 0])
        k_ref[core, 0, 0:hw, at] = hi
        k_ref[core, 0, hw:2 * hw, at] = lo
        k_ref[core, 0, 2 * hw:3 * hw, at] = hi
        k_ref[core, 0, 3 * hw:4 * hw, at] = jnp.zeros_like(hi)
        v = ref[2, 0]
        vh = v.astype(BF16).astype(F32)
        st = jnp.concatenate([vh, v - vh, jnp.ones((hw, span), F32), jnp.zeros((hw, span), F32)], axis=0)
        v_ref[core, 0, at, :] = st.T.astype(BF16)


def stage(n, pieces, parts):
    _, seqs, hw, span = pieces[0].shape
    return pl.pallas_call(
        stage_kernel,
        out_shape=(
            jax.ShapeDtypeStruct((CORES, seqs, parts, span, 4 * hw), BF16),
            jax.ShapeDtypeStruct((CORES, seqs, 4 * hw, parts * span), BF16),
            jax.ShapeDtypeStruct((CORES, seqs, parts * span, 4 * hw), BF16),
        ),
        grid_spec=pltpu.PrefetchScalarGridSpec(
            num_scalar_prefetch=1,
            grid=(seqs,),
            in_specs=[pl.BlockSpec((3, 1, hw, span), lambda s, _: (0, s, 0, 0)) for _ in pieces],
            out_specs=(
                pl.BlockSpec((CORES, 1, parts, span, 4 * hw), lambda s, _: (0, s, 0, 0, 0)),
                pl.BlockSpec((CORES, 1, 4 * hw, parts * span), lambda s, _: (0, s, 0, 0)),
                pl.BlockSpec((CORES, 1, parts * span, 4 * hw), lambda s, _: (0, s, 0, 0)),
            ),
        ),
        compiler_params=PARAMS,
        name="stage",
    )(n, *pieces)


def head_attention_kernel(hw, turn, tiles, at_ref, q_ref, k_ref, v_ref, *refs):
    bias_refs, out_ref = refs[:tiles], refs[-1]
    parts = bias_refs[0].shape[1]
    cores, seqs = q_ref.shape[:2]
    core = at_ref[3 * turn + 2]
    bias = jnp.concatenate(
        [
            jnp.concatenate([sum(b[h ^ core, n] for b in bias_refs) for n in range(parts)], axis=1)
            for h in range(CORES)
        ],
        axis=0,
    )
    score = lambda g, s: mm(q_ref[g, s, 0], k_ref[g, s]) + bias
    items = [(g, s) for s in range(seqs) for g in range(cores)]
    ahead = score(*items[0])
    for i, (g, s) in enumerate(items):
        scores = ahead
        if i + 1 < len(items):
            ahead = score(*items[i + 1])
        top = jnp.max(scores, axis=1, keepdims=True)
        ph, plo = split(jnp.exp(scores - top))
        t = (mm(ph, v_ref[g, s]) + mm(plo, v_ref[g, s])).T
        out_ref[0, g, s] = (t[0:hw] + t[hw:2 * hw]) / t[2 * hw:2 * hw + 1]


def head_attention(at, turn, q, k, v, tiles, prev, hw, step=2):
    cores, seqs, parts, span, _ = q.shape
    before = () if prev is None else (prev,)
    return pl.pallas_call(
        functools.partial(head_attention_kernel, hw, turn, len(tiles)),
        out_shape=jax.ShapeDtypeStruct((parts, cores, seqs, hw, span), F32),
        grid_spec=pltpu.PrefetchScalarGridSpec(
            num_scalar_prefetch=1,
            grid=(seqs // step,),
            in_specs=[
                pl.BlockSpec((cores, step, 1, span, 4 * hw), lambda s, at: (0, s, at[3 * turn], 0, 0)),
                pl.BlockSpec((cores, step, 4 * hw, parts * span), lambda s, at: (0, s, 0, 0)),
                pl.BlockSpec((cores, step, parts * span, 4 * hw), lambda s, at: (0, s, 0, 0)),
            ]
            + [whole(b) for b in tiles]
            + [pl.BlockSpec(memory_space=pl.ANY) for _ in before],
            out_specs=pl.BlockSpec((1, cores, step, hw, span), lambda s, at: (at[3 * turn + 1], 0, s, 0, 0)),
        ),
        input_output_aliases={4 + len(tiles): 0} if before else {},
        compiler_params=PARAMS,
        name="head_attention",
    )(at, q, k, v, *tiles, *before)


def head_merge_kernel(heads, ids_ref, *refs):
    pieces = refs[:heads]
    gate_ref, x_ref, wm_ref, bm_ref, f1_ref, f2_ref = refs[heads:heads + 6]
    next_ref, left_a, left_b, right_ref, m_hi, m_lo, f_st = refs[heads + 6:]
    _, hw, span = pieces[0].shape
    hid = f1_ref.shape[0]
    rows = span // CORES

    @pl.when(pl.program_id(0) == 0)
    def _():
        for k in range(heads):
            hi, lo = split(wm_ref[pl.ds(pl.multiple_of((own_head(ids_ref) ^ k) * hw, hw), hw), :])
            m_hi[k * hw:(k + 1) * hw, :] = hi
            m_lo[k * hw:(k + 1) * hw, :] = lo
        hi, lo = split(jnp.concatenate([f1_ref[...], f2_ref[...]], axis=0))
        f_st[0:2 * hid, :] = hi
        f_st[2 * hid:4 * hid, :] = lo

    swap = ids_ref[0] % CORES == 1
    for s in range(x_ref.shape[0]):
        a = jnp.concatenate([p[s] for p in pieces], axis=0)
        ah, al = split((a * gate_ref[s]).T)
        y = x_ref[s] + (mm(ah, m_hi[...]) + mm(al, m_hi[...]) + mm(ah, m_lo[...])) + bm_ref[...]
        next_ref[s] = y
        zh, zl = split(norm_rows(y))
        p = mm_nt(f_st[...], zh)
        p = p[:2 * hid] + p[2 * hid:] + mm_nt(f_st[0:2 * hid, :], zl)
        left_a[s] = jnp.where(swap, p[:hid, rows:], p[:hid, :rows])
        left_b[s] = jnp.where(swap, p[:hid, :rows], p[:hid, rows:])
        right_ref[s] = p[hid:]


def head_merge(me, pieces, gate, x, wm, bm, f1, f2, step=2):
    seqs, span, ch = x.shape
    heads = len(pieces)
    hw = ch // heads
    hid = f1.shape[0]
    rows = span // CORES
    bm = bm.reshape(1, ch)
    return pl.pallas_call(
        functools.partial(head_merge_kernel, heads),
        out_shape=(jax.ShapeDtypeStruct(x.shape, F32),)
        + (jax.ShapeDtypeStruct((seqs, hid, rows), F32),) * CORES
        + (jax.ShapeDtypeStruct((seqs, hid, span), F32),),
        grid_spec=pltpu.PrefetchScalarGridSpec(
            num_scalar_prefetch=1,
            grid=(seqs // step,),
            in_specs=[pl.BlockSpec((step, hw, span), lambda s, _: (s, 0, 0)) for _ in pieces]
            + [
                pl.BlockSpec((step, ch, span), lambda s, _: (s, 0, 0)),
                pl.BlockSpec((step, span, ch), lambda s, _: (s, 0, 0)),
            ]
            + [whole(a) for a in (wm, bm, f1, f2)],
            out_specs=(
                pl.BlockSpec((step, span, ch), lambda s, _: (s, 0, 0)),
                pl.BlockSpec((step, hid, rows), lambda s, _: (s, 0, 0)),
                pl.BlockSpec((step, hid, rows), lambda s, _: (s, 0, 0)),
                pl.BlockSpec((step, hid, span), lambda s, _: (s, 0, 0)),
            ),
            scratch_shapes=[
                pltpu.VMEM((ch, ch), BF16),
                pltpu.VMEM((ch, ch), BF16),
                pltpu.VMEM((4 * hid, ch), BF16),
            ],
        ),
        compiler_params=PARAMS,
        name="head_merge",
    )(me, *pieces, gate, x, wm, bm, f1, f2)


def packed_pair_kernel(step_rows, group, lefts, slots_ref, *refs):
    left_refs, refs = refs[:lefts], refs[lefts:]
    cores, seqs, hid, rows = left_refs[0].shape
    right_refs, refs = refs[:lefts * cores], refs[lefts * cores:]
    w_ref, pair_ref, ob_ref, up_ref, eb_ref, dn_ref = refs[:6]
    out_ref, r_hi, r_lo, w_st, up_st, dn_st, left, right = refs[6:]
    total = lefts * cores * seqs

    @pl.when(pl.program_id(0) == 0)
    def _():
        pair_weights(w_ref, up_ref, dn_ref, w_st, up_st, dn_st)
        for i, ref in enumerate(right_refs):
            core, plane = divmod(i, lefts)
            right[pl.ds((slots_ref[plane] * cores + core) * seqs, seqs)] = ref[...]
        r_hi[...], r_lo[...] = split(jnp.concatenate([right[:, d, :] for d in range(hid)], axis=0).T)
        for p, ref in enumerate(left_refs):
            for t in range(cores):
                for s in range(seqs):
                    at = (p * cores + t) * seqs + s
                    left[pl.ds(at, rows, stride=total), :] = ref[t, s].T

    pair_rows(
        step_rows, group, total, pl.program_id(0) * step_rows, left, pair_ref, ob_ref, eb_ref, out_ref,
        r_hi, r_lo, w_st, up_st, dn_st,
    )


def packed_pair_update(slots, lefts, rights, w2, pair, ob, up, eb, dn, step_rows=8, group=4):
    rows, cols, cz = pair.shape
    cores, seqs, hid, _ = lefts[0].shape
    total = len(lefts) * cores * seqs
    ob = ob.reshape(1, -1)
    eb = eb.reshape(1, -1)
    tile = pl.BlockSpec((step_rows, cols, cz), lambda i, _: (i, 0, 0))
    return pl.pallas_call(
        functools.partial(packed_pair_kernel, step_rows, group, len(lefts)),
        out_shape=jax.ShapeDtypeStruct(pair.shape, F32),
        grid_spec=pltpu.PrefetchScalarGridSpec(
            num_scalar_prefetch=1,
            grid=(rows // step_rows,),
            in_specs=[whole(a) for a in (*lefts, *rights, w2)] + [tile] + [whole(a) for a in (ob, up, eb, dn)],
            out_specs=tile,
            scratch_shapes=[
                pltpu.VMEM((cols, hid * total), BF16),
                pltpu.VMEM((cols, hid * total), BF16),
                pltpu.VMEM((3 * hid, w2.shape[1]), BF16),
                pltpu.VMEM((3 * cz, up.shape[1]), BF16),
                pltpu.VMEM((up.shape[1], 2 * cz), BF16),
                pltpu.VMEM((rows * total, hid), F32),
                pltpu.VMEM((total, hid, cols), F32),
            ],
        ),
        compiler_params=PARAMS,
        name="packed_pair_update",
    )(slots, *lefts, *rights, w2, pair, ob, up, eb, dn)


def after(x, *deps):
    return lax.optimization_barrier((x, deps))[0]


def per_head(
    parts,
    homolog_embedding,
    pair_state,
    probe_projector,
    lookup_projector,
    content_projector,
    sigmoid_projector,
    sigmoid_offset,
    pair_bias_weight,
    mixing_projector,
    mixing_offset,
    first_factor_projector,
    second_factor_projector,
    outer_product_weight,
    outer_product_bias,
    up_weight,
    expand_bias,
    down_weight,
):
    _, _, ch = homolog_embedding.shape
    _, _, cz = pair_state.shape
    heads = pair_bias_weight.shape[1]
    hw = ch // heads
    hid = first_factor_projector.shape[1]
    ids = jnp.stack([lax.axis_index("wide"), lax.axis_index("narrow")])
    tiles = head_bias(ids, pair_state, pair_bias_weight.T)
    late = after(ids, tiles[0])
    z, c, n = late[0] // CORES, late[0] % CORES, late[1]
    order = jnp.asarray(ORDER, jnp.int32)[z]
    at = jnp.stack([order, order ^ n, jnp.full_like(order, c)], axis=1).reshape(-1)
    slots = (jnp.arange(PLANES, dtype=jnp.int32) ^ z) ^ n
    *qkv, gate = head_project(
        ids, after(homolog_embedding, tiles[0], at, slots), probe_projector, lookup_projector, content_projector,
        sigmoid_projector, sigmoid_offset, heads,
    )
    tiles = after(exchange(tiles, parts), gate)
    bias = jnp.stack(
        [jnp.stack([tiles[p * CORES + r] for p in range(parts)]) for r in range(CORES)]
    )
    near, second, third = line_gather(bias, parts)
    qkv = exchange(after(qkv, bias), parts)
    marked = after(n[None], near, second[0]) + 1
    q, k, v = stage(marked, after(qkv, near, second[0]), parts)
    bias = after(bias, third[0])
    att = None
    for i, tile in enumerate(((bias,), (near,), second, third)):
        att = head_attention(at, i, q, k, v, tile, att, hw)
    pieces = exchange([att[p, r] for p in range(parts) for r in range(CORES)], parts)
    alignment_state_next, left_a, left_b, right = head_merge(
        ids, pieces, gate, homolog_embedding, mixing_projector, mixing_offset,
        first_factor_projector.T, second_factor_projector.T,
    )
    left_b = send(left_b, parts, lambda z0, c0, n0: (n0, c0 ^ 1, z0))
    left_a = send(left_a, parts, lambda z0, c0, n0: (n0, c0, z0))
    left = jnp.stack([left_a, left_b])
    rights = [right] + [send(right, parts, lambda z0, c0, n0, d=d: (z0 ^ d, c0, n0)) for d in range(1, PLANES)]
    lefts = [left] + [send(left, parts, lambda z0, c0, n0, d=d: (z0, c0, n0 ^ d)) for d in range(1, parts)]
    rights += [send(a, parts, lambda z0, c0, n0: (z0, c0 ^ 1, n0)) for a in rights]
    w2 = outer_product_weight.reshape(hid, hid * cz)
    pair_state_next = packed_pair_update(
        slots, lefts, rights, w2, pair_state,
        outer_product_bias, up_weight, expand_bias, down_weight,
    )
    return (alignment_state_next, pair_state_next)


def lines(mesh):
    return mesh.shape["wide"] == PLANES * CORES and mesh.shape["narrow"] == PLANES


def step(mesh, *args):
    parts = mesh.shape["narrow"]
    heads = args[7].shape[1]
    if lines(mesh) and heads == CORES * parts:
        return per_head(parts, *args)
    return spread_heads(parts, *args)


def solution(mesh):
    placed = (P("wide", "narrow", None), P("wide", "narrow", None)) + (P(),) * 15
    return jax.shard_map(
        functools.partial(step, mesh),
        mesh=mesh,
        in_specs=placed,
        out_specs=(P("wide", "narrow", None), P("wide", "narrow", None)),
        check_vma=False,
    )
```
